32 devices in a mesh: fsdp: 8 (over z, x), ctx: 2 (over core), tp: 2 (over y).
Axes of the slice: x: 2, y: 2, z: 4, core: 2. Of those that a mesh axis runs over, the one named last changes fastest.
Arguments:
- hidden_in: bfloat16 [8, 1500, 1280], P('fsdp', ('ctx', 'tp')), may hold values from -6 to 6
- valid_lengths: int32 [8], P('fsdp'), may hold values from 500 to 1500, as said below
- output_grad: bfloat16 [8, 1500, 1280], P('fsdp', ('ctx', 'tp')), may hold values from -6 to 6
- first_gain: bfloat16 [1280], P('fsdp'), may hold values from 0.5 to 1.5
- first_shift: bfloat16 [1280], P('fsdp'), may hold values from -3 to 3
- attention_in: bfloat16 [1280, 3, 1280], P('fsdp', None, 'tp'), may hold values from -0.25 to 0.25
- query_value_bias: bfloat16 [2, 1280], P(None, 'fsdp'), may hold values from -0.5 to 0.5
- attention_out: bfloat16 [1280, 1280], P('tp', 'fsdp'), may hold values from -3 to 3
- attention_bias: bfloat16 [1280], P('fsdp'), may hold values from -3 to 3
- second_gain: bfloat16 [1280], P('fsdp'), may hold values from 0.5 to 1.5
- second_shift: bfloat16 [1280], P('fsdp'), may hold values from -3 to 3
- expand_weight: bfloat16 [1280, 5120], P('fsdp', 'tp'), may hold values from -0.15625 to 0.15625
- expand_bias: bfloat16 [5120], P('fsdp'), may hold values from -3 to 3
- contract_weight: bfloat16 [5120, 1280], P('tp', 'fsdp'), may hold values from -0.078125 to 0.078125
- contract_bias: bfloat16 [1280], P('fsdp'), may hold values from -3 to 3
Outputs:
- hidden_out: bfloat16 [8, 1500, 1280], P('fsdp', ('ctx', 'tp'))
- hidden_grad: float32 [8, 1500, 1280], P('fsdp', ('ctx', 'tp'))
- grad_first_gain: float32 [1280], P(('fsdp', 'ctx'))
- grad_first_shift: float32 [1280], P(('fsdp', 'ctx'))
- grad_attention_in: float32 [1280, 3, 1280], P(('fsdp', 'ctx'), None, 'tp')
- grad_query_value_bias: float32 [2, 1280], P(None, ('fsdp', 'ctx'))
- grad_attention_out: float32 [1280, 1280], P('tp', ('fsdp', 'ctx'))
- grad_attention_bias: float32 [1280], P(('fsdp', 'ctx'))
- grad_second_gain: float32 [1280], P(('fsdp', 'ctx'))
- grad_second_shift: float32 [1280], P(('fsdp', 'ctx'))
- grad_expand_weight: float32 [1280, 5120], P(('fsdp', 'ctx'), 'tp')
- grad_expand_bias: float32 [5120], P(('fsdp', 'ctx'))
- grad_contract_weight: float32 [5120, 1280], P('tp', ('fsdp', 'ctx'))
- grad_contract_bias: float32 [1280], P(('fsdp', 'ctx'))
The draws below stay inside these ranges and needn't reach their ends.
Inputs may be any that keep to these rules, and one draw needn't show every extreme that they name: Tokens 0 to valid_lengths[c] - 1 of clip c are valid; in every draw some clip has all 1500 tokens valid and some has 500.
All inputs are finite; a program needn't handle non-finite values.
Results may differ from the reference program's by a relative error of at most 0.015.
Values may be sent and summed in bfloat16 or wider, within the bound.
A program may use at most 192 MiB of HBM per device.

```python
import jax
import jax.numpy as jnp
from jax import lax

D = 1280
H = 16
HD = 80
FF = 5120
L = 1500
CLIPS = 8


def draw_valid_lengths(key, part):
    lengths_drawn = jax.random.randint(key, (CLIPS,), L // 3, L + 1, dtype=jnp.int32)
    shuffled = jax.random.permutation(jax.random.fold_in(key, 7), CLIPS)
    lengths_drawn = lengths_drawn.at[shuffled[0]].set(L)
    return lengths_drawn.at[shuffled[1]].set(L // 3)


def levels(stream_key, shape, split, smallest, largest):
    factor_of = 1.0
    for dim, parts in split:
        heights = jax.random.uniform(jax.random.fold_in(jax.random.fold_in(stream_key, 6), dim), (parts,), jnp.float32, smallest / len(split), largest / len(split))
        factor_of = factor_of * jnp.repeat(jnp.exp(heights), shape[dim] // parts).reshape((-1,) + (1,) * (len(shape) - 1 - dim))
    return factor_of


def bell_draw(rng, dims, spread, bound, pieces=(), kind=jnp.bfloat16):
    drawn = jax.random.normal(rng, dims, jnp.float32) * spread
    if len(pieces) > 0:
        drawn = levels(rng, dims, pieces, -0.22, 0.18) * drawn
    return jnp.clip(drawn, min=-bound, max=bound).astype(kind)


def setup_inputs(seed: int = 0) -> dict:
    key_list = jax.random.split(jax.random.key(seed), 16)
    hidden_in = bell_draw(key_list[0], (CLIPS, L, D), 1.0, 6.0, ((0, 8), (1, 4)))
    valid_lengths = draw_valid_lengths(jax.random.fold_in(key_list[15], 71), 0)
    output_grad = bell_draw(key_list[2], (CLIPS, L, D), 1.0, 6.0, ((0, 8), (1, 4)))
    first_gain = jnp.clip(1.0 + 0.1 * jax.random.normal(key_list[3], (D,), jnp.float32), 0.5, 1.5).astype(jnp.bfloat16)
    first_shift = bell_draw(key_list[4], (D,), 0.3, 3.0, ((0, 8),))
    attention_in = bell_draw(key_list[5], (D, 3, D), (D // 2) ** -0.5, 0.25, ((0, 8), (2, 2)))
    query_value_bias = bell_draw(key_list[6], (2, D), 0.05, 0.5, ((1, 8),))
    attention_out = bell_draw(key_list[7], (D, D), (max(D // 320, 2)) ** -0.5, 3.0, ((0, 2), (1, 8)))
    attention_bias = bell_draw(key_list[8], (D,), 0.5, 3.0, ((0, 8),))
    second_gain = jnp.clip(1.0 + 0.1 * jax.random.normal(key_list[9], (D,), jnp.float32), 0.5, 1.5).astype(jnp.bfloat16)
    second_shift = bell_draw(key_list[10], (D,), 0.3, 3.0, ((0, 8),))
    expand_weight = bell_draw(key_list[11], (D, FF), D ** -0.5, 0.15625, ((0, 8), (1, 2)))
    expand_bias = bell_draw(key_list[12], (FF,), 0.5, 3.0, ((0, 8),))
    contract_weight = bell_draw(key_list[13], (FF, D), FF ** -0.5, 0.078125, ((0, 2), (1, 8)))
    contract_bias = bell_draw(key_list[14], (D,), 0.5, 3.0, ((0, 8),))
    return dict(hidden_in=hidden_in, valid_lengths=valid_lengths, output_grad=output_grad, first_gain=first_gain, first_shift=first_shift, attention_in=attention_in, query_value_bias=query_value_bias, attention_out=attention_out, attention_bias=attention_bias, second_gain=second_gain, second_shift=second_shift, expand_weight=expand_weight, expand_bias=expand_bias, contract_weight=contract_weight, contract_bias=contract_bias)


highest = lax.Precision.HIGHEST
masked_score = -1e+30

@jax.custom_vjp
def low(v):
    return lax.optimization_barrier(v.astype(jnp.bfloat16)).astype(jnp.float32)

@jax.custom_vjp
def low_back(v):
    return v

def low_keep(v):
    return (low(v), None)

def low_pass(kept, grad):
    return (grad,)

def back_keep(v):
    return (v, None)

def back_low(kept, grad):
    return (low(grad),)
low.defvjp(low_keep, low_pass)
low_back.defvjp(back_keep, back_low)

def layer_norm(values, gain_vector, offset):
    centered = values - lax.optimization_barrier(jnp.mean(values, axis=-1, keepdims=True))
    variance = lax.optimization_barrier(jnp.mean(centered * centered, axis=-1, keepdims=True))
    return centered * lax.rsqrt(variance + 1e-05) * gain_vector + offset

def clip_forward(params, clip_tokens, clip_length):
    first_gain, first_shift, attention_in, query_value_bias, attention_out, attention_bias, second_gain, second_shift, expand_weight, expand_bias, contract_weight, contract_bias = params
    positions = jnp.arange(L, dtype=jnp.int32)
    key_valid = positions < clip_length
    normed_one = low(layer_norm(clip_tokens, first_gain, first_shift))
    triple_bias = jnp.stack([query_value_bias[0], jnp.zeros_like(query_value_bias[0]), query_value_bias[1]])
    projected = jnp.einsum('td,dje->tje', normed_one, attention_in, precision=highest) + triple_bias
    projected = low(low_back(projected))
    queries = projected[:, 0].reshape(L, H, HD)
    keys_all = projected[:, 1].reshape(L, H, HD)
    values_all = projected[:, 2].reshape(L, H, HD)
    scores = low_back(jnp.einsum('qhd,khd->hqk', queries, keys_all, precision=highest) * HD ** (-0.5))
    scores = jnp.where(key_valid[None, None, :], scores, masked_score)
    top_score = lax.optimization_barrier(jnp.max(scores, axis=-1, keepdims=True))
    exponents = jnp.exp(scores - top_score)
    probabilities = exponents / lax.optimization_barrier(jnp.sum(exponents, axis=-1, keepdims=True))
    attended = jnp.einsum('hqk,khd->qhd', low(probabilities), values_all, precision=highest).reshape(L, D)
    attended = low(low_back(attended))
    residual = clip_tokens + low_back(jnp.dot(attended, attention_out, precision=highest) + attention_bias)
    normed_two = low(layer_norm(residual, second_gain, second_shift))
    pre_act = low_back(jnp.dot(normed_two, expand_weight, precision=highest) + expand_bias)
    activated = low(jax.nn.gelu(pre_act, approximate=False))
    return residual + low_back(jnp.dot(activated, contract_weight, precision=highest) + contract_bias)

def reference(hidden_in, valid_lengths, output_grad, first_gain, first_shift, attention_in, query_value_bias, attention_out, attention_bias, second_gain, second_shift, expand_weight, expand_bias, contract_weight, contract_bias):
    params = (first_gain.astype(jnp.float32), first_shift.astype(jnp.float32), attention_in.astype(jnp.float32), query_value_bias.astype(jnp.float32), attention_out.astype(jnp.float32), attention_bias.astype(jnp.float32), second_gain.astype(jnp.float32), second_shift.astype(jnp.float32), expand_weight.astype(jnp.float32), expand_bias.astype(jnp.float32), contract_weight.astype(jnp.float32), contract_bias.astype(jnp.float32))
    inputs = hidden_in.astype(jnp.float32)

    def forward(param_tuple, tokens_all):

        def clip_step(clip_item):
            return clip_forward(param_tuple, clip_item[0], clip_item[1])
        return lax.map(jax.checkpoint(clip_step), (tokens_all, valid_lengths))
    outputs, pullback = jax.vjp(forward, params, inputs)
    query_keep = (jnp.arange(L, dtype=jnp.int32)[None, :] < valid_lengths[:, None]).astype(jnp.float32)
    grad_params, grad_inputs = pullback(output_grad.astype(jnp.float32) * query_keep[:, :, None])
    return (outputs.astype(jnp.bfloat16), grad_inputs, grad_params[0], grad_params[1], grad_params[2], grad_params[3], grad_params[4], grad_params[5], grad_params[6], grad_params[7], grad_params[8], grad_params[9], grad_params[10], grad_params[11])
```

```python
import functools

import jax
import jax.numpy as jnp
from jax import lax
from jax.experimental import pallas as pl
from jax.experimental.pallas import tpu as pltpu
from jax.sharding import PartitionSpec as P

HD = 80
epsilon = 1e-05
masked_score = -1e30
LOG2E = 1.4426950408889634
f32 = jnp.float32
bf16 = jnp.bfloat16
MESH = pl.DeviceIdType.MESH
VMEM = pl.BlockSpec(memory_space=pltpu.VMEM)
HBM = pl.BlockSpec(memory_space=pltpu.HBM)
VMEM_LIMIT = 62 * 1024 * 1024


def params(**kw):
    return pltpu.CompilerParams(vmem_limit_bytes=VMEM_LIMIT, **kw)


def dot(a, b, dims=((1,), (0,))):
    return lax.dot_general(a, b, (dims, ((), ())), preferred_element_type=f32)


NT = ((1,), (1,))
TN = ((0,), (0,))


def swap(value, axis):
    return lax.ppermute(value, axis, [(0, 1), (1, 0)])


def gather_kernel(chunks, w_ref, s_ref, o_ref, so_ref, lsem, zs, zr, xs, xr, cs, cr, ss, sr):
    f = lax.axis_index("fsdp")
    c = lax.axis_index("ctx")
    y = lax.axis_index("tp")
    z, x = f // 2, f % 2
    rows_each = w_ref.shape[0]
    half = rows_each // 2
    width = w_ref.shape[1] // chunks
    bar = pltpu.get_barrier_semaphore()
    sibling = (f, 1 - c, y)
    across = (z * 2 + (1 - x), c, y)
    column = [None] + [(((z + d) % 4) * 2 + x, c, y) for d in (1, 2, 3)]
    others = [((f + d) % 8, c, y) for d in range(1, 8)]
    for p in others + [sibling]:
        pl.semaphore_signal(bar, 1, device_id=p, device_id_type=MESH)
    pl.semaphore_wait(bar, 8)

    def remote(src, dst, s, r, dev):
        copy = pltpu.make_async_remote_copy(
            src_ref=src, dst_ref=dst, send_sem=s, recv_sem=r, device_id=dev, device_id_type=MESH
        )
        copy.start()
        sent.append(copy)

    def rows(owner, part):
        return pl.ds(pl.multiple_of(owner * rows_each + part * half, 16), half)

    def cols(k):
        return pl.ds(k * width, width)

    def arrived(ref, sem):
        pltpu.make_async_copy(ref, ref, sem).wait()

    sent = []
    for d in range(1, 8):
        remote(s_ref, so_ref.at[f], ss.at[d], sr.at[d], others[d - 1])
    local = pltpu.make_async_copy(
        w_ref, o_ref.at[pl.ds(pl.multiple_of(f * rows_each, 16), rows_each)], lsem.at[0]
    )
    local.start()
    local_small = pltpu.make_async_copy(s_ref, so_ref.at[f], lsem.at[1])
    local_small.start()
    own = w_ref.at[pl.ds(pl.multiple_of(c * half, 16), half)]
    for k in range(chunks):
        dst = o_ref.at[rows(f, c), cols(k)]
        for d in (1, 2, 3):
            remote(own.at[:, cols(k)], dst, zs.at[d, k], zr.at[d, k], column[d])
        remote(own.at[:, cols(k)], dst, xs.at[0, k], xr.at[0, k], across)
    for k in range(chunks):
        for d in (1, 3, 2):
            block = o_ref.at[rows(((z - d + 4) % 4) * 2 + x, c), cols(k)]
            arrived(block, zr.at[d, k])
            remote(block, block, xs.at[d, k], xr.at[d, k], across)
            remote(block, block, cs.at[d, k], cr.at[d, k], sibling)
        for d in (0, 1, 3, 2):
            block = o_ref.at[rows(((z - d + 4) % 4) * 2 + (1 - x), c), cols(k)]
            arrived(block, xr.at[d, k])
            remote(block, block, cs.at[4 + d, k], cr.at[4 + d, k], sibling)
    for d in range(1, 8):
        arrived(so_ref.at[(f - d + 8) % 8], sr.at[d])
    for k in range(chunks):
        for d in (1, 2, 3):
            block = o_ref.at[rows(((z - d + 4) % 4) * 2 + x, 1 - c), cols(k)]
            arrived(block, cr.at[d, k])
        for d in (0, 1, 2, 3):
            block = o_ref.at[rows(((z - d + 4) % 4) * 2 + (1 - x), 1 - c), cols(k)]
            arrived(block, cr.at[4 + d, k])
    for copy in sent:
        copy.wait_send()
    local.wait()
    local_small.wait()


def gather_first(weight, smalls, fsdp_count):
    if fsdp_count == 8 and weight.shape[0] % 32 == 0:
        chunks = 5
        sem = pltpu.SemaphoreType.DMA
        return pl.pallas_call(
            functools.partial(gather_kernel, chunks),
            out_shape=(
                jax.ShapeDtypeStruct((8 * weight.shape[0], weight.shape[1]), bf16),
                jax.ShapeDtypeStruct((8,) + smalls.shape, bf16),
            ),
            in_specs=[HBM, HBM],
            out_specs=(HBM, HBM),
            scratch_shapes=[sem((2,))]
            + [sem((4, chunks))] * 4
            + [sem((8, chunks))] * 2
            + [sem((8,))] * 2,
            compiler_params=params(collective_id=1, has_side_effects=True),
        )(weight, smalls)
    return (
        lax.all_gather(weight, "fsdp", axis=0, tiled=True),
        lax.all_gather(smalls, "fsdp", axis=0),
    )


def vector_kernel(v_ref, o_ref, got, lsem, ss, sr):
    f = lax.axis_index("fsdp")
    c = lax.axis_index("ctx")
    y = lax.axis_index("tp")
    me = (f * 2 + c) * 2 + y
    bar = pltpu.get_barrier_semaphore()

    def device(i):
        return (i // 4, (i // 2) % 2, i % 2)

    peers = [(me + d) % 32 for d in range(1, 32)]
    for p in peers:
        pl.semaphore_signal(bar, 1, device_id=device(p), device_id_type=MESH)
    pl.semaphore_wait(bar, 31)
    sent = []
    for d, p in enumerate(peers):
        copy = pltpu.make_async_remote_copy(
            src_ref=v_ref.at[p // 2],
            dst_ref=got.at[d + 1],
            send_sem=ss.at[d],
            recv_sem=sr.at[d],
            device_id=device(p),
            device_id_type=MESH,
        )
        copy.start()
        sent.append(copy)
    local = pltpu.make_async_copy(v_ref.at[me // 2], got.at[0], lsem)
    local.start()
    local.wait()
    total = got[0].astype(f32)
    for d in range(31):
        sent[d].wait_recv()
    for d in range(31):
        total = total + got[d + 1].astype(f32)
    o_ref[...] = total
    for copy in sent:
        copy.wait_send()


def sum_vectors(vectors, fsdp_count):
    if fsdp_count == 8:
        sem = pltpu.SemaphoreType.DMA
        return pl.pallas_call(
            vector_kernel,
            out_shape=jax.ShapeDtypeStruct(vectors.shape[1:], f32),
            in_specs=[VMEM],
            out_specs=VMEM,
            scratch_shapes=[
                pltpu.VMEM((32,) + vectors.shape[1:], bf16),
                sem,
                sem((31,)),
                sem((31,)),
            ],
            compiler_params=params(collective_id=2, has_side_effects=True),
        )(vectors.astype(bf16))
    partial = lax.psum(vectors, "tp")
    return lax.psum_scatter(partial, ("fsdp", "ctx"), scatter_dimension=0, tiled=False)


def normalize(values):
    centered = values - jnp.mean(values, axis=-1, keepdims=True)
    inverse = lax.rsqrt(jnp.mean(centered * centered, axis=-1, keepdims=True) + epsilon)
    return centered * inverse, inverse


def project_kernel(x_ref, gain_ref, shift_ref, w_ref, b_ref, n_ref, p_ref):
    values = x_ref[...].astype(f32)
    hat, _ = normalize(values)
    low = (hat * gain_ref[...] + shift_ref[...]).astype(bf16)
    n_ref[...] = low
    p_ref[...] = (dot(low, w_ref[...]) + b_ref[...]).astype(bf16)


def project(x_all, gain, shift, weight, bias):
    rows, model = x_all.shape
    width = weight.shape[1]
    block = 256
    fixed = lambda i: (0, 0)
    return pl.pallas_call(
        project_kernel,
        grid=(rows // block,),
        in_specs=[
            pl.BlockSpec((block, model), lambda i: (i, 0)),
            pl.BlockSpec((1, model), fixed),
            pl.BlockSpec((1, model), fixed),
            pl.BlockSpec((model, width), fixed),
            pl.BlockSpec((1, width), fixed),
        ],
        out_specs=(
            pl.BlockSpec((block, model), lambda i: (i, 0)),
            pl.BlockSpec((block, width), lambda i: (i, 0)),
        ),
        out_shape=(
            jax.ShapeDtypeStruct((rows, model), bf16),
            jax.ShapeDtypeStruct((rows, width), bf16),
        ),
        compiler_params=params(),
        cost_estimate=pl.CostEstimate(
            flops=2 * rows * model * width, bytes_accessed=12 << 20, transcendentals=0
        ),
    )(x_all, gain, shift, weight, bias)


def head_window(head):
    start = head * HD // 128 * 128
    stop = -(-(head * HD + HD) // 128) * 128
    lanes = lax.broadcasted_iota(jnp.int32, (1, stop - start), 1) + start
    return start, stop, (lanes >= head * HD) & (lanes < head * HD + HD)


def attend_kernel(heads, proj_ref, far_ref, bias_ref, att_ref, lse_ref, acc_ref, stat_ref):
    rows = proj_ref.shape[0]
    width = heads * HD
    block = 256
    acc_ref[...] = jnp.zeros_like(acc_ref)
    stat_ref[...] = jnp.zeros_like(stat_ref)
    score_factor = HD ** (-0.5) * LOG2E

    def step(i, carry):
        at = pl.ds(pl.multiple_of(i * block, block), block)
        for head in range(heads):
            start, stop, mask = head_window(head)
            query = jnp.where(mask, proj_ref[at, start:stop], jnp.zeros((), bf16))
            near = dot(query, proj_ref[:, width + start : width + stop], NT)
            far = dot(query, far_ref[:, start:stop], NT)
            near = near * score_factor + bias_ref[0:1, :rows]
            far = far * score_factor + bias_ref[0:1, rows:]
            top = jnp.maximum(
                jnp.max(near, axis=-1, keepdims=True), jnp.max(far, axis=-1, keepdims=True)
            )
            near = jnp.exp2(near - top)
            far = jnp.exp2(far - top)
            total = jnp.sum(near, axis=-1, keepdims=True) + jnp.sum(far, axis=-1, keepdims=True)
            mixed = dot(near.astype(bf16), proj_ref[:, 2 * width + start : 2 * width + stop])
            mixed = mixed + dot(far.astype(bf16), far_ref[:, width + start : width + stop])
            mixed = mixed * (1.0 / total)
            acc_ref[at, start:stop] += jnp.where(mask, mixed, 0.0)
            lane = lax.broadcasted_iota(jnp.int32, (1, 128), 1)
            stat_ref[at, :] += jnp.where(lane == head, top + jnp.log2(total), 0.0)
        return carry

    lax.fori_loop(0, rows // block, step, 0)
    att_ref[...] = acc_ref[...].astype(bf16)
    lse_ref[...] = stat_ref[...].T


def attend(proj, far, bias, heads):
    rows = proj.shape[0]
    return pl.pallas_call(
        functools.partial(attend_kernel, heads),
        in_specs=[VMEM] * 3,
        out_specs=(VMEM, VMEM),
        out_shape=(
            jax.ShapeDtypeStruct((rows, heads * HD), bf16),
            jax.ShapeDtypeStruct((128, rows), f32),
        ),
        scratch_shapes=[pltpu.VMEM((rows, heads * HD), f32), pltpu.VMEM((rows, 128), f32)],
        compiler_params=params(),
        cost_estimate=pl.CostEstimate(
            flops=4 * heads * rows * 2 * rows * 256, bytes_accessed=8 << 20, transcendentals=0
        ),
    )(proj, far, bias)


def attend_back_kernel(
    heads, proj_ref, far_ref, bias_ref, att_ref, grad_ref, lse_ref,
    dq_ref, dnear_ref, dfar_ref, key_ref, value_ref, keyt_ref, dqt_ref, dot_ref, dkv_ref,
):
    rows = proj_ref.shape[0]
    width = heads * HD
    block = 256
    score_factor = HD ** (-0.5) * LOG2E
    key_ref[:rows] = proj_ref[:, width : 2 * width]
    key_ref[rows:] = far_ref[:, :width]
    value_ref[:rows] = proj_ref[:, 2 * width :]
    value_ref[rows:] = far_ref[:, width:]
    keyt_ref[...] = key_ref[...].T
    dqt_ref[...] = jnp.zeros_like(dqt_ref)
    dkv_ref[...] = jnp.zeros_like(dkv_ref)
    product = grad_ref[...].astype(f32) * att_ref[...].astype(f32)
    high = product.astype(bf16)
    low = (product - high.astype(f32)).astype(bf16)
    lane = lax.broadcasted_iota(jnp.int32, (16, width), 1)
    row = lax.broadcasted_iota(jnp.int32, (16, width), 0)
    pick = jnp.where((lane >= row * HD) & (lane < row * HD + HD), 1.0, 0.0).astype(bf16)
    dot_ref[...] = dot(pick, high, NT) + dot(pick, low, NT)

    def step(i, carry):
        at = pl.ds(pl.multiple_of(i * block, block), block)
        bias = bias_ref[at, 0:1]
        for head in range(heads):
            start, stop, mask = head_window(head)
            zero = jnp.zeros((), bf16)
            query = jnp.where(mask, proj_ref[:, start:stop], zero)
            grad = jnp.where(mask, grad_ref[:, start:stop], zero)
            scores = dot(key_ref[at, start:stop], query, NT) * score_factor + bias
            probs = jnp.exp2(scores - lse_ref[head : head + 1, :])
            grad_probs = dot(value_ref[at, start:stop], grad, NT)
            grad_scores = (probs * (grad_probs - dot_ref[head : head + 1, :])).astype(bf16)
            dkv_ref[at, start:stop] += dot(grad_scores, query)
            dkv_ref[at, width + start : width + stop] += dot(probs.astype(bf16), grad)
            keyt = keyt_ref[head * HD : head * HD + HD, at]
            dqt_ref[head * HD : head * HD + HD, :] += dot(keyt, grad_scores)
        return carry

    lax.fori_loop(0, 2 * rows // block, step, 0)
    scale = HD ** (-0.5)
    dq_ref[...] = (dqt_ref[...].T * scale).astype(bf16)
    dnear_ref[:, :width] = dkv_ref[:rows, :width] * scale
    dnear_ref[:, width:] = dkv_ref[:rows, width:]
    dfar_ref[:, :width] = (dkv_ref[rows:, :width] * scale).astype(bf16)
    dfar_ref[:, width:] = dkv_ref[rows:, width:].astype(bf16)


def attend_back(proj, far, bias, attended, grad, lse, heads):
    rows = proj.shape[0]
    width = heads * HD
    return pl.pallas_call(
        functools.partial(attend_back_kernel, heads),
        in_specs=[VMEM] * 6,
        out_specs=(VMEM, VMEM, VMEM),
        out_shape=(
            jax.ShapeDtypeStruct((rows, width), bf16),
            jax.ShapeDtypeStruct((rows, 2 * width), f32),
            jax.ShapeDtypeStruct((rows, 2 * width), bf16),
        ),
        scratch_shapes=[
            pltpu.VMEM((2 * rows, width), bf16),
            pltpu.VMEM((2 * rows, width), bf16),
            pltpu.VMEM((width, 2 * rows), bf16),
            pltpu.VMEM((width, rows), f32),
            pltpu.VMEM((16, rows), f32),
            pltpu.VMEM((2 * rows, 2 * width), f32),
        ],
        compiler_params=params(),
        cost_estimate=pl.CostEstimate(
            flops=10 * heads * rows * 2 * rows * 256, bytes_accessed=16 << 20, transcendentals=0
        ),
    )(proj, far, bias, attended, grad, lse)


def residual_kernel(x_ref, own_ref, oth_ref, wa_ref, wb_ref, vec_ref, r_ref, n_ref):
    mixed = dot(own_ref[...], wa_ref[...], NT) + dot(oth_ref[...], wb_ref[...], NT)
    residual = x_ref[...].astype(f32) + (mixed + vec_ref[0:1, :])
    r_ref[...] = residual
    hat, _ = normalize(residual)
    n_ref[...] = (hat * vec_ref[1:2, :] + vec_ref[2:3, :]).astype(bf16)


def residual_step(x_all, own, oth, weights, width, vectors):
    rows, model = x_all.shape
    block = 128
    return pl.pallas_call(
        residual_kernel,
        grid=(rows // block,),
        in_specs=[
            pl.BlockSpec((block, model), lambda i: (i, 0)),
            pl.BlockSpec((block, width), lambda i: (i, 0)),
            pl.BlockSpec((block, width), lambda i: ((i + rows // block // 2) % (rows // block), 0)),
            pl.BlockSpec((model, width), lambda i: (0, 0)),
            pl.BlockSpec((model, width), lambda i: (0, 1)),
            pl.BlockSpec(vectors.shape, lambda i: (0, 0)),
        ],
        out_specs=(
            pl.BlockSpec((block, model), lambda i: (i, 0)),
            pl.BlockSpec((block, model), lambda i: (i, 0)),
        ),
        out_shape=(
            jax.ShapeDtypeStruct((rows, model), f32),
            jax.ShapeDtypeStruct((rows, model), bf16),
        ),
        compiler_params=params(),
        cost_estimate=pl.CostEstimate(
            flops=4 * rows * model * width, bytes_accessed=12 << 20, transcendentals=0
        ),
    )(x_all, own, oth, weights, weights, vectors)


def hidden_kernel(blocks, n_ref, g_ref, we_ref, wc_ref, b_ref, act_ref, pre_ref, sum_ref, own_ref, oth_ref, acc_ref):
    k = pl.program_id(0)
    rows = n_ref.shape[0]
    half = rows // 2
    piece = 256

    @pl.when(k == 0)
    def _():
        acc_ref[...] = jnp.zeros_like(acc_ref)

    total = jnp.zeros((1, b_ref.shape[1]), f32)
    for i in range(rows // piece):
        at = slice(i * piece, (i + 1) * piece)
        pre = dot(n_ref[at], we_ref[...]) + b_ref[...]
        back = dot(g_ref[at], wc_ref[...])
        cdf = 0.5 + 0.5 * lax.erf(pre * (0.5**0.5))
        density = jnp.exp(pre * pre * -0.5) * 0.3989422804014327
        act_ref[at] = (pre * cdf).astype(bf16)
        low = (back * (cdf + pre * density)).astype(bf16)
        pre_ref[at] = low
        total = total + jnp.sum(low.astype(f32), axis=0, keepdims=True)
        acc_ref[at] += dot(low, we_ref[...], NT)
    sum_ref[...] = total

    @pl.when(k == blocks - 1)
    def _():
        own_ref[...] = acc_ref[:half]
        oth_ref[...] = acc_ref[half:].astype(bf16)


def hidden_step(normed, grad, weights, expand_at, contract_at, width, bias):
    rows, model = normed.shape
    block = 256
    blocks = width // block
    half = rows // 2
    fixed = lambda k: (0, 0)
    return pl.pallas_call(
        functools.partial(hidden_kernel, blocks),
        grid=(blocks,),
        in_specs=[
            pl.BlockSpec((rows, model), fixed),
            pl.BlockSpec((rows, model), fixed),
            pl.BlockSpec((model, block), lambda k: (0, expand_at // block + k)),
            pl.BlockSpec((model, block), lambda k: (0, contract_at // block + k)),
            pl.BlockSpec((1, block), lambda k: (0, k)),
        ],
        out_specs=(
            pl.BlockSpec((rows, block), lambda k: (0, k)),
            pl.BlockSpec((rows, block), lambda k: (0, k)),
            pl.BlockSpec((1, block), lambda k: (0, k)),
            pl.BlockSpec((half, model), fixed),
            pl.BlockSpec((half, model), fixed),
        ),
        out_shape=(
            jax.ShapeDtypeStruct((rows, width), bf16),
            jax.ShapeDtypeStruct((rows, width), bf16),
            jax.ShapeDtypeStruct((1, width), f32),
            jax.ShapeDtypeStruct((half, model), f32),
            jax.ShapeDtypeStruct((half, model), bf16),
        ),
        scratch_shapes=[pltpu.VMEM((rows, model), f32)],
        compiler_params=params(),
        cost_estimate=pl.CostEstimate(
            flops=6 * rows * model * width, bytes_accessed=28 << 20, transcendentals=0
        ),
    )(normed, grad, weights, weights, bias)


def norm_back_kernel(round_low, own_ref, oth_ref, base_ref, add_ref, gain_ref, *outs):
    i = pl.program_id(0)
    grad = own_ref[...].astype(f32) + oth_ref[...].astype(f32)
    hat, inverse = normalize(base_ref[...].astype(f32))
    scaled = grad * gain_ref[...]
    first = jnp.mean(scaled, axis=-1, keepdims=True)
    second = jnp.mean(scaled * hat, axis=-1, keepdims=True)
    result = add_ref[...].astype(f32) + inverse * (scaled - first - hat * second)
    outs[0][...] = result
    sums = outs[-1]

    @pl.when(i == 0)
    def _():
        sums[...] = jnp.zeros_like(sums)

    sums[0:1] += jnp.sum(grad * hat, axis=0, keepdims=True)
    sums[1:2] += jnp.sum(grad, axis=0, keepdims=True)
    if round_low:
        low = result.astype(bf16)
        outs[1][...] = low
        sums[2:3] += jnp.sum(low.astype(f32), axis=0, keepdims=True)


def norm_back(own, oth, base, add, gain, round_low):
    rows, model = own.shape
    block = 128
    spec = pl.BlockSpec((block, model), lambda i: (i, 0))
    outs = [jax.ShapeDtypeStruct((rows, model), f32)]
    if round_low:
        outs.append(jax.ShapeDtypeStruct((rows, model), bf16))
    outs.append(jax.ShapeDtypeStruct((8, model), f32))
    return pl.pallas_call(
        functools.partial(norm_back_kernel, round_low),
        grid=(rows // block,),
        in_specs=[spec] * 4 + [pl.BlockSpec((1, model), lambda i: (0, 0))],
        out_specs=tuple([spec] * (len(outs) - 1) + [pl.BlockSpec((8, model), lambda i: (0, 0))]),
        out_shape=tuple(outs),
        compiler_params=params(),
    )(own, oth, base, add, gain)


def per_device(
    hidden_in,
    valid_lengths,
    output_grad,
    first_gain,
    first_shift,
    attention_in,
    query_value_bias,
    attention_out,
    attention_bias,
    second_gain,
    second_shift,
    expand_weight,
    expand_bias,
    contract_weight,
    contract_bias,
):
    _, share, model = hidden_in.shape
    tp_rank = lax.axis_index("tp")
    ctx_rank = lax.axis_index("ctx")
    fsdp_count = lax.axis_size("fsdp")
    rows_each = attention_in.shape[0]
    half_each = rows_each // 2
    width = attention_in.shape[2]
    heads = width // HD
    hidden = expand_weight.shape[1]
    slot = -(-share // 128) * 128
    length = valid_lengths[0]

    def padded(value):
        return jnp.pad(value, ((0, slot - share), (0, 0)))

    def starts(ctx):
        return (ctx * 2 + tp_rank) * share, (ctx * 2 + 1 - tp_rank) * share

    own_start, _ = starts(ctx_rank)
    token_valid = (own_start + lax.iota(jnp.int32, share)) < length
    grad_own = jnp.where(token_valid[:, None], output_grad[0], jnp.zeros((), bf16))
    grad_own = padded(grad_own)
    x_own = padded(hidden_in[0])
    x_all = jnp.concatenate([x_own, swap(x_own, "tp")], axis=0)
    grad_all = jnp.concatenate([grad_own, swap(grad_own, "tp")], axis=0)

    smalls = jnp.concatenate(
        [
            jnp.stack(
                [
                    first_gain,
                    first_shift,
                    query_value_bias[0],
                    query_value_bias[1],
                    attention_bias,
                    second_gain,
                    second_shift,
                    contract_bias,
                ]
            ),
            expand_bias.reshape(-1, rows_each),
        ],
        axis=0,
    )
    smalls = jnp.pad(smalls, ((0, 16 - smalls.shape[0]), (0, -rows_each % 128)))
    inner, smalls_all = gather_first(
        attention_in.reshape(rows_each, 3 * width), smalls, fsdp_count
    )
    outer_t = attention_out.T
    late = jnp.concatenate([outer_t, swap(outer_t, "tp"), expand_weight, contract_weight.T], axis=1)
    late = lax.dynamic_slice_in_dim(late, ctx_rank * half_each, half_each, 0)
    late = lax.all_gather(late, ("fsdp", "ctx"), axis=0, tiled=True)
    expand_at = 2 * width
    contract_at = 2 * width + hidden

    smalls_all = smalls_all[:, :, :rows_each].astype(f32)
    vectors = jnp.transpose(smalls_all[:, :8], (1, 0, 2)).reshape(8, model)
    expand_rows = smalls_all[:, 8 : 8 + hidden * 2 // model].reshape(1, 2 * hidden)
    expand_local = lax.dynamic_slice_in_dim(expand_rows, tp_rank * hidden, hidden, 1)
    pair = lax.dynamic_slice_in_dim(vectors[2:4], tp_rank * width, width, 1)
    triple = jnp.concatenate([pair[0:1], jnp.zeros((1, width), f32), pair[1:2]], axis=1)

    normed_one, proj = project(x_all, vectors[0:1], vectors[1:2], inner, triple)
    far = swap(proj[:, width:], "ctx")
    places = lax.iota(jnp.int32, slot)
    inside = places < share

    def key_bias(ctx):
        return [jnp.where(inside & (s + places < length), 0.0, masked_score) for s in starts(ctx)]

    bias = jnp.concatenate(key_bias(ctx_rank) + key_bias(1 - ctx_rank)).astype(f32)
    attended, lse = attend(proj, far, jnp.broadcast_to(bias[None], (8, bias.shape[0])), heads)
    attended_oth = swap(attended, "tp")
    residual, normed_two = residual_step(x_all, attended, attended_oth, late, width, vectors[4:7])

    activated, pre_grad, expand_sum, normed_own, normed_oth = hidden_step(
        normed_two, grad_all, late, expand_at, contract_at, hidden, expand_local
    )
    normed_oth = swap(normed_oth, "tp")
    grad_contract_t = dot(grad_all, activated, TN).astype(bf16)
    grad_expand = dot(normed_two, pre_grad, TN).astype(bf16)
    grad_late = lax.psum_scatter(
        jnp.concatenate([grad_expand, grad_contract_t], axis=1),
        ("fsdp", "ctx"),
        scatter_dimension=0,
        tiled=True,
    ).astype(f32)
    contracted = dot(activated, late[:, contract_at:], NT)
    contracted = contracted[:slot] + swap(contracted[slot:].astype(bf16), "tp").astype(f32)
    hidden_out = (residual[:slot] + (contracted + vectors[7:8])).astype(bf16)

    residual_grad, residual_low, sums_two = norm_back(
        normed_own, normed_oth, residual[:slot], grad_own, vectors[5:6], True
    )
    residual_low_all = jnp.concatenate([residual_low, swap(residual_low, "tp")], axis=0)
    attended_grad = dot(residual_low_all, late[:, :width]).astype(bf16)
    grad_outer_t = dot(residual_low_all, attended, TN).astype(bf16)

    grad_query, grad_near, grad_far = attend_back(
        proj, far, jnp.broadcast_to(bias[:, None], (bias.shape[0], 128)), attended, attended_grad, lse, heads
    )
    grad_near = (grad_near + swap(grad_far, "ctx").astype(f32)).astype(bf16)
    grad_proj = jnp.concatenate([grad_query, grad_near], axis=1)
    normed_grad = dot(grad_proj, inner, NT)
    normed_grad_oth = swap(normed_grad[slot:].astype(bf16), "tp")
    grad_inner = dot(normed_one, grad_proj, TN).astype(bf16)
    proj_sums = jnp.sum(grad_proj.astype(f32), axis=0)
    grad_early = lax.psum_scatter(
        jnp.concatenate([grad_inner, grad_outer_t], axis=1),
        ("fsdp", "ctx"),
        scatter_dimension=0,
        tiled=True,
    ).astype(f32)
    hidden_grad, sums_one = norm_back(
        normed_grad[:slot], normed_grad_oth, x_own, residual_grad, vectors[0:1], False
    )

    def placed(value, total):
        zero = jnp.zeros((total,), f32)
        return lax.dynamic_update_slice_in_dim(zero, value, tp_rank * value.shape[0], 0)

    owned = model // (fsdp_count * 2)
    stacked = jnp.stack(
        [
            sums_one[0],
            sums_one[1],
            placed(proj_sums[:width], model),
            placed(proj_sums[2 * width :], model),
            sums_two[2],
            sums_two[0],
            sums_two[1],
            jnp.sum(grad_own.astype(f32), axis=0),
        ]
    )
    stacked = jnp.transpose(stacked.reshape(8, -1, owned), (1, 0, 2))
    expand_piece = placed(expand_sum[0], 2 * hidden).reshape(fsdp_count * 2, -1, owned)
    stacked = jnp.concatenate([stacked, expand_piece], axis=1)
    stacked = jnp.pad(stacked, ((0, 0), (0, 16 - stacked.shape[1]), (0, 128 - owned)))
    summed = sum_vectors(stacked, fsdp_count)[:, :owned]

    return (
        hidden_out[None, :share],
        hidden_grad[None, :share],
        summed[0],
        summed[1],
        grad_early[:, : 3 * width].reshape(-1, 3, width),
        summed[2:4],
        grad_early[:, 3 * width :].T,
        summed[4],
        summed[5],
        summed[6],
        grad_late[:, :hidden],
        summed[8 : 8 + 2 * hidden // model].reshape(-1),
        grad_late[:, hidden:].T,
        summed[7],
    )


def solution(mesh):
    return jax.shard_map(
        per_device,
        mesh=mesh,
        in_specs=(
            P("fsdp", ("ctx", "tp"), None),
            P("fsdp"),
            P("fsdp", ("ctx", "tp"), None),
            P("fsdp"),
            P("fsdp"),
            P("fsdp", None, "tp"),
            P(None, "fsdp"),
            P("tp", "fsdp"),
            P("fsdp"),
            P("fsdp"),
            P("fsdp"),
            P("fsdp", "tp"),
            P("fsdp"),
            P("tp", "fsdp"),
            P("fsdp"),
        ),
        out_specs=(
            P("fsdp", ("ctx", "tp"), None),
            P("fsdp", ("ctx", "tp"), None),
            P(("fsdp", "ctx")),
            P(("fsdp", "ctx")),
            P(("fsdp", "ctx"), None, "tp"),
            P(None, ("fsdp", "ctx")),
            P("tp", ("fsdp", "ctx")),
            P(("fsdp", "ctx")),
            P(("fsdp", "ctx")),
            P(("fsdp", "ctx")),
            P(("fsdp", "ctx"), "tp"),
            P(("fsdp", "ctx")),
            P("tp", ("fsdp", "ctx")),
            P(("fsdp", "ctx")),
        ),
        check_vma=False,
    )
```

```python
import functools

import jax
import jax.numpy as jnp
from jax import lax
from jax.experimental import pallas as pl
from jax.experimental.pallas import tpu as pltpu
from jax.sharding import PartitionSpec as P

HD = 80
epsilon = 1e-05
masked_score = -1e30
LOG2E = 1.4426950408889634
f32 = jnp.float32
bf16 = jnp.bfloat16
MESH = pl.DeviceIdType.MESH
VMEM = pl.BlockSpec(memory_space=pltpu.VMEM)
HBM = pl.BlockSpec(memory_space=pltpu.HBM)
VMEM_LIMIT = 62 * 1024 * 1024


def params(**kw):
    return pltpu.CompilerParams(vmem_limit_bytes=VMEM_LIMIT, **kw)


def dot(a, b, dims=((1,), (0,))):
    return lax.dot_general(a, b, (dims, ((), ())), preferred_element_type=f32)


NT = ((1,), (1,))
TN = ((0,), (0,))


def swap(value, axis):
    return lax.ppermute(value, axis, [(0, 1), (1, 0)])


def gather_kernel(chunks, w_ref, s_ref, o_ref, so_ref, lsem, zs, zr, xs, xr, cs, cr, ss, sr):
    f = lax.axis_index("fsdp")
    c = lax.axis_index("ctx")
    y = lax.axis_index("tp")
    z, x = f // 2, f % 2
    rows_each = w_ref.shape[0]
    half = rows_each // 2
    width = w_ref.shape[1] // chunks
    bar = pltpu.get_barrier_semaphore()
    sibling = (f, 1 - c, y)
    across = (z * 2 + (1 - x), c, y)
    column = [None] + [(((z + d) % 4) * 2 + x, c, y) for d in (1, 2, 3)]
    others = [((f + d) % 8, c, y) for d in range(1, 8)]
    for p in others + [sibling]:
        pl.semaphore_signal(bar, 1, device_id=p, device_id_type=MESH)
    pl.semaphore_wait(bar, 8)

    def remote(src, dst, s, r, dev):
        copy = pltpu.make_async_remote_copy(
            src_ref=src, dst_ref=dst, send_sem=s, recv_sem=r, device_id=dev, device_id_type=MESH
        )
        copy.start()
        sent.append(copy)

    def rows(owner, part):
        return pl.ds(pl.multiple_of(owner * rows_each + part * half, 16), half)

    def cols(k):
        return pl.ds(k * width, width)

    def arrived(ref, sem):
        pltpu.make_async_copy(ref, ref, sem).wait()

    sent = []
    for d in range(1, 8):
        remote(s_ref, so_ref.at[f], ss.at[d], sr.at[d], others[d - 1])
    local = pltpu.make_async_copy(
        w_ref, o_ref.at[pl.ds(pl.multiple_of(f * rows_each, 16), rows_each)], lsem.at[0]
    )
    local.start()
    local_small = pltpu.make_async_copy(s_ref, so_ref.at[f], lsem.at[1])
    local_small.start()
    own = w_ref.at[pl.ds(pl.multiple_of(c * half, 16), half)]
    for k in range(chunks):
        dst = o_ref.at[rows(f, c), cols(k)]
        for d in (1, 2, 3):
            remote(own.at[:, cols(k)], dst, zs.at[d, k], zr.at[d, k], column[d])
        remote(own.at[:, cols(k)], dst, xs.at[0, k], xr.at[0, k], across)
    for k in range(chunks):
        for d in (1, 3, 2):
            block = o_ref.at[rows(((z - d + 4) % 4) * 2 + x, c), cols(k)]
            arrived(block, zr.at[d, k])
            remote(block, block, xs.at[d, k], xr.at[d, k], across)
            remote(block, block, cs.at[d, k], cr.at[d, k], sibling)
        for d in (0, 1, 3, 2):
            block = o_ref.at[rows(((z - d + 4) % 4) * 2 + (1 - x), c), cols(k)]
            arrived(block, xr.at[d, k])
            remote(block, block, cs.at[4 + d, k], cr.at[4 + d, k], sibling)
    for d in range(1, 8):
        arrived(so_ref.at[(f - d + 8) % 8], sr.at[d])
    for k in range(chunks):
        for d in (1, 2, 3):
            block = o_ref.at[rows(((z - d + 4) % 4) * 2 + x, 1 - c), cols(k)]
            arrived(block, cr.at[d, k])
        for d in (0, 1, 2, 3):
            block = o_ref.at[rows(((z - d + 4) % 4) * 2 + (1 - x), 1 - c), cols(k)]
            arrived(block, cr.at[4 + d, k])
    for copy in sent:
        copy.wait_send()
    local.wait()
    local_small.wait()


def gather_first(weight, smalls, fsdp_count):
    if fsdp_count == 8 and weight.shape[0] % 32 == 0:
        chunks = 5
        sem = pltpu.SemaphoreType.DMA
        return pl.pallas_call(
            functools.partial(gather_kernel, chunks),
            out_shape=(
                jax.ShapeDtypeStruct((8 * weight.shape[0], weight.shape[1]), bf16),
                jax.ShapeDtypeStruct((8,) + smalls.shape, bf16),
            ),
            in_specs=[HBM, HBM],
            out_specs=(HBM, HBM),
            scratch_shapes=[sem((2,))]
            + [sem((4, chunks))] * 4
            + [sem((8, chunks))] * 2
            + [sem((8,))] * 2,
            compiler_params=params(collective_id=1, has_side_effects=True),
        )(weight, smalls)
    return (
        lax.all_gather(weight, "fsdp", axis=0, tiled=True),
        lax.all_gather(smalls, "fsdp", axis=0),
    )


def vector_kernel(v_ref, o_ref, got, lsem, ss, sr):
    f = lax.axis_index("fsdp")
    c = lax.axis_index("ctx")
    y = lax.axis_index("tp")
    me = (f * 2 + c) * 2 + y
    bar = pltpu.get_barrier_semaphore()

    def device(i):
        return (i // 4, (i // 2) % 2, i % 2)

    peers = [(me + d) % 32 for d in range(1, 32)]
    for p in peers:
        pl.semaphore_signal(bar, 1, device_id=device(p), device_id_type=MESH)
    pl.semaphore_wait(bar, 31)
    sent = []
    for d, p in enumerate(peers):
        copy = pltpu.make_async_remote_copy(
            src_ref=v_ref.at[p // 2],
            dst_ref=got.at[d + 1],
            send_sem=ss.at[d],
            recv_sem=sr.at[d],
            device_id=device(p),
            device_id_type=MESH,
        )
        copy.start()
        sent.append(copy)
    local = pltpu.make_async_copy(v_ref.at[me // 2], got.at[0], lsem)
    local.start()
    local.wait()
    total = got[0].astype(f32)
    for d in range(31):
        sent[d].wait_recv()
    for d in range(31):
        total = total + got[d + 1].astype(f32)
    o_ref[...] = total
    for copy in sent:
        copy.wait_send()


def sum_vectors(vectors, fsdp_count):
    if fsdp_count == 8:
        sem = pltpu.SemaphoreType.DMA
        return pl.pallas_call(
            vector_kernel,
            out_shape=jax.ShapeDtypeStruct(vectors.shape[1:], f32),
            in_specs=[VMEM],
            out_specs=VMEM,
            scratch_shapes=[
                pltpu.VMEM((32,) + vectors.shape[1:], bf16),
                sem,
                sem((31,)),
                sem((31,)),
            ],
            compiler_params=params(collective_id=2, has_side_effects=True),
        )(vectors.astype(bf16))
    partial = lax.psum(vectors, "tp")
    return lax.psum_scatter(partial, ("fsdp", "ctx"), scatter_dimension=0, tiled=False)


def scatter_kernel(spans, arrays, *refs):
    ins = refs[:arrays]
    outs = refs[arrays : 2 * arrays]
    own, near, mine, far, pair, last, lsem, cs, cr, xs, xr, zs, zr = refs[2 * arrays :]
    f = lax.axis_index("fsdp")
    c = lax.axis_index("ctx")
    y = lax.axis_index("tp")
    z, x = f // 2, f % 2
    bar = pltpu.get_barrier_semaphore()
    sibling = (f, 1 - c, y)
    across = (z * 2 + (1 - x), c, y)
    column = [None] + [(((z + d) % 4) * 2 + x, c, y) for d in (1, 2, 3)]
    for p in [sibling, across] + column[1:]:
        pl.semaphore_signal(bar, 1, device_id=p, device_id_type=MESH)
    pl.semaphore_wait(bar, 5)

    def remote(src, dst, s, r, dev):
        copy = pltpu.make_async_remote_copy(
            src_ref=src, dst_ref=dst, send_sem=s, recv_sem=r, device_id=dev, device_id_type=MESH
        )
        copy.start()
        return copy

    local, over_ctx, over_x, over_z = {}, {}, {}, {}
    for k, (a, start, width) in enumerate(spans):
        cols = pl.ds(start, width)
        fit = pl.ds(0, width)
        copy = pltpu.make_async_copy(ins[a].at[:, c, :, cols], own.at[k, :, :, fit], lsem.at[k])
        copy.start()
        local[k] = copy
        over_ctx[k] = remote(
            ins[a].at[:, 1 - c, :, cols], near.at[k, :, :, fit], cs.at[k], cr.at[k], sibling
        )

    def first(k):
        width = spans[k][2]
        local[k].wait()
        over_ctx[k].wait_recv()
        for i in range(8):
            total = own[k, i, :, :width].astype(f32) + near[k, i, :, :width].astype(f32)
            mine[k, i // 2, i % 2, :, :width] = total.astype(bf16)
        src = mine.at[k, :, 1 - x, :, pl.ds(0, width)]
        over_x[k] = remote(src, far.at[k, :, :, pl.ds(0, width)], xs.at[k], xr.at[k], across)

    def second(k):
        width = spans[k][2]
        over_x[k].wait_recv()
        for i in range(4):
            total = mine[k, i, x, :, :width].astype(f32) + far[k, i, :, :width].astype(f32)
            pair[k, i, :, :width] = total.astype(bf16)
        over_z[k] = [
            remote(
                pair.at[k, (z + d) % 4, :, pl.ds(0, width)],
                last.at[k, d - 1, :, pl.ds(0, width)],
                zs.at[k, d - 1],
                zr.at[k, d - 1],
                column[d],
            )
            for d in (1, 2, 3)
        ]

    def third(k):
        a, start, width = spans[k]
        total = pair[k, z, :, :width].astype(f32)
        for d in range(3):
            over_z[k][d].wait_recv()
            total = total + last[k, d, :, :width].astype(f32)
        outs[a][:, start : start + width] = total

    count = len(spans)
    for step in range(count + 2):
        if step < count:
            first(step)
        if 0 <= step - 1 < count:
            second(step - 1)
        if 0 <= step - 2 < count:
            third(step - 2)
    for k in range(count):
        over_ctx[k].wait_send()
        over_x[k].wait_send()
        for copy in over_z[k]:
            copy.wait_send()


def scatter_sums(grads, widest, fsdp_count):
    rows = grads[0].shape[0]
    owned = rows // (fsdp_count * 2)
    if fsdp_count == 8 and owned % 16 == 0:
        spans = []
        for a, grad in enumerate(grads):
            for start in range(0, grad.shape[1], widest):
                spans.append((a, start, min(widest, grad.shape[1] - start)))
        count = len(spans)
        sem = pltpu.SemaphoreType.DMA
        return pl.pallas_call(
            functools.partial(scatter_kernel, spans, len(grads)),
            in_specs=[HBM] * len(grads),
            out_specs=tuple([VMEM] * len(grads)),
            out_shape=tuple(jax.ShapeDtypeStruct((owned, g.shape[1]), f32) for g in grads),
            scratch_shapes=[
                pltpu.VMEM((count, 8, owned, widest), bf16),
                pltpu.VMEM((count, 8, owned, widest), bf16),
                pltpu.VMEM((count, 4, 2, owned, widest), bf16),
                pltpu.VMEM((count, 4, owned, widest), bf16),
                pltpu.VMEM((count, 4, owned, widest), bf16),
                pltpu.VMEM((count, 3, owned, widest), bf16),
            ]
            + [sem((count,))] * 5
            + [sem((count, 3))] * 2,
            compiler_params=params(collective_id=3, has_side_effects=True),
        )(*[g.reshape(8, 2, owned, g.shape[1]) for g in grads])
    whole = lax.psum_scatter(
        jnp.concatenate(grads, axis=1), ("fsdp", "ctx"), scatter_dimension=0, tiled=True
    ).astype(f32)
    edges = [sum(g.shape[1] for g in grads[:i]) for i in range(len(grads) + 1)]
    return [whole[:, a:b] for a, b in zip(edges, edges[1:])]


def normalize(values):
    centered = values - jnp.mean(values, axis=-1, keepdims=True)
    inverse = lax.rsqrt(jnp.mean(centered * centered, axis=-1, keepdims=True) + epsilon)
    return centered * inverse, inverse


def project_kernel(x_ref, gain_ref, shift_ref, w_ref, b_ref, n_ref, p_ref):
    values = x_ref[...].astype(f32)
    hat, _ = normalize(values)
    low = (hat * gain_ref[...] + shift_ref[...]).astype(bf16)
    n_ref[...] = low
    p_ref[...] = (dot(low, w_ref[...]) + b_ref[...]).astype(bf16)


def project(x_all, gain, shift, weight, bias):
    rows, model = x_all.shape
    width = weight.shape[1]
    block = 256
    fixed = lambda i: (0, 0)
    return pl.pallas_call(
        project_kernel,
        grid=(rows // block,),
        in_specs=[
            pl.BlockSpec((block, model), lambda i: (i, 0)),
            pl.BlockSpec((1, model), fixed),
            pl.BlockSpec((1, model), fixed),
            pl.BlockSpec((model, width), fixed),
            pl.BlockSpec((1, width), fixed),
        ],
        out_specs=(
            pl.BlockSpec((block, model), lambda i: (i, 0)),
            pl.BlockSpec((block, width), lambda i: (i, 0)),
        ),
        out_shape=(
            jax.ShapeDtypeStruct((rows, model), bf16),
            jax.ShapeDtypeStruct((rows, width), bf16),
        ),
        compiler_params=params(),
        cost_estimate=pl.CostEstimate(
            flops=2 * rows * model * width, bytes_accessed=12 << 20, transcendentals=0
        ),
    )(x_all, gain, shift, weight, bias)


def head_window(head):
    start = head * HD // 128 * 128
    stop = -(-(head * HD + HD) // 128) * 128
    lanes = lax.broadcasted_iota(jnp.int32, (1, stop - start), 1) + start
    return start, stop, (lanes >= head * HD) & (lanes < head * HD + HD)


def attend_kernel(heads, proj_ref, far_ref, bias_ref, att_ref, lse_ref, acc_ref, stat_ref):
    rows = proj_ref.shape[0]
    width = heads * HD
    block = 256
    acc_ref[...] = jnp.zeros_like(acc_ref)
    stat_ref[...] = jnp.zeros_like(stat_ref)
    score_factor = HD ** (-0.5) * LOG2E

    def step(i, carry):
        at = pl.ds(pl.multiple_of(i * block, block), block)
        for head in range(heads):
            start, stop, mask = head_window(head)
            query = jnp.where(mask, proj_ref[at, start:stop], jnp.zeros((), bf16))
            near = dot(query, proj_ref[:, width + start : width + stop], NT)
            far = dot(query, far_ref[:, start:stop], NT)
            near = near * score_factor + bias_ref[0:1, :rows]
            far = far * score_factor + bias_ref[0:1, rows:]
            top = jnp.maximum(
                jnp.max(near, axis=-1, keepdims=True), jnp.max(far, axis=-1, keepdims=True)
            )
            near = jnp.exp2(near - top)
            far = jnp.exp2(far - top)
            total = jnp.sum(near, axis=-1, keepdims=True) + jnp.sum(far, axis=-1, keepdims=True)
            mixed = dot(near.astype(bf16), proj_ref[:, 2 * width + start : 2 * width + stop])
            mixed = mixed + dot(far.astype(bf16), far_ref[:, width + start : width + stop])
            mixed = mixed * (1.0 / total)
            acc_ref[at, start:stop] += jnp.where(mask, mixed, 0.0)
            lane = lax.broadcasted_iota(jnp.int32, (1, 128), 1)
            stat_ref[at, :] += jnp.where(lane == head, top + jnp.log2(total), 0.0)
        return carry

    lax.fori_loop(0, rows // block, step, 0)
    att_ref[...] = acc_ref[...].astype(bf16)
    lse_ref[...] = stat_ref[...].T


def attend(proj, far, bias, heads):
    rows = proj.shape[0]
    return pl.pallas_call(
        functools.partial(attend_kernel, heads),
        in_specs=[VMEM] * 3,
        out_specs=(VMEM, VMEM),
        out_shape=(
            jax.ShapeDtypeStruct((rows, heads * HD), bf16),
            jax.ShapeDtypeStruct((128, rows), f32),
        ),
        scratch_shapes=[pltpu.VMEM((rows, heads * HD), f32), pltpu.VMEM((rows, 128), f32)],
        compiler_params=params(),
        cost_estimate=pl.CostEstimate(
            flops=4 * heads * rows * 2 * rows * 256, bytes_accessed=8 << 20, transcendentals=0
        ),
    )(proj, far, bias)


def attend_back_kernel(
    heads, proj_ref, far_ref, bias_ref, att_ref, grad_ref, lse_ref,
    dq_ref, dnear_ref, dfar_ref, key_ref, value_ref, keyt_ref, dqt_ref, dot_ref, dkv_ref,
):
    rows = proj_ref.shape[0]
    width = heads * HD
    block = 256
    score_factor = HD ** (-0.5) * LOG2E
    key_ref[:rows] = proj_ref[:, width : 2 * width]
    key_ref[rows:] = far_ref[:, :width]
    value_ref[:rows] = proj_ref[:, 2 * width :]
    value_ref[rows:] = far_ref[:, width:]
    keyt_ref[...] = key_ref[...].T
    dqt_ref[...] = jnp.zeros_like(dqt_ref)
    dkv_ref[...] = jnp.zeros_like(dkv_ref)
    product = grad_ref[...].astype(f32) * att_ref[...].astype(f32)
    high = product.astype(bf16)
    low = (product - high.astype(f32)).astype(bf16)
    lane = lax.broadcasted_iota(jnp.int32, (16, width), 1)
    row = lax.broadcasted_iota(jnp.int32, (16, width), 0)
    pick = jnp.where((lane >= row * HD) & (lane < row * HD + HD), 1.0, 0.0).astype(bf16)
    dot_ref[...] = dot(pick, high, NT) + dot(pick, low, NT)

    def step(i, carry):
        at = pl.ds(pl.multiple_of(i * block, block), block)
        bias = bias_ref[at, 0:1]
        for head in range(heads):
            start, stop, mask = head_window(head)
            zero = jnp.zeros((), bf16)
            query = jnp.where(mask, proj_ref[:, start:stop], zero)
            grad = jnp.where(mask, grad_ref[:, start:stop], zero)
            scores = dot(key_ref[at, start:stop], query, NT) * score_factor + bias
            probs = jnp.exp2(scores - lse_ref[head : head + 1, :])
            grad_probs = dot(value_ref[at, start:stop], grad, NT)
            grad_scores = (probs * (grad_probs - dot_ref[head : head + 1, :])).astype(bf16)
            dkv_ref[at, start:stop] += dot(grad_scores, query)
            dkv_ref[at, width + start : width + stop] += dot(probs.astype(bf16), grad)
            keyt = keyt_ref[head * HD : head * HD + HD, at]
            dqt_ref[head * HD : head * HD + HD, :] += dot(keyt, grad_scores)
        return carry

    lax.fori_loop(0, 2 * rows // block, step, 0)
    scale = HD ** (-0.5)
    dq_ref[...] = (dqt_ref[...].T * scale).astype(bf16)
    dnear_ref[:, :width] = dkv_ref[:rows, :width] * scale
    dnear_ref[:, width:] = dkv_ref[:rows, width:]
    dfar_ref[:, :width] = (dkv_ref[rows:, :width] * scale).astype(bf16)
    dfar_ref[:, width:] = dkv_ref[rows:, width:].astype(bf16)


def attend_back(proj, far, bias, attended, grad, lse, heads):
    rows = proj.shape[0]
    width = heads * HD
    return pl.pallas_call(
        functools.partial(attend_back_kernel, heads),
        in_specs=[VMEM] * 6,
        out_specs=(VMEM, VMEM, VMEM),
        out_shape=(
            jax.ShapeDtypeStruct((rows, width), bf16),
            jax.ShapeDtypeStruct((rows, 2 * width), f32),
            jax.ShapeDtypeStruct((rows, 2 * width), bf16),
        ),
        scratch_shapes=[
            pltpu.VMEM((2 * rows, width), bf16),
            pltpu.VMEM((2 * rows, width), bf16),
            pltpu.VMEM((width, 2 * rows), bf16),
            pltpu.VMEM((width, rows), f32),
            pltpu.VMEM((16, rows), f32),
            pltpu.VMEM((2 * rows, 2 * width), f32),
        ],
        compiler_params=params(),
        cost_estimate=pl.CostEstimate(
            flops=10 * heads * rows * 2 * rows * 256, bytes_accessed=16 << 20, transcendentals=0
        ),
    )(proj, far, bias, attended, grad, lse)


def residual_kernel(x_ref, own_ref, oth_ref, wa_ref, wb_ref, vec_ref, r_ref, n_ref):
    mixed = dot(own_ref[...], wa_ref[...], NT) + dot(oth_ref[...], wb_ref[...], NT)
    residual = x_ref[...].astype(f32) + (mixed + vec_ref[0:1, :])
    r_ref[...] = residual
    hat, _ = normalize(residual)
    n_ref[...] = (hat * vec_ref[1:2, :] + vec_ref[2:3, :]).astype(bf16)


def residual_step(x_all, own, oth, weights, width, vectors):
    rows, model = x_all.shape
    block = 128
    return pl.pallas_call(
        residual_kernel,
        grid=(rows // block,),
        in_specs=[
            pl.BlockSpec((block, model), lambda i: (i, 0)),
            pl.BlockSpec((block, width), lambda i: (i, 0)),
            pl.BlockSpec((block, width), lambda i: ((i + rows // block // 2) % (rows // block), 0)),
            pl.BlockSpec((model, width), lambda i: (0, 0)),
            pl.BlockSpec((model, width), lambda i: (0, 1)),
            pl.BlockSpec(vectors.shape, lambda i: (0, 0)),
        ],
        out_specs=(
            pl.BlockSpec((block, model), lambda i: (i, 0)),
            pl.BlockSpec((block, model), lambda i: (i, 0)),
        ),
        out_shape=(
            jax.ShapeDtypeStruct((rows, model), f32),
            jax.ShapeDtypeStruct((rows, model), bf16),
        ),
        compiler_params=params(),
        cost_estimate=pl.CostEstimate(
            flops=4 * rows * model * width, bytes_accessed=12 << 20, transcendentals=0
        ),
    )(x_all, own, oth, weights, weights, vectors)


def hidden_kernel(blocks, n_ref, g_ref, we_ref, wc_ref, b_ref, act_ref, pre_ref, sum_ref, own_ref, oth_ref, acc_ref):
    k = pl.program_id(0)
    rows = n_ref.shape[0]
    half = rows // 2
    piece = 256

    @pl.when(k == 0)
    def _():
        acc_ref[...] = jnp.zeros_like(acc_ref)

    total = jnp.zeros((1, b_ref.shape[1]), f32)
    for i in range(rows // piece):
        at = slice(i * piece, (i + 1) * piece)
        pre = dot(n_ref[at], we_ref[...]) + b_ref[...]
        back = dot(g_ref[at], wc_ref[...])
        cdf = 0.5 + 0.5 * lax.erf(pre * (0.5**0.5))
        density = jnp.exp(pre * pre * -0.5) * 0.3989422804014327
        act_ref[at] = (pre * cdf).astype(bf16)
        low = (back * (cdf + pre * density)).astype(bf16)
        pre_ref[at] = low
        total = total + jnp.sum(low.astype(f32), axis=0, keepdims=True)
        acc_ref[at] += dot(low, we_ref[...], NT)
    sum_ref[...] = total

    @pl.when(k == blocks - 1)
    def _():
        own_ref[...] = acc_ref[:half]
        oth_ref[...] = acc_ref[half:].astype(bf16)


def hidden_step(normed, grad, weights, expand_at, contract_at, width, bias):
    rows, model = normed.shape
    block = 256
    blocks = width // block
    half = rows // 2
    fixed = lambda k: (0, 0)
    return pl.pallas_call(
        functools.partial(hidden_kernel, blocks),
        grid=(blocks,),
        in_specs=[
            pl.BlockSpec((rows, model), fixed),
            pl.BlockSpec((rows, model), fixed),
            pl.BlockSpec((model, block), lambda k: (0, expand_at // block + k)),
            pl.BlockSpec((model, block), lambda k: (0, contract_at // block + k)),
            pl.BlockSpec((1, block), lambda k: (0, k)),
        ],
        out_specs=(
            pl.BlockSpec((rows, block), lambda k: (0, k)),
            pl.BlockSpec((rows, block), lambda k: (0, k)),
            pl.BlockSpec((1, block), lambda k: (0, k)),
            pl.BlockSpec((half, model), fixed),
            pl.BlockSpec((half, model), fixed),
        ),
        out_shape=(
            jax.ShapeDtypeStruct((rows, width), bf16),
            jax.ShapeDtypeStruct((rows, width), bf16),
            jax.ShapeDtypeStruct((1, width), f32),
            jax.ShapeDtypeStruct((half, model), f32),
            jax.ShapeDtypeStruct((half, model), bf16),
        ),
        scratch_shapes=[pltpu.VMEM((rows, model), f32)],
        compiler_params=params(),
        cost_estimate=pl.CostEstimate(
            flops=6 * rows * model * width, bytes_accessed=28 << 20, transcendentals=0
        ),
    )(normed, grad, weights, weights, bias)


def norm_back_kernel(round_low, own_ref, oth_ref, base_ref, add_ref, gain_ref, *outs):
    i = pl.program_id(0)
    grad = own_ref[...].astype(f32) + oth_ref[...].astype(f32)
    hat, inverse = normalize(base_ref[...].astype(f32))
    scaled = grad * gain_ref[...]
    first = jnp.mean(scaled, axis=-1, keepdims=True)
    second = jnp.mean(scaled * hat, axis=-1, keepdims=True)
    result = add_ref[...].astype(f32) + inverse * (scaled - first - hat * second)
    outs[0][...] = result
    sums = outs[-1]

    @pl.when(i == 0)
    def _():
        sums[...] = jnp.zeros_like(sums)

    sums[0:1] += jnp.sum(grad * hat, axis=0, keepdims=True)
    sums[1:2] += jnp.sum(grad, axis=0, keepdims=True)
    if round_low:
        low = result.astype(bf16)
        outs[1][...] = low
        sums[2:3] += jnp.sum(low.astype(f32), axis=0, keepdims=True)


def norm_back(own, oth, base, add, gain, round_low):
    rows, model = own.shape
    block = 128
    spec = pl.BlockSpec((block, model), lambda i: (i, 0))
    outs = [jax.ShapeDtypeStruct((rows, model), f32)]
    if round_low:
        outs.append(jax.ShapeDtypeStruct((rows, model), bf16))
    outs.append(jax.ShapeDtypeStruct((8, model), f32))
    return pl.pallas_call(
        functools.partial(norm_back_kernel, round_low),
        grid=(rows // block,),
        in_specs=[spec] * 4 + [pl.BlockSpec((1, model), lambda i: (0, 0))],
        out_specs=tuple([spec] * (len(outs) - 1) + [pl.BlockSpec((8, model), lambda i: (0, 0))]),
        out_shape=tuple(outs),
        compiler_params=params(),
    )(own, oth, base, add, gain)


def per_device(
    hidden_in,
    valid_lengths,
    output_grad,
    first_gain,
    first_shift,
    attention_in,
    query_value_bias,
    attention_out,
    attention_bias,
    second_gain,
    second_shift,
    expand_weight,
    expand_bias,
    contract_weight,
    contract_bias,
):
    _, share, model = hidden_in.shape
    tp_rank = lax.axis_index("tp")
    ctx_rank = lax.axis_index("ctx")
    fsdp_count = lax.axis_size("fsdp")
    rows_each = attention_in.shape[0]
    half_each = rows_each // 2
    width = attention_in.shape[2]
    heads = width // HD
    hidden = expand_weight.shape[1]
    slot = -(-share // 128) * 128
    length = valid_lengths[0]

    def padded(value):
        return jnp.pad(value, ((0, slot - share), (0, 0)))

    def starts(ctx):
        return (ctx * 2 + tp_rank) * share, (ctx * 2 + 1 - tp_rank) * share

    own_start, _ = starts(ctx_rank)
    token_valid = (own_start + lax.iota(jnp.int32, share)) < length
    grad_own = jnp.where(token_valid[:, None], output_grad[0], jnp.zeros((), bf16))
    grad_own = padded(grad_own)
    x_own = padded(hidden_in[0])
    x_all = jnp.concatenate([x_own, swap(x_own, "tp")], axis=0)
    grad_all = jnp.concatenate([grad_own, swap(grad_own, "tp")], axis=0)

    smalls = jnp.concatenate(
        [
            jnp.stack(
                [
                    first_gain,
                    first_shift,
                    query_value_bias[0],
                    query_value_bias[1],
                    attention_bias,
                    second_gain,
                    second_shift,
                    contract_bias,
                ]
            ),
            expand_bias.reshape(-1, rows_each),
        ],
        axis=0,
    )
    smalls = jnp.pad(smalls, ((0, 16 - smalls.shape[0]), (0, -rows_each % 128)))
    inner, smalls_all = gather_first(
        attention_in.reshape(rows_each, 3 * width), smalls, fsdp_count
    )
    outer_t = attention_out.T
    late = jnp.concatenate([outer_t, swap(outer_t, "tp"), expand_weight, contract_weight.T], axis=1)
    late = lax.dynamic_slice_in_dim(late, ctx_rank * half_each, half_each, 0)
    late = lax.all_gather(late, ("fsdp", "ctx"), axis=0, tiled=True)
    expand_at = 2 * width
    contract_at = 2 * width + hidden

    smalls_all = smalls_all[:, :, :rows_each].astype(f32)
    vectors = jnp.transpose(smalls_all[:, :8], (1, 0, 2)).reshape(8, model)
    expand_rows = smalls_all[:, 8 : 8 + hidden * 2 // model].reshape(1, 2 * hidden)
    expand_local = lax.dynamic_slice_in_dim(expand_rows, tp_rank * hidden, hidden, 1)
    pair = lax.dynamic_slice_in_dim(vectors[2:4], tp_rank * width, width, 1)
    triple = jnp.concatenate([pair[0:1], jnp.zeros((1, width), f32), pair[1:2]], axis=1)

    normed_one, proj = project(x_all, vectors[0:1], vectors[1:2], inner, triple)
    far = swap(proj[:, width:], "ctx")
    places = lax.iota(jnp.int32, slot)
    inside = places < share

    def key_bias(ctx):
        return [jnp.where(inside & (s + places < length), 0.0, masked_score) for s in starts(ctx)]

    bias = jnp.concatenate(key_bias(ctx_rank) + key_bias(1 - ctx_rank)).astype(f32)
    attended, lse = attend(proj, far, jnp.broadcast_to(bias[None], (8, bias.shape[0])), heads)
    attended_oth = swap(attended, "tp")
    residual, normed_two = residual_step(x_all, attended, attended_oth, late, width, vectors[4:7])

    activated, pre_grad, expand_sum, normed_own, normed_oth = hidden_step(
        normed_two, grad_all, late, expand_at, contract_at, hidden, expand_local
    )
    normed_oth = swap(normed_oth, "tp")
    grad_contract_t = dot(grad_all, activated, TN).astype(bf16)
    grad_expand = dot(normed_two, pre_grad, TN).astype(bf16)
    normed_own, normed_oth, grad_late = lax.optimization_barrier(
        (normed_own, normed_oth, jnp.concatenate([grad_expand, grad_contract_t], axis=1))
    )
    grad_late = lax.psum_scatter(
        grad_late, ("fsdp", "ctx"), scatter_dimension=0, tiled=True
    ).astype(f32)
    contracted = dot(activated, late[:, contract_at:], NT)
    contracted = contracted[:slot] + swap(contracted[slot:].astype(bf16), "tp").astype(f32)
    hidden_out = (residual[:slot] + (contracted + vectors[7:8])).astype(bf16)

    residual_grad, residual_low, sums_two = norm_back(
        normed_own, normed_oth, residual[:slot], grad_own, vectors[5:6], True
    )
    residual_low_all = jnp.concatenate([residual_low, swap(residual_low, "tp")], axis=0)
    attended_grad = dot(residual_low_all, late[:, :width]).astype(bf16)
    grad_outer_t = dot(residual_low_all, attended, TN).astype(bf16)

    grad_query, grad_near, grad_far = attend_back(
        proj, far, jnp.broadcast_to(bias[:, None], (bias.shape[0], 128)), attended, attended_grad, lse, heads
    )
    grad_near = (grad_near + swap(grad_far, "ctx").astype(f32)).astype(bf16)
    grad_proj = jnp.concatenate([grad_query, grad_near], axis=1)
    normed_grad = dot(grad_proj, inner, NT)
    normed_grad_oth = swap(normed_grad[slot:].astype(bf16), "tp")
    grad_inner = dot(normed_one, grad_proj, TN).astype(bf16)
    proj_sums = jnp.sum(grad_proj.astype(f32), axis=0)
    grad_inner, grad_outer_t = scatter_sums([grad_inner, grad_outer_t], 384, fsdp_count)
    hidden_grad, sums_one = norm_back(
        normed_grad[:slot], normed_grad_oth, x_own, residual_grad, vectors[0:1], False
    )

    def placed(value, total):
        zero = jnp.zeros((total,), f32)
        return lax.dynamic_update_slice_in_dim(zero, value, tp_rank * value.shape[0], 0)

    owned = model // (fsdp_count * 2)
    stacked = jnp.stack(
        [
            sums_one[0],
            sums_one[1],
            placed(proj_sums[:width], model),
            placed(proj_sums[2 * width :], model),
            sums_two[2],
            sums_two[0],
            sums_two[1],
            jnp.sum(grad_own.astype(f32), axis=0),
        ]
    )
    stacked = jnp.transpose(stacked.reshape(8, -1, owned), (1, 0, 2))
    expand_piece = placed(expand_sum[0], 2 * hidden).reshape(fsdp_count * 2, -1, owned)
    stacked = jnp.concatenate([stacked, expand_piece], axis=1)
    stacked = jnp.pad(stacked, ((0, 0), (0, 16 - stacked.shape[1]), (0, 128 - owned)))
    summed = sum_vectors(stacked, fsdp_count)[:, :owned]

    return (
        hidden_out[None, :share],
        hidden_grad[None, :share],
        summed[0],
        summed[1],
        grad_inner.reshape(-1, 3, width),
        summed[2:4],
        grad_outer_t.T,
        summed[4],
        summed[5],
        summed[6],
        grad_late[:, :hidden],
        summed[8 : 8 + 2 * hidden // model].reshape(-1),
        grad_late[:, hidden:].T,
        summed[7],
    )


def solution(mesh):
    return jax.shard_map(
        per_device,
        mesh=mesh,
        in_specs=(
            P("fsdp", ("ctx", "tp"), None),
            P("fsdp"),
            P("fsdp", ("ctx", "tp"), None),
            P("fsdp"),
            P("fsdp"),
            P("fsdp", None, "tp"),
            P(None, "fsdp"),
            P("tp", "fsdp"),
            P("fsdp"),
            P("fsdp"),
            P("fsdp"),
            P("fsdp", "tp"),
            P("fsdp"),
            P("tp", "fsdp"),
            P("fsdp"),
        ),
        out_specs=(
            P("fsdp", ("ctx", "tp"), None),
            P("fsdp", ("ctx", "tp"), None),
            P(("fsdp", "ctx")),
            P(("fsdp", "ctx")),
            P(("fsdp", "ctx"), None, "tp"),
            P(None, ("fsdp", "ctx")),
            P("tp", ("fsdp", "ctx")),
            P(("fsdp", "ctx")),
            P(("fsdp", "ctx")),
            P(("fsdp", "ctx")),
            P(("fsdp", "ctx"), "tp"),
            P(("fsdp", "ctx")),
            P("tp", ("fsdp", "ctx")),
            P(("fsdp", "ctx")),
        ),
        check_vma=False,
    )
```

```python
import functools

import jax
import jax.numpy as jnp
from jax import lax
from jax.experimental import pallas as pl
from jax.experimental.pallas import tpu as pltpu
from jax.sharding import PartitionSpec as P

HD = 80
epsilon = 1e-05
masked_score = -1e30
LOG2E = 1.4426950408889634
f32 = jnp.float32
bf16 = jnp.bfloat16
MESH = pl.DeviceIdType.MESH
VMEM = pl.BlockSpec(memory_space=pltpu.VMEM)
HBM = pl.BlockSpec(memory_space=pltpu.HBM)
VMEM_LIMIT = 62 * 1024 * 1024


def params(**kw):
    return pltpu.CompilerParams(vmem_limit_bytes=VMEM_LIMIT, **kw)


def dot(a, b, dims=((1,), (0,))):
    return lax.dot_general(a, b, (dims, ((), ())), preferred_element_type=f32)


NT = ((1,), (1,))
TN = ((0,), (0,))


def swap(value, axis):
    return lax.ppermute(value, axis, [(0, 1), (1, 0)])


def vector_kernel(v_ref, o_ref, got, lsem, ss, sr):
    f = lax.axis_index("fsdp")
    c = lax.axis_index("ctx")
    y = lax.axis_index("tp")
    me = (f * 2 + c) * 2 + y
    bar = pltpu.get_barrier_semaphore()

    def device(i):
        return (i // 4, (i // 2) % 2, i % 2)

    peers = [(me + d) % 32 for d in range(1, 32)]
    for p in peers:
        pl.semaphore_signal(bar, 1, device_id=device(p), device_id_type=MESH)
    pl.semaphore_wait(bar, 31)
    sent = []
    for d, p in enumerate(peers):
        copy = pltpu.make_async_remote_copy(
            src_ref=v_ref.at[p // 2],
            dst_ref=got.at[d + 1],
            send_sem=ss.at[d],
            recv_sem=sr.at[d],
            device_id=device(p),
            device_id_type=MESH,
        )
        copy.start()
        sent.append(copy)
    local = pltpu.make_async_copy(v_ref.at[me // 2], got.at[0], lsem)
    local.start()
    local.wait()
    total = got[0].astype(f32)
    for d in range(31):
        sent[d].wait_recv()
    for d in range(31):
        total = total + got[d + 1].astype(f32)
    o_ref[...] = total
    for copy in sent:
        copy.wait_send()


def sum_vectors(vectors, fsdp_count):
    if fsdp_count == 8:
        sem = pltpu.SemaphoreType.DMA
        return pl.pallas_call(
            vector_kernel,
            out_shape=jax.ShapeDtypeStruct(vectors.shape[1:], f32),
            in_specs=[VMEM],
            out_specs=VMEM,
            scratch_shapes=[
                pltpu.VMEM((32,) + vectors.shape[1:], bf16),
                sem,
                sem((31,)),
                sem((31,)),
            ],
            compiler_params=params(collective_id=2, has_side_effects=True),
        )(vectors.astype(bf16))
    partial = lax.psum(vectors, "tp")
    return lax.psum_scatter(partial, ("fsdp", "ctx"), scatter_dimension=0, tiled=False)


def scatter_kernel(spans, arrays, *refs):
    ins = refs[:arrays]
    outs = refs[arrays : 2 * arrays]
    own, near, mine, far, pair, last, lsem, cs, cr, xs, xr, zs, zr = refs[2 * arrays :]
    f = lax.axis_index("fsdp")
    c = lax.axis_index("ctx")
    y = lax.axis_index("tp")
    z, x = f // 2, f % 2
    bar = pltpu.get_barrier_semaphore()
    sibling = (f, 1 - c, y)
    across = (z * 2 + (1 - x), c, y)
    column = [None] + [(((z + d) % 4) * 2 + x, c, y) for d in (1, 2, 3)]
    for p in [sibling, across] + column[1:]:
        pl.semaphore_signal(bar, 1, device_id=p, device_id_type=MESH)
    pl.semaphore_wait(bar, 5)

    def remote(src, dst, s, r, dev):
        copy = pltpu.make_async_remote_copy(
            src_ref=src, dst_ref=dst, send_sem=s, recv_sem=r, device_id=dev, device_id_type=MESH
        )
        copy.start()
        return copy

    local, over_ctx, over_x, over_z = {}, {}, {}, {}
    for k, (a, start, width) in enumerate(spans):
        cols = pl.ds(start, width)
        fit = pl.ds(0, width)
        copy = pltpu.make_async_copy(ins[a].at[:, c, :, cols], own.at[k, :, :, fit], lsem.at[k])
        copy.start()
        local[k] = copy
        over_ctx[k] = remote(
            ins[a].at[:, 1 - c, :, cols], near.at[k, :, :, fit], cs.at[k], cr.at[k], sibling
        )

    def first(k):
        width = spans[k][2]
        local[k].wait()
        over_ctx[k].wait_recv()
        for i in range(8):
            total = own[k, i, :, :width].astype(f32) + near[k, i, :, :width].astype(f32)
            mine[k, i // 2, i % 2, :, :width] = total.astype(bf16)
        src = mine.at[k, :, 1 - x, :, pl.ds(0, width)]
        over_x[k] = remote(src, far.at[k, :, :, pl.ds(0, width)], xs.at[k], xr.at[k], across)

    def second(k):
        width = spans[k][2]
        over_x[k].wait_recv()
        for i in range(4):
            total = mine[k, i, x, :, :width].astype(f32) + far[k, i, :, :width].astype(f32)
            pair[k, i, :, :width] = total.astype(bf16)
        over_z[k] = [
            remote(
                pair.at[k, (z + d) % 4, :, pl.ds(0, width)],
                last.at[k, d - 1, :, pl.ds(0, width)],
                zs.at[k, d - 1],
                zr.at[k, d - 1],
                column[d],
            )
            for d in (1, 2, 3)
        ]

    def third(k):
        a, start, width = spans[k]
        total = pair[k, z, :, :width].astype(f32)
        for d in range(3):
            over_z[k][d].wait_recv()
            total = total + last[k, d, :, :width].astype(f32)
        outs[a][:, start : start + width] = total

    count = len(spans)
    for step in range(count + 2):
        if step < count:
            first(step)
        if 0 <= step - 1 < count:
            second(step - 1)
        if 0 <= step - 2 < count:
            third(step - 2)
    for k in range(count):
        over_ctx[k].wait_send()
        over_x[k].wait_send()
        for copy in over_z[k]:
            copy.wait_send()


def scatter_sums(grads, widest, fsdp_count):
    rows = grads[0].shape[0]
    owned = rows // (fsdp_count * 2)
    if fsdp_count == 8 and owned % 16 == 0:
        spans = []
        for a, grad in enumerate(grads):
            for start in range(0, grad.shape[1], widest):
                spans.append((a, start, min(widest, grad.shape[1] - start)))
        count = len(spans)
        sem = pltpu.SemaphoreType.DMA
        return pl.pallas_call(
            functools.partial(scatter_kernel, spans, len(grads)),
            in_specs=[HBM] * len(grads),
            out_specs=tuple([VMEM] * len(grads)),
            out_shape=tuple(jax.ShapeDtypeStruct((owned, g.shape[1]), f32) for g in grads),
            scratch_shapes=[
                pltpu.VMEM((count, 8, owned, widest), bf16),
                pltpu.VMEM((count, 8, owned, widest), bf16),
                pltpu.VMEM((count, 4, 2, owned, widest), bf16),
                pltpu.VMEM((count, 4, owned, widest), bf16),
                pltpu.VMEM((count, 4, owned, widest), bf16),
                pltpu.VMEM((count, 3, owned, widest), bf16),
            ]
            + [sem((count,))] * 5
            + [sem((count, 3))] * 2,
            compiler_params=params(collective_id=3, has_side_effects=True),
        )(*[g.reshape(8, 2, owned, g.shape[1]) for g in grads])
    whole = lax.psum_scatter(
        jnp.concatenate(grads, axis=1), ("fsdp", "ctx"), scatter_dimension=0, tiled=True
    ).astype(f32)
    edges = [sum(g.shape[1] for g in grads[:i]) for i in range(len(grads) + 1)]
    return [whole[:, a:b] for a, b in zip(edges, edges[1:])]


def normalize(values):
    centered = values - jnp.mean(values, axis=-1, keepdims=True)
    inverse = lax.rsqrt(jnp.mean(centered * centered, axis=-1, keepdims=True) + epsilon)
    return centered * inverse, inverse


def project_kernel(x_ref, gain_ref, shift_ref, w_ref, b_ref, n_ref, p_ref):
    values = x_ref[...].astype(f32)
    hat, _ = normalize(values)
    low = (hat * gain_ref[...] + shift_ref[...]).astype(bf16)
    n_ref[...] = low
    p_ref[...] = (dot(low, w_ref[...]) + b_ref[...]).astype(bf16)


def project(x_all, gain, shift, weight, bias):
    rows, model = x_all.shape
    width = weight.shape[1]
    block = 256
    fixed = lambda i: (0, 0)
    return pl.pallas_call(
        project_kernel,
        grid=(rows // block,),
        in_specs=[
            pl.BlockSpec((block, model), lambda i: (i, 0)),
            pl.BlockSpec((1, model), fixed),
            pl.BlockSpec((1, model), fixed),
            pl.BlockSpec((model, width), fixed),
            pl.BlockSpec((1, width), fixed),
        ],
        out_specs=(
            pl.BlockSpec((block, model), lambda i: (i, 0)),
            pl.BlockSpec((block, width), lambda i: (i, 0)),
        ),
        out_shape=(
            jax.ShapeDtypeStruct((rows, model), bf16),
            jax.ShapeDtypeStruct((rows, width), bf16),
        ),
        compiler_params=params(),
        cost_estimate=pl.CostEstimate(
            flops=2 * rows * model * width, bytes_accessed=12 << 20, transcendentals=0
        ),
    )(x_all, gain, shift, weight, bias)


def head_window(head):
    start = head * HD // 128 * 128
    stop = -(-(head * HD + HD) // 128) * 128
    lanes = lax.broadcasted_iota(jnp.int32, (1, stop - start), 1) + start
    return start, stop, (lanes >= head * HD) & (lanes < head * HD + HD)


def attend_kernel(heads, proj_ref, far_ref, bias_ref, att_ref, lse_ref, acc_ref, stat_ref):
    rows = proj_ref.shape[0]
    width = heads * HD
    block = 256
    acc_ref[...] = jnp.zeros_like(acc_ref)
    stat_ref[...] = jnp.zeros_like(stat_ref)
    score_factor = HD ** (-0.5) * LOG2E

    def step(i, carry):
        at = pl.ds(pl.multiple_of(i * block, block), block)
        for head in range(heads):
            start, stop, mask = head_window(head)
            query = jnp.where(mask, proj_ref[at, start:stop], jnp.zeros((), bf16))
            near = dot(query, proj_ref[:, width + start : width + stop], NT)
            far = dot(query, far_ref[:, start:stop], NT)
            near = near * score_factor + bias_ref[0:1, :rows]
            far = far * score_factor + bias_ref[0:1, rows:]
            top = jnp.maximum(
                jnp.max(near, axis=-1, keepdims=True), jnp.max(far, axis=-1, keepdims=True)
            )
            near = jnp.exp2(near - top)
            far = jnp.exp2(far - top)
            total = jnp.sum(near, axis=-1, keepdims=True) + jnp.sum(far, axis=-1, keepdims=True)
            mixed = dot(near.astype(bf16), proj_ref[:, 2 * width + start : 2 * width + stop])
            mixed = mixed + dot(far.astype(bf16), far_ref[:, width + start : width + stop])
            mixed = mixed * (1.0 / total)
            acc_ref[at, start:stop] += jnp.where(mask, mixed, 0.0)
            lane = lax.broadcasted_iota(jnp.int32, (1, 128), 1)
            stat_ref[at, :] += jnp.where(lane == head, top + jnp.log2(total), 0.0)
        return carry

    lax.fori_loop(0, rows // block, step, 0)
    att_ref[...] = acc_ref[...].astype(bf16)
    lse_ref[...] = stat_ref[...].T


def attend(proj, far, bias, heads):
    rows = proj.shape[0]
    return pl.pallas_call(
        functools.partial(attend_kernel, heads),
        in_specs=[VMEM] * 3,
        out_specs=(VMEM, VMEM),
        out_shape=(
            jax.ShapeDtypeStruct((rows, heads * HD), bf16),
            jax.ShapeDtypeStruct((128, rows), f32),
        ),
        scratch_shapes=[pltpu.VMEM((rows, heads * HD), f32), pltpu.VMEM((rows, 128), f32)],
        compiler_params=params(),
        cost_estimate=pl.CostEstimate(
            flops=4 * heads * rows * 2 * rows * 256, bytes_accessed=8 << 20, transcendentals=0
        ),
    )(proj, far, bias)


def attend_back_kernel(
    heads, proj_ref, far_ref, bias_ref, att_ref, grad_ref, lse_ref,
    dq_ref, dnear_ref, dfar_ref, key_ref, value_ref, keyt_ref, dqt_ref, dot_ref, dkv_ref,
):
    rows = proj_ref.shape[0]
    width = heads * HD
    block = 256
    score_factor = HD ** (-0.5) * LOG2E
    key_ref[:rows] = proj_ref[:, width : 2 * width]
    key_ref[rows:] = far_ref[:, :width]
    value_ref[:rows] = proj_ref[:, 2 * width :]
    value_ref[rows:] = far_ref[:, width:]
    keyt_ref[...] = key_ref[...].T
    dqt_ref[...] = jnp.zeros_like(dqt_ref)
    dkv_ref[...] = jnp.zeros_like(dkv_ref)
    product = grad_ref[...].astype(f32) * att_ref[...].astype(f32)
    high = product.astype(bf16)
    low = (product - high.astype(f32)).astype(bf16)
    lane = lax.broadcasted_iota(jnp.int32, (16, width), 1)
    row = lax.broadcasted_iota(jnp.int32, (16, width), 0)
    pick = jnp.where((lane >= row * HD) & (lane < row * HD + HD), 1.0, 0.0).astype(bf16)
    dot_ref[...] = dot(pick, high, NT) + dot(pick, low, NT)

    def step(i, carry):
        at = pl.ds(pl.multiple_of(i * block, block), block)
        bias = bias_ref[at, 0:1]
        for head in range(heads):
            start, stop, mask = head_window(head)
            zero = jnp.zeros((), bf16)
            query = jnp.where(mask, proj_ref[:, start:stop], zero)
            grad = jnp.where(mask, grad_ref[:, start:stop], zero)
            scores = dot(key_ref[at, start:stop], query, NT) * score_factor + bias
            probs = jnp.exp2(scores - lse_ref[head : head + 1, :])
            grad_probs = dot(value_ref[at, start:stop], grad, NT)
            grad_scores = (probs * (grad_probs - dot_ref[head : head + 1, :])).astype(bf16)
            dkv_ref[at, start:stop] += dot(grad_scores, query)
            dkv_ref[at, width + start : width + stop] += dot(probs.astype(bf16), grad)
            keyt = keyt_ref[head * HD : head * HD + HD, at]
            dqt_ref[head * HD : head * HD + HD, :] += dot(keyt, grad_scores)
        return carry

    lax.fori_loop(0, 2 * rows // block, step, 0)
    scale = HD ** (-0.5)
    dq_ref[...] = (dqt_ref[...].T * scale).astype(bf16)
    dnear_ref[:, :width] = dkv_ref[:rows, :width] * scale
    dnear_ref[:, width:] = dkv_ref[:rows, width:]
    dfar_ref[:, :width] = (dkv_ref[rows:, :width] * scale).astype(bf16)
    dfar_ref[:, width:] = dkv_ref[rows:, width:].astype(bf16)


def attend_back(proj, far, bias, attended, grad, lse, heads):
    rows = proj.shape[0]
    width = heads * HD
    return pl.pallas_call(
        functools.partial(attend_back_kernel, heads),
        in_specs=[VMEM] * 6,
        out_specs=(VMEM, VMEM, VMEM),
        out_shape=(
            jax.ShapeDtypeStruct((rows, width), bf16),
            jax.ShapeDtypeStruct((rows, 2 * width), f32),
            jax.ShapeDtypeStruct((rows, 2 * width), bf16),
        ),
        scratch_shapes=[
            pltpu.VMEM((2 * rows, width), bf16),
            pltpu.VMEM((2 * rows, width), bf16),
            pltpu.VMEM((width, 2 * rows), bf16),
            pltpu.VMEM((width, rows), f32),
            pltpu.VMEM((16, rows), f32),
            pltpu.VMEM((2 * rows, 2 * width), f32),
        ],
        compiler_params=params(),
        cost_estimate=pl.CostEstimate(
            flops=10 * heads * rows * 2 * rows * 256, bytes_accessed=16 << 20, transcendentals=0
        ),
    )(proj, far, bias, attended, grad, lse)


def residual_kernel(x_ref, own_ref, oth_ref, wa_ref, wb_ref, vec_ref, r_ref, n_ref):
    mixed = dot(own_ref[...], wa_ref[...], NT) + dot(oth_ref[...], wb_ref[...], NT)
    residual = x_ref[...].astype(f32) + (mixed + vec_ref[0:1, :])
    r_ref[...] = residual
    hat, _ = normalize(residual)
    n_ref[...] = (hat * vec_ref[1:2, :] + vec_ref[2:3, :]).astype(bf16)


def residual_step(x_all, own, oth, weights, width, vectors):
    rows, model = x_all.shape
    block = 128
    return pl.pallas_call(
        residual_kernel,
        grid=(rows // block,),
        in_specs=[
            pl.BlockSpec((block, model), lambda i: (i, 0)),
            pl.BlockSpec((block, width), lambda i: (i, 0)),
            pl.BlockSpec((block, width), lambda i: ((i + rows // block // 2) % (rows // block), 0)),
            pl.BlockSpec((model, width), lambda i: (0, 0)),
            pl.BlockSpec((model, width), lambda i: (0, 1)),
            pl.BlockSpec(vectors.shape, lambda i: (0, 0)),
        ],
        out_specs=(
            pl.BlockSpec((block, model), lambda i: (i, 0)),
            pl.BlockSpec((block, model), lambda i: (i, 0)),
        ),
        out_shape=(
            jax.ShapeDtypeStruct((rows, model), f32),
            jax.ShapeDtypeStruct((rows, model), bf16),
        ),
        compiler_params=params(),
        cost_estimate=pl.CostEstimate(
            flops=4 * rows * model * width, bytes_accessed=12 << 20, transcendentals=0
        ),
    )(x_all, own, oth, weights, weights, vectors)


def hidden_kernel(blocks, n_ref, g_ref, we_ref, wc_ref, b_ref, act_ref, pre_ref, sum_ref, own_ref, oth_ref, acc_ref):
    k = pl.program_id(0)
    rows = n_ref.shape[0]
    half = rows // 2
    piece = 256

    @pl.when(k == 0)
    def _():
        acc_ref[...] = jnp.zeros_like(acc_ref)

    total = jnp.zeros((1, b_ref.shape[1]), f32)
    for i in range(rows // piece):
        at = slice(i * piece, (i + 1) * piece)
        pre = dot(n_ref[at], we_ref[...]) + b_ref[...]
        back = dot(g_ref[at], wc_ref[...])
        cdf = 0.5 + 0.5 * lax.erf(pre * (0.5**0.5))
        density = jnp.exp(pre * pre * -0.5) * 0.3989422804014327
        act_ref[at] = (pre * cdf).astype(bf16)
        low = (back * (cdf + pre * density)).astype(bf16)
        pre_ref[at] = low
        total = total + jnp.sum(low.astype(f32), axis=0, keepdims=True)
        acc_ref[at] += dot(low, we_ref[...], NT)
    sum_ref[...] = total

    @pl.when(k == blocks - 1)
    def _():
        own_ref[...] = acc_ref[:half]
        oth_ref[...] = acc_ref[half:].astype(bf16)


def hidden_step(normed, grad, weights, expand_at, contract_at, width, bias):
    rows, model = normed.shape
    block = 256
    blocks = width // block
    half = rows // 2
    fixed = lambda k: (0, 0)
    return pl.pallas_call(
        functools.partial(hidden_kernel, blocks),
        grid=(blocks,),
        in_specs=[
            pl.BlockSpec((rows, model), fixed),
            pl.BlockSpec((rows, model), fixed),
            pl.BlockSpec((model, block), lambda k: (0, expand_at // block + k)),
            pl.BlockSpec((model, block), lambda k: (0, contract_at // block + k)),
            pl.BlockSpec((1, block), lambda k: (0, k)),
        ],
        out_specs=(
            pl.BlockSpec((rows, block), lambda k: (0, k)),
            pl.BlockSpec((rows, block), lambda k: (0, k)),
            pl.BlockSpec((1, block), lambda k: (0, k)),
            pl.BlockSpec((half, model), fixed),
            pl.BlockSpec((half, model), fixed),
        ),
        out_shape=(
            jax.ShapeDtypeStruct((rows, width), bf16),
            jax.ShapeDtypeStruct((rows, width), bf16),
            jax.ShapeDtypeStruct((1, width), f32),
            jax.ShapeDtypeStruct((half, model), f32),
            jax.ShapeDtypeStruct((half, model), bf16),
        ),
        scratch_shapes=[pltpu.VMEM((rows, model), f32)],
        compiler_params=params(),
        cost_estimate=pl.CostEstimate(
            flops=6 * rows * model * width, bytes_accessed=28 << 20, transcendentals=0
        ),
    )(normed, grad, weights, weights, bias)


def norm_back_kernel(round_low, own_ref, oth_ref, base_ref, add_ref, gain_ref, *outs):
    i = pl.program_id(0)
    grad = own_ref[...].astype(f32) + oth_ref[...].astype(f32)
    hat, inverse = normalize(base_ref[...].astype(f32))
    scaled = grad * gain_ref[...]
    first = jnp.mean(scaled, axis=-1, keepdims=True)
    second = jnp.mean(scaled * hat, axis=-1, keepdims=True)
    result = add_ref[...].astype(f32) + inverse * (scaled - first - hat * second)
    outs[0][...] = result
    sums = outs[-1]

    @pl.when(i == 0)
    def _():
        sums[...] = jnp.zeros_like(sums)

    sums[0:1] += jnp.sum(grad * hat, axis=0, keepdims=True)
    sums[1:2] += jnp.sum(grad, axis=0, keepdims=True)
    if round_low:
        low = result.astype(bf16)
        outs[1][...] = low
        sums[2:3] += jnp.sum(low.astype(f32), axis=0, keepdims=True)


def norm_back(own, oth, base, add, gain, round_low):
    rows, model = own.shape
    block = 128
    spec = pl.BlockSpec((block, model), lambda i: (i, 0))
    outs = [jax.ShapeDtypeStruct((rows, model), f32)]
    if round_low:
        outs.append(jax.ShapeDtypeStruct((rows, model), bf16))
    outs.append(jax.ShapeDtypeStruct((8, model), f32))
    return pl.pallas_call(
        functools.partial(norm_back_kernel, round_low),
        grid=(rows // block,),
        in_specs=[spec] * 4 + [pl.BlockSpec((1, model), lambda i: (0, 0))],
        out_specs=tuple([spec] * (len(outs) - 1) + [pl.BlockSpec((8, model), lambda i: (0, 0))]),
        out_shape=tuple(outs),
        compiler_params=params(),
    )(own, oth, base, add, gain)


def forward_kernel(
    x_in, g_in, s_in, wa, wo, we, wc, bias_ref,
    inner_out, outer_out, n1_out, proj_out, far_out, att_out, lse_ref, res_out, n2_out, g_out,
    act_out, pre_out, esum_ref, dn_own, dn_oth, ho_own, ho_oth, vec_ref,
    so, ina, oa, ob, la, xb, gb, n1, proj, far, tb, eb, acc, stat, att, atto, res, n2, stage, dn, ho,
    ld, ss, sr, zs, zr, xs, xr, cs, cr, ys, yr, fs, fr, outs,
):
    f = lax.axis_index("fsdp")
    c = lax.axis_index("ctx")
    y = lax.axis_index("tp")
    z, x = f // 2, f % 2
    rows, model = xb.shape
    slot = rows // 2
    width = wo.shape[2]
    hidden = we.shape[2]
    each = wa.shape[1] * 2
    blocks = la.shape[0] // 2
    block = la.shape[-1]
    a_count, a_width = ina.shape[0], ina.shape[-1]
    heads = width // HD
    sibling = (f, 1 - c, y)
    across = (z * 2 + (1 - x), c, y)
    partner = (f, c, 1 - y)
    column = [(((z + d) % 4) * 2 + x, c, y) for d in (1, 2, 3)]
    others = [((f + d) % 8, c, y) for d in range(1, 8)]

    def remote(src, dst, s, r, dev):
        copy = pltpu.make_async_remote_copy(
            src_ref=src, dst_ref=dst, send_sem=s, recv_sem=r, device_id=dev, device_id_type=MESH
        )
        copy.start()
        return copy

    def local(src, dst, s):
        copy = pltpu.make_async_copy(src, dst, s)
        copy.start()
        return copy

    def taken(ref, sem):
        pltpu.make_async_copy(ref, ref, sem).wait()

    order = list(range(1, a_count)) + [0]
    own_x = local(x_in, xb.at[pl.ds(0, slot)], ld.at[0])
    own_s = local(s_in, so.at[f], ld.at[1])
    own_g = local(g_in, gb.at[pl.ds(0, slot)], ld.at[2])
    own_o = local(wo.at[c], oa.at[z, x, c], ld.at[3])
    own_a = [
        local(wa.at[c, :, pl.ds(k * a_width, a_width)], ina.at[k, z, x, c], ld.at[4 + k])
        for k in order
    ]
    own_l = [
        local(
            (we if j % 2 == 0 else wc).at[c, :, pl.ds(j // 2 * block, block)],
            la.at[j, z, x, c],
            ld.at[4 + a_count + j],
        )
        for j in range(2 * blocks)
    ]
    bar = pltpu.get_barrier_semaphore()
    for p in others + [sibling, partner]:
        pl.semaphore_signal(bar, 1, device_id=p, device_id_type=MESH)
    pl.semaphore_wait(bar, 9)

    def over_z(q, buf):
        piece = buf.at[z, x, c]
        return [remote(piece, piece, zs.at[q, d], zr.at[q], column[d]) for d in range(3)]

    def over_x(q, buf):
        taken(buf.at[pl.ds(0, 3), 0, 0], zr.at[q])
        remote(buf.at[:, x, c], buf.at[:, x, c], xs.at[q], xr.at[q], across)

    def over_c(q, buf):
        taken(buf.at[:, 0, 0], xr.at[q])
        remote(buf.at[:, :, c], buf.at[:, :, c], cs.at[q], cr.at[q], sibling)

    def ready(q, buf):
        taken(buf.at[:, :, 0], cr.at[q])

    sent = []
    own_s.wait()
    sent += [remote(so.at[f], so.at[f], ss.at[d], sr.at[d], others[d]) for d in range(7)]
    own_x.wait()
    sent.append(
        remote(xb.at[pl.ds(0, slot)], xb.at[pl.ds(slot, slot)], ys.at[0], yr.at[0], partner)
    )
    a_at = {}
    for q, k in enumerate(order):
        own_a[q].wait()
        sent += over_z(q, ina.at[k])
        a_at[q] = ina.at[k]
    o_q = a_count
    l_q = a_count + 1
    own_o.wait()
    sent += over_z(o_q, oa)
    for j in range(2 * blocks):
        own_l[j].wait()
        sent += over_z(l_q + j, la.at[j])
    own_g.wait()
    sent.append(
        remote(gb.at[pl.ds(0, slot)], gb.at[pl.ds(slot, slot)], ys.at[1], yr.at[1], partner)
    )

    for d in range(7):
        taken(so.at[(f - d - 1 + 8) % 8], sr.at[d])
    lanes = so.shape[2]
    step_row = lax.broadcasted_iota(jnp.int32, (lanes, model), 0)
    step_col = lax.broadcasted_iota(jnp.int32, (lanes, model), 1)
    total = jnp.zeros((so.shape[1], model), f32)
    for i in range(8):
        pick = (step_col == step_row + i * each) & (step_row < each)
        total = total + dot(so[i], jnp.where(pick, 1.0, 0.0).astype(bf16))
    vec_ref[...] = total
    per = hidden // 4
    step_row = lax.broadcasted_iota(jnp.int32, (lanes, per), 0)
    step_col = lax.broadcasted_iota(jnp.int32, (lanes, per), 1)
    for i in range(4):
        total = jnp.zeros((so.shape[1], per), f32)
        which = lax.broadcasted_iota(jnp.int32, (so.shape[1], 1), 0)
        for r in range(per // each):
            pick = (step_col == step_row + r * each) & (step_row < each)
            row = jnp.where(which == 8 + r, so[4 * y + i], jnp.zeros((), bf16))
            total = total + dot(row, jnp.where(pick, 1.0, 0.0).astype(bf16))
        eb[:, i * per : (i + 1) * per] = jnp.sum(total, axis=0, keepdims=True)
    near = pl.ds(pl.multiple_of(y * width, 128), width)
    tb[:, :width] = vec_ref[2:3, near]
    tb[:, width : 2 * width] = jnp.zeros((1, width), f32)
    tb[:, 2 * width :] = vec_ref[3:4, near]

    def first_norm(start):
        def body(i, carry):
            at = pl.ds(pl.multiple_of(start + i * 128, 128), 128)
            hat, _ = normalize(xb[at].astype(f32))
            n1[at] = (hat * vec_ref[0:1] + vec_ref[1:2]).astype(bf16)
            return carry

        lax.fori_loop(0, slot // 128, body, 0)

    first_norm(0)
    over_x(0, a_at[0])
    over_x(1, a_at[1])
    over_c(0, a_at[0])
    over_x(2, a_at[2])
    over_c(1, a_at[1])
    over_x(3, a_at[3])
    over_c(2, a_at[2])
    taken(xb.at[pl.ds(slot, slot)], yr.at[0])
    first_norm(slot)

    def project_chunk(q):
        k = order[q]
        ready(q, a_at[q])
        cols = slice(k * a_width, (k + 1) * a_width)

        def body(i, carry):
            at = pl.ds(pl.multiple_of(i * 256, 256), 256)
            proj[at, cols] = (dot(n1[at], ina[k].reshape(model, a_width)) + tb[:, cols]).astype(bf16)
            return carry

        lax.fori_loop(0, rows // 256, body, 0)
        start, stop = max(k * a_width, width), (k + 1) * a_width
        if start < stop:
            sent.append(
                remote(
                    proj.at[:, pl.ds(start, stop - start)],
                    far.at[:, pl.ds(start - width, stop - start)],
                    fs.at[k],
                    fr.at[k],
                    sibling,
                )
            )

    project_chunk(0)
    project_chunk(1)
    over_x(4, a_at[4])
    over_c(3, a_at[3])
    project_chunk(2)
    project_chunk(3)
    over_c(4, a_at[4])
    over_x(o_q, oa)
    project_chunk(4)
    writes = [local(n1, n1_out, outs.at[0]), local(proj, proj_out, outs.at[1])]
    for k in range(1, a_count):
        start, stop = max(k * a_width, width), (k + 1) * a_width
        taken(far.at[:, pl.ds(start - width, stop - start)], fr.at[k])
    writes.append(local(far, far_out, outs.at[2]))

    stat[...] = jnp.zeros_like(stat)
    score_factor = HD ** (-0.5) * LOG2E
    tall = acc.shape[0]

    def attend_step(i, carry):
        at = pl.ds(pl.multiple_of(i * tall, tall), tall)
        acc[...] = jnp.zeros_like(acc)
        for head in range(heads):
            start, stop, mask = head_window(head)
            query = jnp.where(mask, proj[at, start:stop], jnp.zeros((), bf16))
            a = dot(query, proj[:, width + start : width + stop], NT)
            b = dot(query, far[:, start:stop], NT)
            a = a * score_factor + bias_ref[0:1, :rows]
            b = b * score_factor + bias_ref[0:1, rows:]
            top = jnp.maximum(
                jnp.max(a, axis=-1, keepdims=True), jnp.max(b, axis=-1, keepdims=True)
            )
            a = jnp.exp2(a - top)
            b = jnp.exp2(b - top)
            total = jnp.sum(a, axis=-1, keepdims=True) + jnp.sum(b, axis=-1, keepdims=True)
            mixed = dot(a.astype(bf16), proj[:, 2 * width + start : 2 * width + stop])
            mixed = mixed + dot(b.astype(bf16), far[:, width + start : width + stop])
            mixed = mixed * (1.0 / total)
            acc[:, start:stop] += jnp.where(mask, mixed, 0.0)
            lane = lax.broadcasted_iota(jnp.int32, (1, 128), 1)
            stat[at, :] += jnp.where(lane == head, top + jnp.log2(total), 0.0)
        att[at] = acc[...].astype(bf16)
        remote(att.at[at], atto.at[at], ys.at[3 + i], yr.at[3 + i], partner)
        over_x(l_q + i, la.at[i])

        @pl.when(i == 0)
        def _():
            over_c(o_q, oa)
            remote(oa.at[:, :, c], ob.at[:, :, c], ys.at[2], yr.at[2], partner)

        @pl.when(i > 0)
        def _():
            over_c(l_q + i - 1, la.at[i - 1])

        return carry

    steps = rows // tall
    lax.fori_loop(0, steps, attend_step, 0)
    lse_ref[...] = stat[...].T
    writes.append(local(att, att_out, outs.at[3]))
    over_x(l_q + 3, la.at[3])
    over_c(l_q + 2, la.at[2])
    taken(ob.at[:, :, c], yr.at[2])
    b_q = zs.shape[0] - 1
    remote(ob.at[:, :, c], ob.at[:, :, c], cs.at[b_q], cr.at[b_q], sibling)
    over_x(l_q + 4, la.at[4])
    over_c(l_q + 3, la.at[3])
    over_x(l_q + 5, la.at[5])
    over_c(l_q + 4, la.at[4])
    ready(o_q, oa)
    ready(b_q, ob)
    writes.append(local(oa, outer_out, outs.at[4]))
    for q, k in enumerate(order):
        writes.append(
            local(ina.at[k], inner_out.at[:, :, :, :, pl.ds(k * a_width, a_width)], outs.at[5 + k])
        )
    for i in range(steps):
        at = pl.ds(i * tall, tall)
        taken(atto.at[at], yr.at[3 + i])

    def residual_half(i):
        at = slice(i * slot, (i + 1) * slot)
        back = slice((1 - i) * slot, (2 - i) * slot)
        mixed = dot(att[at], oa[...].reshape(model, width), NT)
        res[at] = mixed + dot(atto[back], ob[...].reshape(model, width), NT)

        def body(j, carry):
            row = pl.ds(pl.multiple_of(i * slot + j * 128, 128), 128)
            value = xb[row].astype(f32) + (res[row] + vec_ref[4:5])
            res[row] = value
            hat, _ = normalize(value)
            n2[row] = (hat * vec_ref[5:6] + vec_ref[6:7]).astype(bf16)
            return carry

        lax.fori_loop(0, slot // 128, body, 0)

    residual_half(0)
    over_x(l_q + 6, la.at[6])
    over_c(l_q + 5, la.at[5])
    residual_half(1)
    late_writes = [
        local(res.at[pl.ds(0, slot)], res_out, outs.at[5 + a_count]),
        local(n2, n2_out, outs.at[6 + a_count]),
    ]
    taken(gb.at[pl.ds(slot, slot)], yr.at[1])
    late_writes.append(local(gb, g_out, outs.at[7 + a_count]))
    dn[...] = jnp.zeros_like(dn)
    ho[...] = jnp.zeros_like(ho)
    s_at = 8 + a_count

    def hidden_step_in(b, carry):
        ready(l_q + 2 * b, la.at[2 * b])
        ready(l_q + 2 * b + 1, la.at[2 * b + 1])
        turn = b % 2
        cols = pl.ds(pl.multiple_of(b * block, block), block)

        @pl.when(b > 1)
        def _():
            taken(stage.at[0, turn], outs.at[s_at + turn])
            taken(stage.at[1, turn], outs.at[s_at + 2 + turn])

        shift = eb[:, cols]
        total = jnp.zeros((1, block), f32)
        for i in range(rows // 256):
            at = slice(i * 256, (i + 1) * 256)
            pre = dot(n2[at], la[2 * b].reshape(model, block)) + shift
            back = dot(gb[at], la[2 * b + 1].reshape(model, block))
            cdf = 0.5 + 0.5 * lax.erf(pre * (0.5**0.5))
            density = jnp.exp(pre * pre * -0.5) * 0.3989422804014327
            low = (back * (cdf + pre * density)).astype(bf16)
            active = (pre * cdf).astype(bf16)
            stage[0, turn, at] = active
            stage[1, turn, at] = low
            total = total + jnp.sum(low.astype(f32), axis=0, keepdims=True)
            dn[at] += dot(low, la[2 * b].reshape(model, block), NT)
            ho[at] += dot(active, la[2 * b + 1].reshape(model, block), NT)
        esum_ref[:, cols] = total
        local(stage.at[0, turn], act_out.at[:, cols], outs.at[s_at + turn])
        local(stage.at[1, turn], pre_out.at[:, cols], outs.at[s_at + 2 + turn])

        @pl.when(b < 3)
        def _():
            over_x(l_q + 7 + b, la.at[7 + b])

        @pl.when(b < 4)
        def _():
            over_c(l_q + 6 + b, la.at[6 + b])

        return carry

    lax.fori_loop(0, blocks, hidden_step_in, 0)
    for copy in writes:
        copy.wait()
    n1[:slot] = dn[slot:].astype(bf16)
    n1[slot:] = ho[slot:].astype(bf16)
    last = [
        local(dn.at[pl.ds(0, slot)], dn_own, ld.at[0]),
        local(ho.at[pl.ds(0, slot)], ho_own, ld.at[1]),
        local(n1.at[pl.ds(0, slot)], dn_oth, ld.at[2]),
        local(n1.at[pl.ds(slot, slot)], ho_oth, ld.at[3]),
    ]
    for turn in range(2):
        taken(stage.at[0, turn], outs.at[s_at + turn])
        taken(stage.at[1, turn], outs.at[s_at + 2 + turn])
    for copy in late_writes + last:
        copy.wait()
    for copy in sent:
        copy.wait_send()
    for q in range(zs.shape[0]):
        if q < a_count:
            buf = a_at[q]
        elif q == o_q:
            buf = oa
        elif q == b_q:
            buf = ob
        else:
            buf = la.at[q - l_q]
        taken(buf.at[:, :, 0], cs.at[q])
        if q != b_q:
            taken(buf.at[:, 0, 0], xs.at[q])
    taken(oa.at[:, :, 0], ys.at[2])
    for i in range(steps):
        taken(att.at[pl.ds(i * tall, tall)], ys.at[3 + i])


def forward(x_own, g_own, smalls, wa, wo, we, wc, bias):
    slot, model = x_own.shape
    rows = 2 * slot
    each = wa.shape[0]
    width, hidden = wo.shape[1], we.shape[1]
    half = each // 2
    a_width, block = 384, 512
    a_count, blocks = 3 * width // a_width, hidden // block
    grid = (4, 2, 2, half)
    chunks = a_count + 2 + 2 * blocks
    sem = pltpu.SemaphoreType.DMA
    out = jax.ShapeDtypeStruct

    def halves(w):
        return w.reshape(2, half, w.shape[1])

    return pl.pallas_call(
        forward_kernel,
        in_specs=[HBM] * 7 + [VMEM],
        out_specs=(HBM,) * 6 + (VMEM,) + (HBM,) * 5 + (VMEM,) + (HBM,) * 4 + (VMEM,),
        out_shape=(
            out(grid + (3 * width,), bf16),
            out(grid + (width,), bf16),
            out((rows, model), bf16),
            out((rows, 3 * width), bf16),
            out((rows, 2 * width), bf16),
            out((rows, width), bf16),
            out((128, rows), f32),
            out((slot, model), f32),
            out((rows, model), bf16),
            out((rows, model), bf16),
            out((rows, hidden), bf16),
            out((rows, hidden), bf16),
            out((1, hidden), f32),
            out((slot, model), f32),
            out((slot, model), bf16),
            out((slot, model), f32),
            out((slot, model), bf16),
            out((16, model), f32),
        ),
        scratch_shapes=[
            pltpu.VMEM((8,) + smalls.shape, bf16),
            pltpu.VMEM((a_count,) + grid + (a_width,), bf16),
            pltpu.VMEM(grid + (width,), bf16),
            pltpu.VMEM(grid + (width,), bf16),
            pltpu.VMEM((2 * blocks,) + grid + (block,), bf16),
            pltpu.VMEM((rows, model), bf16),
            pltpu.VMEM((rows, model), bf16),
            pltpu.VMEM((rows, model), bf16),
            pltpu.VMEM((rows, 3 * width), bf16),
            pltpu.VMEM((rows, 2 * width), bf16),
            pltpu.VMEM((1, 3 * width), f32),
            pltpu.VMEM((1, hidden), f32),
            pltpu.VMEM((256, width), f32),
            pltpu.VMEM((rows, 128), f32),
            pltpu.VMEM((rows, width), bf16),
            pltpu.VMEM((rows, width), bf16),
            pltpu.VMEM((rows, model), f32),
            pltpu.VMEM((rows, model), bf16),
            pltpu.VMEM((2, 2, rows, block), bf16),
            pltpu.VMEM((rows, model), f32),
            pltpu.VMEM((rows, model), f32),
            sem((4 + a_count + 2 * blocks,)),
            sem((7,)),
            sem((7,)),
            sem((chunks, 3)),
            sem((chunks,)),
            sem((chunks,)),
            sem((chunks,)),
            sem((chunks,)),
            sem((chunks,)),
            sem((3 + rows // 256,)),
            sem((3 + rows // 256,)),
            sem((a_count,)),
            sem((a_count,)),
            sem((12 + a_count,)),
        ],
        compiler_params=params(collective_id=1, has_side_effects=True),
    )(x_own, g_own, smalls, halves(wa), halves(wo), halves(we), halves(wc), bias)


def key_biases(share, slot, length, tp_rank, ctx_rank):
    places = lax.iota(jnp.int32, slot)
    pieces = []
    for ctx in (ctx_rank, 1 - ctx_rank):
        for tp in (tp_rank, 1 - tp_rank):
            start = (ctx * 2 + tp) * share
            valid = (places < share) & (start + places < length)
            pieces.append(jnp.where(valid, 0.0, masked_score).astype(f32))
    return jnp.concatenate(pieces)


def forward_parts(x_own, grad_own, smalls, inner, outer_t, expand_weight, contract_t, bias):
    slot, model = x_own.shape
    rows_each = inner.shape[0]
    half_each = rows_each // 2
    width, hidden = outer_t.shape[1], expand_weight.shape[1]
    heads = width // HD
    tp_rank = lax.axis_index("tp")
    ctx_rank = lax.axis_index("ctx")
    x_all = jnp.concatenate([x_own, swap(x_own, "tp")], axis=0)
    grad_all = jnp.concatenate([grad_own, swap(grad_own, "tp")], axis=0)
    inner = lax.all_gather(inner, "fsdp", axis=0, tiled=True)
    smalls_all = lax.all_gather(smalls, "fsdp", axis=0)
    late = jnp.concatenate([outer_t, swap(outer_t, "tp"), expand_weight, contract_t], axis=1)
    late = lax.dynamic_slice_in_dim(late, ctx_rank * half_each, half_each, 0)
    late = lax.all_gather(late, ("fsdp", "ctx"), axis=0, tiled=True)
    expand_at = 2 * width
    contract_at = 2 * width + hidden
    smalls_all = smalls_all[:, :, :rows_each].astype(f32)
    vectors = jnp.transpose(smalls_all[:, :8], (1, 0, 2)).reshape(8, model)
    expand_rows = smalls_all[:, 8 : 8 + hidden * 2 // model].reshape(1, 2 * hidden)
    expand_local = lax.dynamic_slice_in_dim(expand_rows, tp_rank * hidden, hidden, 1)
    pair = lax.dynamic_slice_in_dim(vectors[2:4], tp_rank * width, width, 1)
    triple = jnp.concatenate([pair[0:1], jnp.zeros((1, width), f32), pair[1:2]], axis=1)
    normed_one, proj = project(x_all, vectors[0:1], vectors[1:2], inner, triple)
    far = swap(proj[:, width:], "ctx")
    attended, lse = attend(proj, far, jnp.broadcast_to(bias[None], (8, bias.shape[0])), heads)
    attended_oth = swap(attended, "tp")
    residual, normed_two = residual_step(x_all, attended, attended_oth, late, width, vectors[4:7])
    activated, pre_grad, expand_sum, normed_own, normed_oth = hidden_step(
        normed_two, grad_all, late, expand_at, contract_at, hidden, expand_local
    )
    contracted = dot(activated, late[:, contract_at:], NT)
    return (
        inner, late[:, :width], normed_one, proj, far, attended, lse, residual[:slot], normed_two,
        grad_all, activated, pre_grad, expand_sum, normed_own, normed_oth, contracted[:slot],
        contracted[slot:].astype(bf16), vectors,
    )


def per_device(
    hidden_in,
    valid_lengths,
    output_grad,
    first_gain,
    first_shift,
    attention_in,
    query_value_bias,
    attention_out,
    attention_bias,
    second_gain,
    second_shift,
    expand_weight,
    expand_bias,
    contract_weight,
    contract_bias,
):
    _, share, model = hidden_in.shape
    tp_rank = lax.axis_index("tp")
    ctx_rank = lax.axis_index("ctx")
    fsdp_count = lax.axis_size("fsdp")
    rows_each = attention_in.shape[0]
    width = attention_in.shape[2]
    heads = width // HD
    hidden = expand_weight.shape[1]
    slot = -(-share // 128) * 128
    length = valid_lengths[0]

    def padded(value):
        return jnp.pad(value, ((0, slot - share), (0, 0)))

    own_start = (ctx_rank * 2 + tp_rank) * share
    token_valid = (own_start + lax.iota(jnp.int32, share)) < length
    grad_own = jnp.where(token_valid[:, None], output_grad[0], jnp.zeros((), bf16))
    grad_own = padded(grad_own)
    x_own = padded(hidden_in[0])

    smalls = jnp.concatenate(
        [
            jnp.stack(
                [
                    first_gain,
                    first_shift,
                    query_value_bias[0],
                    query_value_bias[1],
                    attention_bias,
                    second_gain,
                    second_shift,
                    contract_bias,
                ]
            ),
            expand_bias.reshape(-1, rows_each),
        ],
        axis=0,
    )
    smalls = jnp.pad(smalls, ((0, 16 - smalls.shape[0]), (0, -rows_each % 128)))
    bias = key_biases(share, slot, length, tp_rank, ctx_rank)
    inner = attention_in.reshape(rows_each, 3 * width)
    outer_t, contract_t = attention_out.T, contract_weight.T
    if fsdp_count == 8 and rows_each == 160:
        (
            inner, outer_t, normed_one, proj, far, attended, lse, residual, normed_two, grad_all,
            activated, pre_grad, expand_sum, normed_own, normed_oth, out_own, out_oth, vectors,
        ) = forward(
            x_own, grad_own, smalls, inner, outer_t, expand_weight, contract_t,
            jnp.broadcast_to(bias[None], (8, bias.shape[0])),
        )
        inner = inner.reshape(model, 3 * width)
        outer_t = outer_t.reshape(model, width)
    else:
        (
            inner, outer_t, normed_one, proj, far, attended, lse, residual, normed_two, grad_all,
            activated, pre_grad, expand_sum, normed_own, normed_oth, out_own, out_oth, vectors,
        ) = forward_parts(
            x_own, grad_own, smalls, inner, outer_t, expand_weight, contract_t, bias
        )
    normed_oth = swap(normed_oth, "tp")
    grad_contract_t = dot(grad_all, activated, TN).astype(bf16)
    grad_expand = dot(normed_two, pre_grad, TN).astype(bf16)
    normed_own, normed_oth, grad_late = lax.optimization_barrier(
        (normed_own, normed_oth, jnp.concatenate([grad_expand, grad_contract_t], axis=1))
    )
    grad_late = lax.psum_scatter(
        grad_late, ("fsdp", "ctx"), scatter_dimension=0, tiled=True
    ).astype(f32)
    contracted = out_own + swap(out_oth, "tp").astype(f32)
    hidden_out = (residual + (contracted + vectors[7:8])).astype(bf16)

    residual_grad, residual_low, sums_two = norm_back(
        normed_own, normed_oth, residual, grad_own, vectors[5:6], True
    )
    residual_low_all = jnp.concatenate([residual_low, swap(residual_low, "tp")], axis=0)
    attended_grad = dot(residual_low_all, outer_t).astype(bf16)
    grad_outer_t = dot(residual_low_all, attended, TN).astype(bf16)

    grad_query, grad_near, grad_far = attend_back(
        proj, far, jnp.broadcast_to(bias[:, None], (bias.shape[0], 128)), attended, attended_grad, lse, heads
    )
    grad_near = (grad_near + swap(grad_far, "ctx").astype(f32)).astype(bf16)
    grad_proj = jnp.concatenate([grad_query, grad_near], axis=1)
    normed_grad = dot(grad_proj, inner, NT)
    normed_grad_oth = swap(normed_grad[slot:].astype(bf16), "tp")
    grad_inner = dot(normed_one, grad_proj, TN).astype(bf16)
    proj_sums = jnp.sum(grad_proj.astype(f32), axis=0)
    grad_inner, grad_outer_t = scatter_sums([grad_inner, grad_outer_t], 384, fsdp_count)
    hidden_grad, sums_one = norm_back(
        normed_grad[:slot], normed_grad_oth, x_own, residual_grad, vectors[0:1], False
    )

    def placed(value, total):
        zero = jnp.zeros((total,), f32)
        return lax.dynamic_update_slice_in_dim(zero, value, tp_rank * value.shape[0], 0)

    owned = model // (fsdp_count * 2)
    stacked = jnp.stack(
        [
            sums_one[0],
            sums_one[1],
            placed(proj_sums[:width], model),
            placed(proj_sums[2 * width :], model),
            sums_two[2],
            sums_two[0],
            sums_two[1],
            jnp.sum(grad_own.astype(f32), axis=0),
        ]
    )
    stacked = jnp.transpose(stacked.reshape(8, -1, owned), (1, 0, 2))
    expand_piece = placed(expand_sum[0], 2 * hidden).reshape(fsdp_count * 2, -1, owned)
    stacked = jnp.concatenate([stacked, expand_piece], axis=1)
    stacked = jnp.pad(stacked, ((0, 0), (0, 16 - stacked.shape[1]), (0, 128 - owned)))
    summed = sum_vectors(stacked, fsdp_count)[:, :owned]

    return (
        hidden_out[None, :share],
        hidden_grad[None, :share],
        summed[0],
        summed[1],
        grad_inner.reshape(-1, 3, width),
        summed[2:4],
        grad_outer_t.T,
        summed[4],
        summed[5],
        summed[6],
        grad_late[:, :hidden],
        summed[8 : 8 + 2 * hidden // model].reshape(-1),
        grad_late[:, hidden:].T,
        summed[7],
    )


def solution(mesh):
    return jax.shard_map(
        per_device,
        mesh=mesh,
        in_specs=(
            P("fsdp", ("ctx", "tp"), None),
            P("fsdp"),
            P("fsdp", ("ctx", "tp"), None),
            P("fsdp"),
            P("fsdp"),
            P("fsdp", None, "tp"),
            P(None, "fsdp"),
            P("tp", "fsdp"),
            P("fsdp"),
            P("fsdp"),
            P("fsdp"),
            P("fsdp", "tp"),
            P("fsdp"),
            P("tp", "fsdp"),
            P("fsdp"),
        ),
        out_specs=(
            P("fsdp", ("ctx", "tp"), None),
            P("fsdp", ("ctx", "tp"), None),
            P(("fsdp", "ctx")),
            P(("fsdp", "ctx")),
            P(("fsdp", "ctx"), None, "tp"),
            P(None, ("fsdp", "ctx")),
            P("tp", ("fsdp", "ctx")),
            P(("fsdp", "ctx")),
            P(("fsdp", "ctx")),
            P(("fsdp", "ctx")),
            P(("fsdp", "ctx"), "tp"),
            P(("fsdp", "ctx")),
            P("tp", ("fsdp", "ctx")),
            P(("fsdp", "ctx")),
        ),
        check_vma=False,
    )
```

```python
import functools

import jax
import jax.numpy as jnp
from jax import lax
from jax.experimental import pallas as pl
from jax.experimental.pallas import tpu as pltpu
from jax.sharding import PartitionSpec as P

HD = 80
epsilon = 1e-05
masked_score = -1e30
LOG2E = 1.4426950408889634
f32 = jnp.float32
bf16 = jnp.bfloat16
MESH = pl.DeviceIdType.MESH
VMEM = pl.BlockSpec(memory_space=pltpu.VMEM)
HBM = pl.BlockSpec(memory_space=pltpu.HBM)
VMEM_LIMIT = 62 * 1024 * 1024


def params(**kw):
    return pltpu.CompilerParams(vmem_limit_bytes=VMEM_LIMIT, **kw)


def dot(a, b, dims=((1,), (0,))):
    return lax.dot_general(a, b, (dims, ((), ())), preferred_element_type=f32)


NT = ((1,), (1,))
TN = ((0,), (0,))


def swap(value, axis):
    return lax.ppermute(value, axis, [(0, 1), (1, 0)])


def vector_kernel(v_ref, o_ref, got, lsem, ss, sr):
    f = lax.axis_index("fsdp")
    c = lax.axis_index("ctx")
    y = lax.axis_index("tp")
    me = (f * 2 + c) * 2 + y
    bar = pltpu.get_barrier_semaphore()

    def device(i):
        return (i // 4, (i // 2) % 2, i % 2)

    peers = [(me + d) % 32 for d in range(1, 32)]
    for p in peers:
        pl.semaphore_signal(bar, 1, device_id=device(p), device_id_type=MESH)
    pl.semaphore_wait(bar, 31)
    sent = []
    for d, p in enumerate(peers):
        copy = pltpu.make_async_remote_copy(
            src_ref=v_ref.at[p // 2],
            dst_ref=got.at[d + 1],
            send_sem=ss.at[d],
            recv_sem=sr.at[d],
            device_id=device(p),
            device_id_type=MESH,
        )
        copy.start()
        sent.append(copy)
    local = pltpu.make_async_copy(v_ref.at[me // 2], got.at[0], lsem)
    local.start()
    local.wait()
    total = got[0].astype(f32)
    for d in range(31):
        sent[d].wait_recv()
    for d in range(31):
        total = total + got[d + 1].astype(f32)
    o_ref[...] = total
    for copy in sent:
        copy.wait_send()


def sum_vectors(vectors, fsdp_count):
    if fsdp_count == 8:
        sem = pltpu.SemaphoreType.DMA
        return pl.pallas_call(
            vector_kernel,
            out_shape=jax.ShapeDtypeStruct(vectors.shape[1:], f32),
            in_specs=[VMEM],
            out_specs=VMEM,
            scratch_shapes=[
                pltpu.VMEM((32,) + vectors.shape[1:], bf16),
                sem,
                sem((31,)),
                sem((31,)),
            ],
            compiler_params=params(collective_id=2, has_side_effects=True),
        )(vectors.astype(bf16))
    partial = lax.psum(vectors, "tp")
    return lax.psum_scatter(partial, ("fsdp", "ctx"), scatter_dimension=0, tiled=False)


def scatter_kernel(spans, arrays, *refs):
    ins = refs[:arrays]
    outs = refs[arrays : 2 * arrays]
    own, near, mine, far, pair, last, lsem, cs, cr, xs, xr, zs, zr = refs[2 * arrays :]
    f = lax.axis_index("fsdp")
    c = lax.axis_index("ctx")
    y = lax.axis_index("tp")
    z, x = f // 2, f % 2
    bar = pltpu.get_barrier_semaphore()
    sibling = (f, 1 - c, y)
    across = (z * 2 + (1 - x), c, y)
    column = [None] + [(((z + d) % 4) * 2 + x, c, y) for d in (1, 2, 3)]
    for p in [sibling, across] + column[1:]:
        pl.semaphore_signal(bar, 1, device_id=p, device_id_type=MESH)
    pl.semaphore_wait(bar, 5)

    def remote(src, dst, s, r, dev):
        copy = pltpu.make_async_remote_copy(
            src_ref=src, dst_ref=dst, send_sem=s, recv_sem=r, device_id=dev, device_id_type=MESH
        )
        copy.start()
        return copy

    local, over_ctx, over_x, over_z = {}, {}, {}, {}
    for k, (a, start, width) in enumerate(spans):
        cols = pl.ds(start, width)
        fit = pl.ds(0, width)
        copy = pltpu.make_async_copy(ins[a].at[:, c, :, cols], own.at[k, :, :, fit], lsem.at[k])
        copy.start()
        local[k] = copy
        over_ctx[k] = remote(
            ins[a].at[:, 1 - c, :, cols], near.at[k, :, :, fit], cs.at[k], cr.at[k], sibling
        )

    def first(k):
        width = spans[k][2]
        local[k].wait()
        over_ctx[k].wait_recv()
        for i in range(8):
            total = own[k, i, :, :width].astype(f32) + near[k, i, :, :width].astype(f32)
            mine[k, i // 2, i % 2, :, :width] = total.astype(bf16)
        src = mine.at[k, :, 1 - x, :, pl.ds(0, width)]
        over_x[k] = remote(src, far.at[k, :, :, pl.ds(0, width)], xs.at[k], xr.at[k], across)

    def second(k):
        width = spans[k][2]
        over_x[k].wait_recv()
        for i in range(4):
            total = mine[k, i, x, :, :width].astype(f32) + far[k, i, :, :width].astype(f32)
            pair[k, i, :, :width] = total.astype(bf16)
        over_z[k] = [
            remote(
                pair.at[k, (z + d) % 4, :, pl.ds(0, width)],
                last.at[k, d - 1, :, pl.ds(0, width)],
                zs.at[k, d - 1],
                zr.at[k, d - 1],
                column[d],
            )
            for d in (1, 2, 3)
        ]

    def third(k):
        a, start, width = spans[k]
        total = pair[k, z, :, :width].astype(f32)
        for d in range(3):
            over_z[k][d].wait_recv()
            total = total + last[k, d, :, :width].astype(f32)
        outs[a][:, start : start + width] = total

    count = len(spans)
    for step in range(count + 2):
        if step < count:
            first(step)
        if 0 <= step - 1 < count:
            second(step - 1)
        if 0 <= step - 2 < count:
            third(step - 2)
    for k in range(count):
        over_ctx[k].wait_send()
        over_x[k].wait_send()
        for copy in over_z[k]:
            copy.wait_send()


def scatter_sums(grads, widest, fsdp_count):
    rows = grads[0].shape[0]
    owned = rows // (fsdp_count * 2)
    if fsdp_count == 8 and owned % 16 == 0:
        spans = []
        for a, grad in enumerate(grads):
            for start in range(0, grad.shape[1], widest):
                spans.append((a, start, min(widest, grad.shape[1] - start)))
        count = len(spans)
        sem = pltpu.SemaphoreType.DMA
        return pl.pallas_call(
            functools.partial(scatter_kernel, spans, len(grads)),
            in_specs=[HBM] * len(grads),
            out_specs=tuple([VMEM] * len(grads)),
            out_shape=tuple(jax.ShapeDtypeStruct((owned, g.shape[1]), f32) for g in grads),
            scratch_shapes=[
                pltpu.VMEM((count, 8, owned, widest), bf16),
                pltpu.VMEM((count, 8, owned, widest), bf16),
                pltpu.VMEM((count, 4, 2, owned, widest), bf16),
                pltpu.VMEM((count, 4, owned, widest), bf16),
                pltpu.VMEM((count, 4, owned, widest), bf16),
                pltpu.VMEM((count, 3, owned, widest), bf16),
            ]
            + [sem((count,))] * 5
            + [sem((count, 3))] * 2,
            compiler_params=params(collective_id=3, has_side_effects=True),
        )(*[g.reshape(8, 2, owned, g.shape[1]) for g in grads])
    whole = lax.psum_scatter(
        jnp.concatenate(grads, axis=1), ("fsdp", "ctx"), scatter_dimension=0, tiled=True
    ).astype(f32)
    edges = [sum(g.shape[1] for g in grads[:i]) for i in range(len(grads) + 1)]
    return [whole[:, a:b] for a, b in zip(edges, edges[1:])]


def normalize(values):
    centered = values - jnp.mean(values, axis=-1, keepdims=True)
    inverse = lax.rsqrt(jnp.mean(centered * centered, axis=-1, keepdims=True) + epsilon)
    return centered * inverse, inverse


def project_kernel(x_ref, gain_ref, shift_ref, w_ref, b_ref, n_ref, p_ref):
    values = x_ref[...].astype(f32)
    hat, _ = normalize(values)
    low = (hat * gain_ref[...] + shift_ref[...]).astype(bf16)
    n_ref[...] = low
    p_ref[...] = (dot(low, w_ref[...]) + b_ref[...]).astype(bf16)


def project(x_all, gain, shift, weight, bias):
    rows, model = x_all.shape
    width = weight.shape[1]
    block = 256
    fixed = lambda i: (0, 0)
    return pl.pallas_call(
        project_kernel,
        grid=(rows // block,),
        in_specs=[
            pl.BlockSpec((block, model), lambda i: (i, 0)),
            pl.BlockSpec((1, model), fixed),
            pl.BlockSpec((1, model), fixed),
            pl.BlockSpec((model, width), fixed),
            pl.BlockSpec((1, width), fixed),
        ],
        out_specs=(
            pl.BlockSpec((block, model), lambda i: (i, 0)),
            pl.BlockSpec((block, width), lambda i: (i, 0)),
        ),
        out_shape=(
            jax.ShapeDtypeStruct((rows, model), bf16),
            jax.ShapeDtypeStruct((rows, width), bf16),
        ),
        compiler_params=params(),
        cost_estimate=pl.CostEstimate(
            flops=2 * rows * model * width, bytes_accessed=12 << 20, transcendentals=0
        ),
    )(x_all, gain, shift, weight, bias)


def head_window(head):
    start = head * HD // 128 * 128
    stop = -(-(head * HD + HD) // 128) * 128
    lanes = lax.broadcasted_iota(jnp.int32, (1, stop - start), 1) + start
    return start, stop, (lanes >= head * HD) & (lanes < head * HD + HD)


def attend_kernel(heads, proj_ref, far_ref, bias_ref, att_ref, lse_ref, acc_ref, stat_ref):
    rows = proj_ref.shape[0]
    width = heads * HD
    block = 256
    acc_ref[...] = jnp.zeros_like(acc_ref)
    stat_ref[...] = jnp.zeros_like(stat_ref)
    score_factor = HD ** (-0.5) * LOG2E

    def step(i, carry):
        at = pl.ds(pl.multiple_of(i * block, block), block)
        for head in range(heads):
            start, stop, mask = head_window(head)
            query = jnp.where(mask, proj_ref[at, start:stop], jnp.zeros((), bf16))
            near = dot(query, proj_ref[:, width + start : width + stop], NT)
            far = dot(query, far_ref[:, start:stop], NT)
            near = near * score_factor + bias_ref[0:1, :rows]
            far = far * score_factor + bias_ref[0:1, rows:]
            top = jnp.maximum(
                jnp.max(near, axis=-1, keepdims=True), jnp.max(far, axis=-1, keepdims=True)
            )
            near = jnp.exp2(near - top)
            far = jnp.exp2(far - top)
            total = jnp.sum(near, axis=-1, keepdims=True) + jnp.sum(far, axis=-1, keepdims=True)
            mixed = dot(near.astype(bf16), proj_ref[:, 2 * width + start : 2 * width + stop])
            mixed = mixed + dot(far.astype(bf16), far_ref[:, width + start : width + stop])
            mixed = mixed * (1.0 / total)
            acc_ref[at, start:stop] += jnp.where(mask, mixed, 0.0)
            lane = lax.broadcasted_iota(jnp.int32, (1, 128), 1)
            stat_ref[at, :] += jnp.where(lane == head, top + jnp.log2(total), 0.0)
        return carry

    lax.fori_loop(0, rows // block, step, 0)
    att_ref[...] = acc_ref[...].astype(bf16)
    lse_ref[...] = stat_ref[...].T


def attend(proj, far, bias, heads):
    rows = proj.shape[0]
    return pl.pallas_call(
        functools.partial(attend_kernel, heads),
        in_specs=[VMEM] * 3,
        out_specs=(VMEM, VMEM),
        out_shape=(
            jax.ShapeDtypeStruct((rows, heads * HD), bf16),
            jax.ShapeDtypeStruct((128, rows), f32),
        ),
        scratch_shapes=[pltpu.VMEM((rows, heads * HD), f32), pltpu.VMEM((rows, 128), f32)],
        compiler_params=params(),
        cost_estimate=pl.CostEstimate(
            flops=4 * heads * rows * 2 * rows * 256, bytes_accessed=8 << 20, transcendentals=0
        ),
    )(proj, far, bias)


def attend_back_kernel(
    heads, proj_ref, far_ref, bias_ref, att_ref, grad_ref, lse_ref,
    dq_ref, dnear_ref, dfar_ref, key_ref, value_ref, keyt_ref, dqt_ref, dot_ref, dkv_ref,
):
    rows = proj_ref.shape[0]
    width = heads * HD
    block = 256
    score_factor = HD ** (-0.5) * LOG2E
    key_ref[:rows] = proj_ref[:, width : 2 * width]
    key_ref[rows:] = far_ref[:, :width]
    value_ref[:rows] = proj_ref[:, 2 * width :]
    value_ref[rows:] = far_ref[:, width:]
    keyt_ref[...] = key_ref[...].T
    dqt_ref[...] = jnp.zeros_like(dqt_ref)
    dkv_ref[...] = jnp.zeros_like(dkv_ref)
    product = grad_ref[...].astype(f32) * att_ref[...].astype(f32)
    high = product.astype(bf16)
    low = (product - high.astype(f32)).astype(bf16)
    lane = lax.broadcasted_iota(jnp.int32, (16, width), 1)
    row = lax.broadcasted_iota(jnp.int32, (16, width), 0)
    pick = jnp.where((lane >= row * HD) & (lane < row * HD + HD), 1.0, 0.0).astype(bf16)
    dot_ref[...] = dot(pick, high, NT) + dot(pick, low, NT)

    def step(i, carry):
        at = pl.ds(pl.multiple_of(i * block, block), block)
        bias = bias_ref[at, 0:1]
        for head in range(heads):
            start, stop, mask = head_window(head)
            zero = jnp.zeros((), bf16)
            query = jnp.where(mask, proj_ref[:, start:stop], zero)
            grad = jnp.where(mask, grad_ref[:, start:stop], zero)
            scores = dot(key_ref[at, start:stop], query, NT) * score_factor + bias
            probs = jnp.exp2(scores - lse_ref[head : head + 1, :])
            grad_probs = dot(value_ref[at, start:stop], grad, NT)
            grad_scores = (probs * (grad_probs - dot_ref[head : head + 1, :])).astype(bf16)
            dkv_ref[at, start:stop] += dot(grad_scores, query)
            dkv_ref[at, width + start : width + stop] += dot(probs.astype(bf16), grad)
            keyt = keyt_ref[head * HD : head * HD + HD, at]
            dqt_ref[head * HD : head * HD + HD, :] += dot(keyt, grad_scores)
        return carry

    lax.fori_loop(0, 2 * rows // block, step, 0)
    scale = HD ** (-0.5)
    dq_ref[...] = (dqt_ref[...].T * scale).astype(bf16)
    dnear_ref[:, :width] = dkv_ref[:rows, :width] * scale
    dnear_ref[:, width:] = dkv_ref[:rows, width:]
    dfar_ref[:, :width] = (dkv_ref[rows:, :width] * scale).astype(bf16)
    dfar_ref[:, width:] = dkv_ref[rows:, width:].astype(bf16)


def attend_back(proj, far, bias, attended, grad, lse, heads):
    rows = proj.shape[0]
    width = heads * HD
    return pl.pallas_call(
        functools.partial(attend_back_kernel, heads),
        in_specs=[VMEM] * 6,
        out_specs=(VMEM, VMEM, VMEM),
        out_shape=(
            jax.ShapeDtypeStruct((rows, width), bf16),
            jax.ShapeDtypeStruct((rows, 2 * width), f32),
            jax.ShapeDtypeStruct((rows, 2 * width), bf16),
        ),
        scratch_shapes=[
            pltpu.VMEM((2 * rows, width), bf16),
            pltpu.VMEM((2 * rows, width), bf16),
            pltpu.VMEM((width, 2 * rows), bf16),
            pltpu.VMEM((width, rows), f32),
            pltpu.VMEM((16, rows), f32),
            pltpu.VMEM((2 * rows, 2 * width), f32),
        ],
        compiler_params=params(),
        cost_estimate=pl.CostEstimate(
            flops=10 * heads * rows * 2 * rows * 256, bytes_accessed=16 << 20, transcendentals=0
        ),
    )(proj, far, bias, attended, grad, lse)


def residual_kernel(x_ref, own_ref, oth_ref, wa_ref, wb_ref, vec_ref, r_ref, n_ref):
    mixed = dot(own_ref[...], wa_ref[...], NT) + dot(oth_ref[...], wb_ref[...], NT)
    residual = x_ref[...].astype(f32) + (mixed + vec_ref[0:1, :])
    r_ref[...] = residual
    hat, _ = normalize(residual)
    n_ref[...] = (hat * vec_ref[1:2, :] + vec_ref[2:3, :]).astype(bf16)


def residual_step(x_all, own, oth, weights, width, vectors):
    rows, model = x_all.shape
    block = 128
    return pl.pallas_call(
        residual_kernel,
        grid=(rows // block,),
        in_specs=[
            pl.BlockSpec((block, model), lambda i: (i, 0)),
            pl.BlockSpec((block, width), lambda i: (i, 0)),
            pl.BlockSpec((block, width), lambda i: ((i + rows // block // 2) % (rows // block), 0)),
            pl.BlockSpec((model, width), lambda i: (0, 0)),
            pl.BlockSpec((model, width), lambda i: (0, 1)),
            pl.BlockSpec(vectors.shape, lambda i: (0, 0)),
        ],
        out_specs=(
            pl.BlockSpec((block, model), lambda i: (i, 0)),
            pl.BlockSpec((block, model), lambda i: (i, 0)),
        ),
        out_shape=(
            jax.ShapeDtypeStruct((rows, model), f32),
            jax.ShapeDtypeStruct((rows, model), bf16),
        ),
        compiler_params=params(),
        cost_estimate=pl.CostEstimate(
            flops=4 * rows * model * width, bytes_accessed=12 << 20, transcendentals=0
        ),
    )(x_all, own, oth, weights, weights, vectors)


def hidden_kernel(blocks, n_ref, g_ref, we_ref, wc_ref, b_ref, act_ref, pre_ref, sum_ref, own_ref, oth_ref, acc_ref):
    k = pl.program_id(0)
    rows = n_ref.shape[0]
    half = rows // 2
    piece = 256

    @pl.when(k == 0)
    def _():
        acc_ref[...] = jnp.zeros_like(acc_ref)

    total = jnp.zeros((1, b_ref.shape[1]), f32)
    for i in range(rows // piece):
        at = slice(i * piece, (i + 1) * piece)
        pre = dot(n_ref[at], we_ref[...]) + b_ref[...]
        back = dot(g_ref[at], wc_ref[...])
        cdf = 0.5 + 0.5 * lax.erf(pre * (0.5**0.5))
        density = jnp.exp(pre * pre * -0.5) * 0.3989422804014327
        act_ref[at] = (pre * cdf).astype(bf16)
        low = (back * (cdf + pre * density)).astype(bf16)
        pre_ref[at] = low
        total = total + jnp.sum(low.astype(f32), axis=0, keepdims=True)
        acc_ref[at] += dot(low, we_ref[...], NT)
    sum_ref[...] = total

    @pl.when(k == blocks - 1)
    def _():
        own_ref[...] = acc_ref[:half]
        oth_ref[...] = acc_ref[half:].astype(bf16)


def hidden_step(normed, grad, weights, expand_at, contract_at, width, bias):
    rows, model = normed.shape
    block = 256
    blocks = width // block
    half = rows // 2
    fixed = lambda k: (0, 0)
    return pl.pallas_call(
        functools.partial(hidden_kernel, blocks),
        grid=(blocks,),
        in_specs=[
            pl.BlockSpec((rows, model), fixed),
            pl.BlockSpec((rows, model), fixed),
            pl.BlockSpec((model, block), lambda k: (0, expand_at // block + k)),
            pl.BlockSpec((model, block), lambda k: (0, contract_at // block + k)),
            pl.BlockSpec((1, block), lambda k: (0, k)),
        ],
        out_specs=(
            pl.BlockSpec((rows, block), lambda k: (0, k)),
            pl.BlockSpec((rows, block), lambda k: (0, k)),
            pl.BlockSpec((1, block), lambda k: (0, k)),
            pl.BlockSpec((half, model), fixed),
            pl.BlockSpec((half, model), fixed),
        ),
        out_shape=(
            jax.ShapeDtypeStruct((rows, width), bf16),
            jax.ShapeDtypeStruct((rows, width), bf16),
            jax.ShapeDtypeStruct((1, width), f32),
            jax.ShapeDtypeStruct((half, model), f32),
            jax.ShapeDtypeStruct((half, model), bf16),
        ),
        scratch_shapes=[pltpu.VMEM((rows, model), f32)],
        compiler_params=params(),
        cost_estimate=pl.CostEstimate(
            flops=6 * rows * model * width, bytes_accessed=28 << 20, transcendentals=0
        ),
    )(normed, grad, weights, weights, bias)


def norm_back_kernel(round_low, own_ref, oth_ref, base_ref, add_ref, gain_ref, *outs):
    i = pl.program_id(0)
    grad = own_ref[...].astype(f32) + oth_ref[...].astype(f32)
    hat, inverse = normalize(base_ref[...].astype(f32))
    scaled = grad * gain_ref[...]
    first = jnp.mean(scaled, axis=-1, keepdims=True)
    second = jnp.mean(scaled * hat, axis=-1, keepdims=True)
    result = add_ref[...].astype(f32) + inverse * (scaled - first - hat * second)
    outs[0][...] = result
    sums = outs[-1]

    @pl.when(i == 0)
    def _():
        sums[...] = jnp.zeros_like(sums)

    sums[0:1] += jnp.sum(grad * hat, axis=0, keepdims=True)
    sums[1:2] += jnp.sum(grad, axis=0, keepdims=True)
    if round_low:
        low = result.astype(bf16)
        outs[1][...] = low
        sums[2:3] += jnp.sum(low.astype(f32), axis=0, keepdims=True)


def norm_back(own, oth, base, add, gain, round_low):
    rows, model = own.shape
    block = 128
    spec = pl.BlockSpec((block, model), lambda i: (i, 0))
    outs = [jax.ShapeDtypeStruct((rows, model), f32)]
    if round_low:
        outs.append(jax.ShapeDtypeStruct((rows, model), bf16))
    outs.append(jax.ShapeDtypeStruct((8, model), f32))
    return pl.pallas_call(
        functools.partial(norm_back_kernel, round_low),
        grid=(rows // block,),
        in_specs=[spec] * 4 + [pl.BlockSpec((1, model), lambda i: (0, 0))],
        out_specs=tuple([spec] * (len(outs) - 1) + [pl.BlockSpec((8, model), lambda i: (0, 0))]),
        out_shape=tuple(outs),
        compiler_params=params(),
    )(own, oth, base, add, gain)


def forward_kernel(
    x_in, g_in, s_in, wa, wo, we, wc, bias_ref,
    inner_out, outer_out, n1_out, proj_out, far_out, att_out, lse_ref, res_out, n2_out, g_out,
    act_out, pre_out, esum_ref, dn_own, dn_oth, ho_own, ho_oth, vec_ref,
    so, ina, oa, ob, la, xb, gb, n1, proj, far, tb, eb, acc, stat, att, atto, res, n2, stage, dn, ho,
    ld, ss, sr, zs, zr, xs, xr, cs, cr, ys, yr, fs, fr, outs,
):
    f = lax.axis_index("fsdp")
    c = lax.axis_index("ctx")
    y = lax.axis_index("tp")
    z, x = f // 2, f % 2
    rows, model = xb.shape
    slot = rows // 2
    width = wo.shape[2]
    hidden = we.shape[2]
    each = wa.shape[1] * 2
    blocks = la.shape[0] // 2
    block = la.shape[-1]
    a_count, a_width = ina.shape[0], ina.shape[-1]
    heads = width // HD
    sibling = (f, 1 - c, y)
    across = (z * 2 + (1 - x), c, y)
    partner = (f, c, 1 - y)
    column = [(((z + d) % 4) * 2 + x, c, y) for d in (1, 2, 3)]
    others = [((f + d) % 8, c, y) for d in range(1, 8)]

    def remote(src, dst, s, r, dev):
        copy = pltpu.make_async_remote_copy(
            src_ref=src, dst_ref=dst, send_sem=s, recv_sem=r, device_id=dev, device_id_type=MESH
        )
        copy.start()
        return copy

    def local(src, dst, s):
        copy = pltpu.make_async_copy(src, dst, s)
        copy.start()
        return copy

    def taken(ref, sem):
        pltpu.make_async_copy(ref, ref, sem).wait()

    order = list(range(1, a_count)) + [0]
    own_x = local(x_in, xb.at[pl.ds(0, slot)], ld.at[0])
    own_s = local(s_in, so.at[f], ld.at[1])
    own_g = local(g_in, gb.at[pl.ds(0, slot)], ld.at[2])
    own_o = local(wo.at[c], oa.at[z, x, c], ld.at[3])
    own_a = [
        local(wa.at[c, :, pl.ds(k * a_width, a_width)], ina.at[k, z, x, c], ld.at[4 + k])
        for k in order
    ]
    own_l = [
        local(
            (we if j % 2 == 0 else wc).at[c, :, pl.ds(j // 2 * block, block)],
            la.at[j, z, x, c],
            ld.at[4 + a_count + j],
        )
        for j in range(2 * blocks)
    ]
    bar = pltpu.get_barrier_semaphore()
    for p in others + [sibling, partner]:
        pl.semaphore_signal(bar, 1, device_id=p, device_id_type=MESH)
    pl.semaphore_wait(bar, 9)

    def over_z(q, buf):
        piece = buf.at[z, x, c]
        return [remote(piece, piece, zs.at[q, d], zr.at[q], column[d]) for d in range(3)]

    def over_x(q, buf):
        taken(buf.at[pl.ds(0, 3), 0, 0], zr.at[q])
        remote(buf.at[:, x, c], buf.at[:, x, c], xs.at[q], xr.at[q], across)

    def over_c(q, buf):
        taken(buf.at[:, 0, 0], xr.at[q])
        remote(buf.at[:, :, c], buf.at[:, :, c], cs.at[q], cr.at[q], sibling)

    def ready(q, buf):
        taken(buf.at[:, :, 0], cr.at[q])

    sent = []
    own_s.wait()
    sent += [remote(so.at[f], so.at[f], ss.at[d], sr.at[d], others[d]) for d in range(7)]
    own_x.wait()
    sent.append(
        remote(xb.at[pl.ds(0, slot)], xb.at[pl.ds(slot, slot)], ys.at[0], yr.at[0], partner)
    )
    a_at = {}
    for q, k in enumerate(order):
        own_a[q].wait()
        sent += over_z(q, ina.at[k])
        a_at[q] = ina.at[k]
    o_q = a_count
    l_q = a_count + 1
    own_o.wait()
    sent += over_z(o_q, oa)
    for j in range(2 * blocks):
        own_l[j].wait()
        sent += over_z(l_q + j, la.at[j])
    own_g.wait()
    sent.append(
        remote(gb.at[pl.ds(0, slot)], gb.at[pl.ds(slot, slot)], ys.at[1], yr.at[1], partner)
    )

    for d in range(7):
        taken(so.at[(f - d - 1 + 8) % 8], sr.at[d])
    lanes = so.shape[2]
    step_row = lax.broadcasted_iota(jnp.int32, (lanes, model), 0)
    step_col = lax.broadcasted_iota(jnp.int32, (lanes, model), 1)
    total = jnp.zeros((so.shape[1], model), f32)
    for i in range(8):
        pick = (step_col == step_row + i * each) & (step_row < each)
        total = total + dot(so[i], jnp.where(pick, 1.0, 0.0).astype(bf16))
    vec_ref[...] = total
    per = hidden // 4
    step_row = lax.broadcasted_iota(jnp.int32, (lanes, per), 0)
    step_col = lax.broadcasted_iota(jnp.int32, (lanes, per), 1)
    for i in range(4):
        total = jnp.zeros((so.shape[1], per), f32)
        which = lax.broadcasted_iota(jnp.int32, (so.shape[1], 1), 0)
        for r in range(per // each):
            pick = (step_col == step_row + r * each) & (step_row < each)
            row = jnp.where(which == 8 + r, so[4 * y + i], jnp.zeros((), bf16))
            total = total + dot(row, jnp.where(pick, 1.0, 0.0).astype(bf16))
        eb[:, i * per : (i + 1) * per] = jnp.sum(total, axis=0, keepdims=True)
    near = pl.ds(pl.multiple_of(y * width, 128), width)
    tb[:, :width] = vec_ref[2:3, near]
    tb[:, width : 2 * width] = jnp.zeros((1, width), f32)
    tb[:, 2 * width :] = vec_ref[3:4, near]

    def first_norm(start):
        def body(i, carry):
            at = pl.ds(pl.multiple_of(start + i * 128, 128), 128)
            hat, _ = normalize(xb[at].astype(f32))
            n1[at] = (hat * vec_ref[0:1] + vec_ref[1:2]).astype(bf16)
            return carry

        lax.fori_loop(0, slot // 128, body, 0)

    first_norm(0)
    over_x(0, a_at[0])
    over_x(1, a_at[1])
    over_c(0, a_at[0])
    over_x(2, a_at[2])
    over_c(1, a_at[1])
    over_x(3, a_at[3])
    over_c(2, a_at[2])
    taken(xb.at[pl.ds(slot, slot)], yr.at[0])
    first_norm(slot)

    def project_chunk(q):
        k = order[q]
        ready(q, a_at[q])
        cols = slice(k * a_width, (k + 1) * a_width)

        def body(i, carry):
            at = pl.ds(pl.multiple_of(i * 256, 256), 256)
            proj[at, cols] = (dot(n1[at], ina[k].reshape(model, a_width)) + tb[:, cols]).astype(bf16)
            return carry

        lax.fori_loop(0, rows // 256, body, 0)
        start, stop = max(k * a_width, width), (k + 1) * a_width
        if start < stop:
            sent.append(
                remote(
                    proj.at[:, pl.ds(start, stop - start)],
                    far.at[:, pl.ds(start - width, stop - start)],
                    fs.at[k],
                    fr.at[k],
                    sibling,
                )
            )

    project_chunk(0)
    project_chunk(1)
    over_x(4, a_at[4])
    over_c(3, a_at[3])
    project_chunk(2)
    project_chunk(3)
    over_c(4, a_at[4])
    over_x(o_q, oa)
    project_chunk(4)
    writes = [local(n1, n1_out, outs.at[0]), local(proj, proj_out, outs.at[1])]
    for k in range(1, a_count):
        start, stop = max(k * a_width, width), (k + 1) * a_width
        taken(far.at[:, pl.ds(start - width, stop - start)], fr.at[k])
    writes.append(local(far, far_out, outs.at[2]))

    stat[...] = jnp.zeros_like(stat)
    score_factor = HD ** (-0.5) * LOG2E
    tall = acc.shape[0]

    def attend_step(i, carry):
        at = pl.ds(pl.multiple_of(i * tall, tall), tall)
        acc[...] = jnp.zeros_like(acc)
        for head in range(heads):
            start, stop, mask = head_window(head)
            query = jnp.where(mask, proj[at, start:stop], jnp.zeros((), bf16))
            a = dot(query, proj[:, width + start : width + stop], NT)
            b = dot(query, far[:, start:stop], NT)
            a = a * score_factor + bias_ref[0:1, :rows]
            b = b * score_factor + bias_ref[0:1, rows:]
            top = jnp.maximum(
                jnp.max(a, axis=-1, keepdims=True), jnp.max(b, axis=-1, keepdims=True)
            )
            a = jnp.exp2(a - top)
            b = jnp.exp2(b - top)
            total = jnp.sum(a, axis=-1, keepdims=True) + jnp.sum(b, axis=-1, keepdims=True)
            mixed = dot(a.astype(bf16), proj[:, 2 * width + start : 2 * width + stop])
            mixed = mixed + dot(b.astype(bf16), far[:, width + start : width + stop])
            mixed = mixed * (1.0 / total)
            acc[:, start:stop] += jnp.where(mask, mixed, 0.0)
            lane = lax.broadcasted_iota(jnp.int32, (1, 128), 1)
            stat[at, :] += jnp.where(lane == head, top + jnp.log2(total), 0.0)
        att[at] = acc[...].astype(bf16)
        remote(att.at[at], atto.at[at], ys.at[3 + i], yr.at[3 + i], partner)
        over_x(l_q + i, la.at[i])

        @pl.when(i == 0)
        def _():
            over_c(o_q, oa)
            remote(oa.at[:, :, c], ob.at[:, :, c], ys.at[2], yr.at[2], partner)

        @pl.when(i > 0)
        def _():
            over_c(l_q + i - 1, la.at[i - 1])

        return carry

    steps = rows // tall
    lax.fori_loop(0, steps, attend_step, 0)
    lse_ref[...] = stat[...].T
    writes.append(local(att, att_out, outs.at[3]))
    over_x(l_q + 3, la.at[3])
    over_c(l_q + 2, la.at[2])
    taken(ob.at[:, :, c], yr.at[2])
    b_q = zs.shape[0] - 1
    remote(ob.at[:, :, c], ob.at[:, :, c], cs.at[b_q], cr.at[b_q], sibling)
    over_x(l_q + 4, la.at[4])
    over_c(l_q + 3, la.at[3])
    over_x(l_q + 5, la.at[5])
    over_c(l_q + 4, la.at[4])
    ready(o_q, oa)
    ready(b_q, ob)
    writes.append(local(oa, outer_out, outs.at[4]))
    for q, k in enumerate(order):
        writes.append(
            local(ina.at[k], inner_out.at[:, :, :, :, pl.ds(k * a_width, a_width)], outs.at[5 + k])
        )
    for i in range(steps):
        at = pl.ds(i * tall, tall)
        taken(atto.at[at], yr.at[3 + i])

    def residual_half(i):
        at = slice(i * slot, (i + 1) * slot)
        back = slice((1 - i) * slot, (2 - i) * slot)
        mixed = dot(att[at], oa[...].reshape(model, width), NT)
        res[at] = mixed + dot(atto[back], ob[...].reshape(model, width), NT)

        def body(j, carry):
            row = pl.ds(pl.multiple_of(i * slot + j * 128, 128), 128)
            value = xb[row].astype(f32) + (res[row] + vec_ref[4:5])
            res[row] = value
            hat, _ = normalize(value)
            n2[row] = (hat * vec_ref[5:6] + vec_ref[6:7]).astype(bf16)
            return carry

        lax.fori_loop(0, slot // 128, body, 0)

    residual_half(0)
    over_x(l_q + 6, la.at[6])
    over_c(l_q + 5, la.at[5])
    residual_half(1)
    late_writes = [
        local(res.at[pl.ds(0, slot)], res_out, outs.at[5 + a_count]),
        local(n2, n2_out, outs.at[6 + a_count]),
    ]
    taken(gb.at[pl.ds(slot, slot)], yr.at[1])
    late_writes.append(local(gb, g_out, outs.at[7 + a_count]))
    dn[...] = jnp.zeros_like(dn)
    ho[...] = jnp.zeros_like(ho)
    s_at = 8 + a_count

    def hidden_step_in(b, carry):
        ready(l_q + 2 * b, la.at[2 * b])
        ready(l_q + 2 * b + 1, la.at[2 * b + 1])
        turn = b % 2
        cols = pl.ds(pl.multiple_of(b * block, block), block)

        @pl.when(b > 1)
        def _():
            taken(stage.at[0, turn], outs.at[s_at + turn])
            taken(stage.at[1, turn], outs.at[s_at + 2 + turn])

        shift = eb[:, cols]
        total = jnp.zeros((1, block), f32)
        for i in range(rows // 256):
            at = slice(i * 256, (i + 1) * 256)
            pre = dot(n2[at], la[2 * b].reshape(model, block)) + shift
            back = dot(gb[at], la[2 * b + 1].reshape(model, block))
            cdf = 0.5 + 0.5 * lax.erf(pre * (0.5**0.5))
            density = jnp.exp(pre * pre * -0.5) * 0.3989422804014327
            low = (back * (cdf + pre * density)).astype(bf16)
            active = (pre * cdf).astype(bf16)
            stage[0, turn, at] = active
            stage[1, turn, at] = low
            total = total + jnp.sum(low.astype(f32), axis=0, keepdims=True)
            dn[at] += dot(low, la[2 * b].reshape(model, block), NT)
            ho[at] += dot(active, la[2 * b + 1].reshape(model, block), NT)
        esum_ref[:, cols] = total
        local(stage.at[0, turn], act_out.at[:, cols], outs.at[s_at + turn])
        local(stage.at[1, turn], pre_out.at[:, cols], outs.at[s_at + 2 + turn])

        @pl.when(b < 3)
        def _():
            over_x(l_q + 7 + b, la.at[7 + b])

        @pl.when(b < 4)
        def _():
            over_c(l_q + 6 + b, la.at[6 + b])

        return carry

    lax.fori_loop(0, blocks, hidden_step_in, 0)
    for copy in writes:
        copy.wait()
    n1[:slot] = dn[slot:].astype(bf16)
    n1[slot:] = ho[slot:].astype(bf16)
    last = [
        local(dn.at[pl.ds(0, slot)], dn_own, ld.at[0]),
        local(ho.at[pl.ds(0, slot)], ho_own, ld.at[1]),
        local(n1.at[pl.ds(0, slot)], dn_oth, ld.at[2]),
        local(n1.at[pl.ds(slot, slot)], ho_oth, ld.at[3]),
    ]
    for turn in range(2):
        taken(stage.at[0, turn], outs.at[s_at + turn])
        taken(stage.at[1, turn], outs.at[s_at + 2 + turn])
    for copy in late_writes + last:
        copy.wait()
    for copy in sent:
        copy.wait_send()
    for q in range(zs.shape[0]):
        if q < a_count:
            buf = a_at[q]
        elif q == o_q:
            buf = oa
        elif q == b_q:
            buf = ob
        else:
            buf = la.at[q - l_q]
        taken(buf.at[:, :, 0], cs.at[q])
        if q != b_q:
            taken(buf.at[:, 0, 0], xs.at[q])
    taken(oa.at[:, :, 0], ys.at[2])
    for i in range(steps):
        taken(att.at[pl.ds(i * tall, tall)], ys.at[3 + i])


def forward(x_own, g_own, smalls, wa, wo, we, wc, bias):
    slot, model = x_own.shape
    rows = 2 * slot
    each = wa.shape[0]
    width, hidden = wo.shape[1], we.shape[1]
    half = each // 2
    a_width, block = 384, 512
    a_count, blocks = 3 * width // a_width, hidden // block
    grid = (4, 2, 2, half)
    chunks = a_count + 2 + 2 * blocks
    sem = pltpu.SemaphoreType.DMA
    out = jax.ShapeDtypeStruct

    def halves(w):
        return w.reshape(2, half, w.shape[1])

    return pl.pallas_call(
        forward_kernel,
        in_specs=[HBM] * 7 + [VMEM],
        out_specs=(HBM,) * 6 + (VMEM,) + (HBM,) * 5 + (VMEM,) + (HBM,) * 4 + (VMEM,),
        out_shape=(
            out(grid + (3 * width,), bf16),
            out(grid + (width,), bf16),
            out((rows, model), bf16),
            out((rows, 3 * width), bf16),
            out((rows, 2 * width), bf16),
            out((rows, width), bf16),
            out((128, rows), f32),
            out((slot, model), f32),
            out((rows, model), bf16),
            out((rows, model), bf16),
            out((rows, hidden), bf16),
            out((rows, hidden), bf16),
            out((1, hidden), f32),
            out((slot, model), f32),
            out((slot, model), bf16),
            out((slot, model), f32),
            out((slot, model), bf16),
            out((16, model), f32),
        ),
        scratch_shapes=[
            pltpu.VMEM((8,) + smalls.shape, bf16),
            pltpu.VMEM((a_count,) + grid + (a_width,), bf16),
            pltpu.VMEM(grid + (width,), bf16),
            pltpu.VMEM(grid + (width,), bf16),
            pltpu.VMEM((2 * blocks,) + grid + (block,), bf16),
            pltpu.VMEM((rows, model), bf16),
            pltpu.VMEM((rows, model), bf16),
            pltpu.VMEM((rows, model), bf16),
            pltpu.VMEM((rows, 3 * width), bf16),
            pltpu.VMEM((rows, 2 * width), bf16),
            pltpu.VMEM((1, 3 * width), f32),
            pltpu.VMEM((1, hidden), f32),
            pltpu.VMEM((256, width), f32),
            pltpu.VMEM((rows, 128), f32),
            pltpu.VMEM((rows, width), bf16),
            pltpu.VMEM((rows, width), bf16),
            pltpu.VMEM((rows, model), f32),
            pltpu.VMEM((rows, model), bf16),
            pltpu.VMEM((2, 2, rows, block), bf16),
            pltpu.VMEM((rows, model), f32),
            pltpu.VMEM((rows, model), f32),
            sem((4 + a_count + 2 * blocks,)),
            sem((7,)),
            sem((7,)),
            sem((chunks, 3)),
            sem((chunks,)),
            sem((chunks,)),
            sem((chunks,)),
            sem((chunks,)),
            sem((chunks,)),
            sem((3 + rows // 256,)),
            sem((3 + rows // 256,)),
            sem((a_count,)),
            sem((a_count,)),
            sem((12 + a_count,)),
        ],
        compiler_params=params(collective_id=1, has_side_effects=True),
    )(x_own, g_own, smalls, halves(wa), halves(wo), halves(we), halves(wc), bias)


def backward_kernel(
    act_in, pre_in, n2_in, g_in, dn_in, dno_in, res_in, proj_in, far_in, att_in, n1_in, inner_in, outer_in, x_in,
    lse_ref, bias_ref, vec_ref,
    hg_out, gm_ref, go_ref, ga_ref, sums_ref, psum_ref,
    u, att, dqt, keyt, dots, acc, drecv, oa, b1, b2, t1, t2, res, dn, dnr, stream, gproj, xb, own, near, far, last,
    ld, cs, cr, xs, xr, zs, zr, ys, yr, fs, fr, free,
):
    f = lax.axis_index("fsdp")
    c = lax.axis_index("ctx")
    y = lax.axis_index("tp")
    z, x = f // 2, f % 2
    rows, model = b1.shape
    slot = rows // 2
    width = att.shape[1]
    heads = width // HD
    ring = own.shape[0]
    block = acc.shape[0]
    tile = 128
    sibling = (f, 1 - c, y)
    across = (z * 2 + (1 - x), c, y)
    partner = (f, c, 1 - y)
    column = [(((z + d) % 4) * 2 + x, c, y) for d in (1, 2, 3)]

    def remote(src, dst, s, r, dev):
        pltpu.make_async_remote_copy(
            src_ref=src, dst_ref=dst, send_sem=s, recv_sem=r, device_id=dev, device_id_type=MESH
        ).start()

    def local(src, dst, s):
        copy = pltpu.make_async_copy(src, dst, s)
        copy.start()
        return copy

    def taken(ref, sem):
        pltpu.make_async_copy(ref, ref, sem).wait()

    def columns(k):
        return pl.ds(pl.multiple_of(k * width, tile), width)

    own_n2 = local(n2_in, b1, ld.at[0])
    own_g = local(g_in, b2, ld.at[1])
    for k in range(2):
        local(pre_in.at[:, columns(k)], stream.at[k], ld.at[2 + k])
    own_res = local(res_in, res, ld.at[4])
    own_dn = local(dn_in, dn, ld.at[5])
    own_oa = local(outer_in, oa, ld.at[6])
    own_att = local(att_in, att, ld.at[7])
    own_proj = local(proj_in, u.at[pl.ds(0, rows)], ld.at[8])
    own_far = local(far_in, u.at[pl.ds(rows, rows), pl.ds(width, 2 * width)], ld.at[9])
    own_x = local(x_in, xb, ld.at[10])
    bar = pltpu.get_barrier_semaphore()
    for p in [sibling, across, partner] + column:
        pl.semaphore_signal(bar, 1, device_id=p, device_id_type=MESH)
    pl.semaphore_wait(bar, 6)
    remote(dno_in, dnr, ys.at[0], yr.at[0], partner)

    def turned(dst, src, start, count):
        def body(i, carry):
            at = pl.ds(pl.multiple_of(start + i * tile, tile), tile)
            dst[:, at] = src[at].T
            return carry

        lax.fori_loop(0, count // tile, body, 0)

    def produce(k, left, right):
        def body(i, carry):
            at = pl.ds(pl.multiple_of(i * (model // 2), tile), model // 2)
            part = dot(left[at], right).astype(bf16)
            own[k % ring, pl.ds(2 * i, 2)] = part.reshape((2,) + own.shape[2:])
            return carry

        lax.fori_loop(0, 2, body, 0)
        remote(own.at[k % ring, :, :, 1 - c], near.at[k], cs.at[k], cr.at[k], sibling)

    def first(k):
        taken(near.at[k], cr.at[k])

        def body(i, carry):
            for j in range(2):
                near[k, i, j] = near[k, i, j] + own[k % ring, i, j, c]
            return carry

        lax.fori_loop(0, 4, body, 0)
        remote(near.at[k, :, 1 - x], far.at[k], xs.at[k], xr.at[k], across)

    def second(k):
        taken(far.at[k], xr.at[k])

        def body(i, carry):
            near[k, i, x] = near[k, i, x] + far[k, i]
            return carry

        lax.fori_loop(0, 4, body, 0)
        for d in range(3):
            remote(near.at[k, (z + d + 1) % 4, x], last.at[k, d], zs.at[k], zr.at[k], column[d])

    def third(k, ref, j):
        taken(last.at[k], zr.at[k])
        total = near[k, z, x].astype(f32)
        for d in range(3):
            total = total + last[k, d].astype(f32)
        ref[:, columns(j)] = total

    own_n2.wait()
    turned(t1, b1, 0, rows)
    pl.semaphore_signal(free, 1, device_id=partner, device_id_type=MESH)
    per = pre_in.shape[1] // width

    def expand_chunk(k, carry):
        taken(stream.at[k % 2], ld.at[2 + k % 2])

        @pl.when(k >= ring)
        def _():
            taken(near.at[k - ring], cs.at[k - ring])

        produce(k, t1, stream[k % 2])

        @pl.when(k + 2 < per)
        def _():
            local(pre_in.at[:, columns(k + 2)], stream.at[k % 2], ld.at[2 + k % 2])

        @pl.when(k + 2 >= per)
        def _():
            local(act_in.at[:, columns(k + 2 - per)], stream.at[k % 2], ld.at[2 + k % 2])

        @pl.when(k > 0)
        def _():
            first(k - 1)

        return carry

    lax.fori_loop(0, per, expand_chunk, 0)
    own_g.wait()
    turned(t2, b2, 0, rows)

    def contract_chunk(k, carry):
        taken(stream.at[k % 2], ld.at[2 + k % 2])
        taken(near.at[k - ring], cs.at[k - ring])
        produce(k, t2, stream[k % 2])

        @pl.when(k + 2 < 2 * per)
        def _():
            local(act_in.at[:, columns(k + 2 - per)], stream.at[k % 2], ld.at[2 + k % 2])

        first(k - 1)
        return carry

    lax.fori_loop(per, 2 * per, contract_chunk, 0)
    o_at = 2 * per
    first(o_at - 1)
    second(0)

    own_res.wait()
    own_dn.wait()
    taken(dnr, yr.at[0])
    pl.semaphore_wait(free, 1)
    sums_ref[...] = jnp.zeros_like(sums_ref)

    def second_norm(i, carry):
        at = pl.ds(pl.multiple_of(i * tile, tile), tile)
        grad = dn[at] + dnr[at].astype(f32)
        hat, inverse = normalize(res[at])
        scaled = grad * vec_ref[5:6]
        mean = jnp.mean(scaled, axis=-1, keepdims=True)
        slope = jnp.mean(scaled * hat, axis=-1, keepdims=True)
        out_grad = b2[at].astype(f32)
        result = out_grad + inverse * (scaled - mean - hat * slope)
        low = result.astype(bf16)
        dn[at] = result
        b1[at] = low
        sums_ref[0:1] += jnp.sum(grad * hat, axis=0, keepdims=True)
        sums_ref[1:2] += jnp.sum(grad, axis=0, keepdims=True)
        sums_ref[2:3] += jnp.sum(low.astype(f32), axis=0, keepdims=True)
        sums_ref[3:4] += jnp.sum(out_grad, axis=0, keepdims=True)
        there = pl.ds(pl.multiple_of(slot + i * tile, tile), tile)
        remote(b1.at[at], b1.at[there], ys.at[1 + i], yr.at[1 + i], partner)
        return carry

    pieces = slot // tile
    lax.fori_loop(0, pieces, second_norm, 0)
    own_n1 = local(n1_in, b2, ld.at[1])
    second(1)
    own_oa.wait()
    own_proj.wait()
    own_far.wait()
    own_att.wait()

    def attended_grad(half):
        at = slice(half * slot, (half + 1) * slot)
        turned(t2, b1, half * slot, slot)
        u[rows + half * slot : rows + (half + 1) * slot, :width] = dot(b1[at], oa[...]).astype(bf16)

    attended_grad(0)
    own_n1.wait()
    turned(t1, b2, 0, rows)
    second(2)
    third(0, gm_ref, 0)
    second(3)
    third(1, gm_ref, 1)
    for i in range(pieces):
        taken(b1.at[pl.ds(slot + i * tile, tile)], yr.at[1 + i])
    attended_grad(1)
    taken(near.at[o_at - ring], cs.at[o_at - ring])
    produce(o_at, t2, att[...])
    dots[...] = jnp.zeros_like(dots)

    def head_sums(i, carry):
        at = pl.ds(pl.multiple_of(i * block, block), block)
        there = pl.ds(pl.multiple_of(rows + i * block, block), block)
        product = u[there, :width].astype(f32) * att[at].astype(f32)
        high = product.astype(bf16)
        low = (product - high.astype(f32)).astype(bf16)
        lane = lax.broadcasted_iota(jnp.int32, (16, width), 1)
        row = lax.broadcasted_iota(jnp.int32, (16, width), 0)
        pick = jnp.where((lane >= row * HD) & (lane < row * HD + HD), 1.0, 0.0).astype(bf16)
        dots[:, at] = dot(pick, high, NT) + dot(pick, low, NT)
        return carry

    lax.fori_loop(0, rows // block, head_sums, 0)
    first(o_at)
    second(4)
    third(2, gm_ref, 2)

    dqt[...] = jnp.zeros_like(dqt)
    score_factor = HD ** (-0.5) * LOG2E
    scale = HD ** (-0.5)
    near_blocks = rows // block

    def attend_step(i, carry):
        b = (i + near_blocks) % (2 * near_blocks)
        at = pl.ds(pl.multiple_of(b * block, block), block)
        acc[...] = jnp.zeros_like(acc)
        keyt[...] = u[at, width : 2 * width].T
        bias = bias_ref[at, 0:1]
        for head in range(heads):
            start, stop, mask = head_window(head)
            zero = jnp.zeros((), bf16)
            query = jnp.where(mask, u[:rows, start:stop], zero)
            grad = jnp.where(mask, u[rows:, start:stop], zero)
            scores = dot(u[at, width + start : width + stop], query, NT) * score_factor + bias
            probs = jnp.exp2(scores - lse_ref[head : head + 1, :])
            grad_probs = dot(u[at, 2 * width + start : 2 * width + stop], grad, NT)
            grad_scores = (probs * (grad_probs - dots[head : head + 1, :])).astype(bf16)
            acc[:, start:stop] += dot(grad_scores, query)
            acc[:, width + start : width + stop] += dot(probs.astype(bf16), grad)
            dqt[head * HD : head * HD + HD, :] += dot(keyt[head * HD : head * HD + HD, :], grad_scores)

        @pl.when(i < near_blocks)
        def _():
            piece = pl.ds(pl.multiple_of(i * block, block), block)
            stream[0, piece] = (acc[:, :width] * scale).astype(bf16)
            stream[1, piece] = acc[:, width:].astype(bf16)
            remote(stream.at[:, piece], drecv.at[:, piece], fs.at[i], fr.at[i], sibling)

        @pl.when(i >= near_blocks)
        def _():
            piece = pl.ds(pl.multiple_of((i - near_blocks) * block, block), block)
            taken(drecv.at[:, piece], fr.at[i - near_blocks])
            key = acc[:, :width] * scale + drecv[0, piece].astype(f32)
            gproj[piece, width : 2 * width] = key.astype(bf16)
            value = acc[:, width:] + drecv[1, piece].astype(f32)
            gproj[piece, 2 * width :] = value.astype(bf16)

        @pl.when(i == 1)
        def _():
            second(5)
            third(3, gm_ref, 3)

        @pl.when(i == 2)
        def _():
            second(6)

        @pl.when(i == 3)
        def _():
            third(4, gm_ref, 4)

        @pl.when(i == 4)
        def _():
            second(7)
            third(5, gm_ref, 5)

        return carry

    lax.fori_loop(0, 2 * near_blocks, attend_step, 0)
    own_inner = local(inner_in, u.at[pl.ds(0, model)], ld.at[8])
    gproj[:, :width] = (dqt[...].T * scale).astype(bf16)

    def project_chunk(j):
        k = o_at + 1 + j
        taken(near.at[k - ring], cs.at[k - ring])
        produce(k, t1, gproj[:, j * width : (j + 1) * width])

    project_chunk(0)
    project_chunk(1)
    first(o_at + 1)
    project_chunk(2)
    first(o_at + 2)
    second(8)
    third(6, gm_ref, 6)
    own_inner.wait()
    for i in range(pieces):
        taken(b1.at[pl.ds(i * tile, tile)], ys.at[1 + i])
    split = model // 2
    for n in range(2):
        at = slice(n * split, (n + 1) * split)
        b1[:slot, at] = dot(gproj[slot:], u[at], NT).astype(bf16)
    remote(b1.at[pl.ds(0, slot)], dnr, ys.at[1 + pieces], yr.at[1 + pieces], partner)
    first(o_at + 3)
    for n in range(2):
        at = slice(n * split, (n + 1) * split)
        res[:, at] = dot(gproj[:slot], u[at], NT)
    psum_ref[...] = dot(jnp.ones((8, rows), bf16), gproj[...])
    second(9)
    third(7, gm_ref, 7)
    third(8, go_ref, 0)
    own_x.wait()
    taken(dnr, yr.at[1 + pieces])

    def first_norm(i, carry):
        at = pl.ds(pl.multiple_of(i * tile, tile), tile)
        grad = res[at] + dnr[at].astype(f32)
        hat, inverse = normalize(xb[at].astype(f32))
        scaled = grad * vec_ref[0:1]
        mean = jnp.mean(scaled, axis=-1, keepdims=True)
        slope = jnp.mean(scaled * hat, axis=-1, keepdims=True)
        dn[at] = dn[at] + inverse * (scaled - mean - hat * slope)
        sums_ref[4:5] += jnp.sum(grad * hat, axis=0, keepdims=True)
        sums_ref[5:6] += jnp.sum(grad, axis=0, keepdims=True)
        return carry

    lax.fori_loop(0, pieces, first_norm, 0)
    write = local(dn, hg_out, ld.at[5])
    second(10)
    third(9, ga_ref, 0)
    second(11)
    third(10, ga_ref, 1)
    third(11, ga_ref, 2)
    write.wait()
    taken(dnr, ys.at[0])
    taken(dnr, ys.at[1 + pieces])
    for i in range(near_blocks):
        piece = pl.ds(i * block, block)
        taken(stream.at[:, piece], fs.at[i])
    count = near.shape[0]
    for k in range(count):
        if k + ring >= count:
            taken(near.at[k], cs.at[k])
        taken(far.at[k], xs.at[k])
        taken(last.at[k], zs.at[k])


def backward(act, pre, n2, g, dn, dno, res, proj, far, att, n1, inner, outer, x_own, lse, bias, vectors):
    rows, model = n2.shape
    slot = rows // 2
    width = att.shape[1]
    hidden = act.shape[1]
    owned = model // 16
    block = 256
    chunks = 2 * hidden // width + 4
    ring = 3
    sem = pltpu.SemaphoreType.DMA
    out = jax.ShapeDtypeStruct
    return pl.pallas_call(
        backward_kernel,
        in_specs=[HBM] * 14 + [VMEM] * 3,
        out_specs=(HBM,) + (VMEM,) * 5,
        out_shape=(
            out((slot, model), f32),
            out((owned, 2 * hidden), f32),
            out((owned, width), f32),
            out((owned, 3 * width), f32),
            out((8, model), f32),
            out((8, 3 * width), f32),
        ),
        scratch_shapes=[
            pltpu.VMEM((2 * rows, 3 * width), bf16),
            pltpu.VMEM((rows, width), bf16),
            pltpu.VMEM((width, rows), f32),
            pltpu.VMEM((width, block), bf16),
            pltpu.VMEM((16, rows), f32),
            pltpu.VMEM((block, 2 * width), f32),
            pltpu.VMEM((2, rows, width), bf16),
            pltpu.VMEM((model, width), bf16),
            pltpu.VMEM((rows, model), bf16),
            pltpu.VMEM((rows, model), bf16),
            pltpu.VMEM((model, rows), bf16),
            pltpu.VMEM((model, rows), bf16),
            pltpu.VMEM((slot, model), f32),
            pltpu.VMEM((slot, model), f32),
            pltpu.VMEM((slot, model), bf16),
            pltpu.VMEM((2, rows, width), bf16),
            pltpu.VMEM((rows, 3 * width), bf16),
            pltpu.VMEM((slot, model), bf16),
            pltpu.VMEM((ring, 4, 2, 2, owned, width), bf16),
            pltpu.VMEM((chunks, 4, 2, owned, width), bf16),
            pltpu.VMEM((chunks, 4, owned, width), bf16),
            pltpu.VMEM((chunks, 3, owned, width), bf16),
            sem((11,)),
            sem((chunks,)),
            sem((chunks,)),
            sem((chunks,)),
            sem((chunks,)),
            sem((chunks,)),
            sem((chunks,)),
            sem((2 + slot // 128,)),
            sem((2 + slot // 128,)),
            sem((rows // block,)),
            sem((rows // block,)),
            pltpu.SemaphoreType.REGULAR,
        ],
        compiler_params=params(collective_id=4, has_side_effects=True),
    )(act, pre, n2, g, dn, dno, res, proj, far, att, n1, inner, outer, x_own, lse, bias, vectors)


def key_biases(share, slot, length, tp_rank, ctx_rank):
    places = lax.iota(jnp.int32, slot)
    pieces = []
    for ctx in (ctx_rank, 1 - ctx_rank):
        for tp in (tp_rank, 1 - tp_rank):
            start = (ctx * 2 + tp) * share
            valid = (places < share) & (start + places < length)
            pieces.append(jnp.where(valid, 0.0, masked_score).astype(f32))
    return jnp.concatenate(pieces)


def forward_parts(x_own, grad_own, smalls, inner, outer_t, expand_weight, contract_t, bias):
    slot, model = x_own.shape
    rows_each = inner.shape[0]
    half_each = rows_each // 2
    width, hidden = outer_t.shape[1], expand_weight.shape[1]
    heads = width // HD
    tp_rank = lax.axis_index("tp")
    ctx_rank = lax.axis_index("ctx")
    x_all = jnp.concatenate([x_own, swap(x_own, "tp")], axis=0)
    grad_all = jnp.concatenate([grad_own, swap(grad_own, "tp")], axis=0)
    inner = lax.all_gather(inner, "fsdp", axis=0, tiled=True)
    smalls_all = lax.all_gather(smalls, "fsdp", axis=0)
    late = jnp.concatenate([outer_t, swap(outer_t, "tp"), expand_weight, contract_t], axis=1)
    late = lax.dynamic_slice_in_dim(late, ctx_rank * half_each, half_each, 0)
    late = lax.all_gather(late, ("fsdp", "ctx"), axis=0, tiled=True)
    expand_at = 2 * width
    contract_at = 2 * width + hidden
    smalls_all = smalls_all[:, :, :rows_each].astype(f32)
    vectors = jnp.transpose(smalls_all[:, :8], (1, 0, 2)).reshape(8, model)
    expand_rows = smalls_all[:, 8 : 8 + hidden * 2 // model].reshape(1, 2 * hidden)
    expand_local = lax.dynamic_slice_in_dim(expand_rows, tp_rank * hidden, hidden, 1)
    pair = lax.dynamic_slice_in_dim(vectors[2:4], tp_rank * width, width, 1)
    triple = jnp.concatenate([pair[0:1], jnp.zeros((1, width), f32), pair[1:2]], axis=1)
    normed_one, proj = project(x_all, vectors[0:1], vectors[1:2], inner, triple)
    far = swap(proj[:, width:], "ctx")
    attended, lse = attend(proj, far, jnp.broadcast_to(bias[None], (8, bias.shape[0])), heads)
    attended_oth = swap(attended, "tp")
    residual, normed_two = residual_step(x_all, attended, attended_oth, late, width, vectors[4:7])
    activated, pre_grad, expand_sum, normed_own, normed_oth = hidden_step(
        normed_two, grad_all, late, expand_at, contract_at, hidden, expand_local
    )
    contracted = dot(activated, late[:, contract_at:], NT)
    return (
        inner, late[:, :width], normed_one, proj, far, attended, lse, residual[:slot], normed_two,
        grad_all, activated, pre_grad, expand_sum, normed_own, normed_oth, contracted[:slot],
        contracted[slot:].astype(bf16), vectors,
    )


def per_device(
    hidden_in,
    valid_lengths,
    output_grad,
    first_gain,
    first_shift,
    attention_in,
    query_value_bias,
    attention_out,
    attention_bias,
    second_gain,
    second_shift,
    expand_weight,
    expand_bias,
    contract_weight,
    contract_bias,
):
    _, share, model = hidden_in.shape
    tp_rank = lax.axis_index("tp")
    ctx_rank = lax.axis_index("ctx")
    fsdp_count = lax.axis_size("fsdp")
    rows_each = attention_in.shape[0]
    width = attention_in.shape[2]
    heads = width // HD
    hidden = expand_weight.shape[1]
    slot = -(-share // 128) * 128
    length = valid_lengths[0]

    def padded(value):
        return jnp.pad(value, ((0, slot - share), (0, 0)))

    own_start = (ctx_rank * 2 + tp_rank) * share
    token_valid = (own_start + lax.iota(jnp.int32, share)) < length
    grad_own = jnp.where(token_valid[:, None], output_grad[0], jnp.zeros((), bf16))
    grad_own = padded(grad_own)
    x_own = padded(hidden_in[0])

    smalls = jnp.concatenate(
        [
            jnp.stack(
                [
                    first_gain,
                    first_shift,
                    query_value_bias[0],
                    query_value_bias[1],
                    attention_bias,
                    second_gain,
                    second_shift,
                    contract_bias,
                ]
            ),
            expand_bias.reshape(-1, rows_each),
        ],
        axis=0,
    )
    smalls = jnp.pad(smalls, ((0, 16 - smalls.shape[0]), (0, -rows_each % 128)))
    bias = key_biases(share, slot, length, tp_rank, ctx_rank)
    inner = attention_in.reshape(rows_each, 3 * width)
    outer_t, contract_t = attention_out.T, contract_weight.T
    if fsdp_count == 8 and rows_each == 160 and 2 * hidden == 8 * width:
        (
            inner, outer_t, normed_one, proj, far, attended, lse, residual, normed_two, grad_all,
            activated, pre_grad, expand_sum, normed_own, normed_oth, out_own, out_oth, vectors,
        ) = forward(
            x_own, grad_own, smalls, inner, outer_t, expand_weight, contract_t,
            jnp.broadcast_to(bias[None], (8, bias.shape[0])),
        )
        hidden_grad, grad_late, grad_outer_t, grad_inner, sums, sums_proj = backward(
            activated, pre_grad, normed_two, grad_all, normed_own, normed_oth, residual, proj, far,
            attended, normed_one, inner.reshape(model, 3 * width), outer_t.reshape(model, width), x_own, lse,
            jnp.broadcast_to(bias[:, None], (bias.shape[0], 128)), vectors,
        )
        contracted = out_own + swap(out_oth, "tp").astype(f32)
        hidden_out = (residual + (contracted + vectors[7:8])).astype(bf16)
        sums_one, sums_two, proj_sums = sums[4:6], sums[0:3], sums_proj[0]
        grad_sum = sums[3]
    else:
        (
            inner, outer_t, normed_one, proj, far, attended, lse, residual, normed_two, grad_all,
            activated, pre_grad, expand_sum, normed_own, normed_oth, out_own, out_oth, vectors,
        ) = forward_parts(
            x_own, grad_own, smalls, inner, outer_t, expand_weight, contract_t, bias
        )
        normed_oth = swap(normed_oth, "tp")
        grad_contract_t = dot(grad_all, activated, TN).astype(bf16)
        grad_expand = dot(normed_two, pre_grad, TN).astype(bf16)
        normed_own, normed_oth, grad_late = lax.optimization_barrier(
            (normed_own, normed_oth, jnp.concatenate([grad_expand, grad_contract_t], axis=1))
        )
        grad_late = lax.psum_scatter(
            grad_late, ("fsdp", "ctx"), scatter_dimension=0, tiled=True
        ).astype(f32)
        contracted = out_own + swap(out_oth, "tp").astype(f32)
        hidden_out = (residual + (contracted + vectors[7:8])).astype(bf16)

        residual_grad, residual_low, sums_two = norm_back(
            normed_own, normed_oth, residual, grad_own, vectors[5:6], True
        )
        residual_low_all = jnp.concatenate([residual_low, swap(residual_low, "tp")], axis=0)
        attended_grad = dot(residual_low_all, outer_t).astype(bf16)
        grad_outer_t = dot(residual_low_all, attended, TN).astype(bf16)

        grad_query, grad_near, grad_far = attend_back(
            proj, far, jnp.broadcast_to(bias[:, None], (bias.shape[0], 128)), attended, attended_grad, lse, heads
        )
        grad_near = (grad_near + swap(grad_far, "ctx").astype(f32)).astype(bf16)
        grad_proj = jnp.concatenate([grad_query, grad_near], axis=1)
        normed_grad = dot(grad_proj, inner, NT)
        normed_grad_oth = swap(normed_grad[slot:].astype(bf16), "tp")
        grad_inner = dot(normed_one, grad_proj, TN).astype(bf16)
        proj_sums = jnp.sum(grad_proj.astype(f32), axis=0)
        grad_inner, grad_outer_t = scatter_sums([grad_inner, grad_outer_t], 384, fsdp_count)
        hidden_grad, sums_one = norm_back(
            normed_grad[:slot], normed_grad_oth, x_own, residual_grad, vectors[0:1], False
        )
        grad_sum = jnp.sum(grad_own.astype(f32), axis=0)

    def placed(value, total):
        zero = jnp.zeros((total,), f32)
        return lax.dynamic_update_slice_in_dim(zero, value, tp_rank * value.shape[0], 0)

    owned = model // (fsdp_count * 2)
    stacked = jnp.stack(
        [
            sums_one[0],
            sums_one[1],
            placed(proj_sums[:width], model),
            placed(proj_sums[2 * width :], model),
            sums_two[2],
            sums_two[0],
            sums_two[1],
            grad_sum,
        ]
    )
    stacked = jnp.transpose(stacked.reshape(8, -1, owned), (1, 0, 2))
    expand_piece = placed(expand_sum[0], 2 * hidden).reshape(fsdp_count * 2, -1, owned)
    stacked = jnp.concatenate([stacked, expand_piece], axis=1)
    stacked = jnp.pad(stacked, ((0, 0), (0, 16 - stacked.shape[1]), (0, 128 - owned)))
    summed = sum_vectors(stacked, fsdp_count)[:, :owned]

    return (
        hidden_out[None, :share],
        hidden_grad[None, :share],
        summed[0],
        summed[1],
        grad_inner.reshape(-1, 3, width),
        summed[2:4],
        grad_outer_t.T,
        summed[4],
        summed[5],
        summed[6],
        grad_late[:, :hidden],
        summed[8 : 8 + 2 * hidden // model].reshape(-1),
        grad_late[:, hidden:].T,
        summed[7],
    )


def solution(mesh):
    return jax.shard_map(
        per_device,
        mesh=mesh,
        in_specs=(
            P("fsdp", ("ctx", "tp"), None),
            P("fsdp"),
            P("fsdp", ("ctx", "tp"), None),
            P("fsdp"),
            P("fsdp"),
            P("fsdp", None, "tp"),
            P(None, "fsdp"),
            P("tp", "fsdp"),
            P("fsdp"),
            P("fsdp"),
            P("fsdp"),
            P("fsdp", "tp"),
            P("fsdp"),
            P("tp", "fsdp"),
            P("fsdp"),
        ),
        out_specs=(
            P("fsdp", ("ctx", "tp"), None),
            P("fsdp", ("ctx", "tp"), None),
            P(("fsdp", "ctx")),
            P(("fsdp", "ctx")),
            P(("fsdp", "ctx"), None, "tp"),
            P(None, ("fsdp", "ctx")),
            P("tp", ("fsdp", "ctx")),
            P(("fsdp", "ctx")),
            P(("fsdp", "ctx")),
            P(("fsdp", "ctx")),
            P(("fsdp", "ctx"), "tp"),
            P(("fsdp", "ctx")),
            P("tp", ("fsdp", "ctx")),
            P(("fsdp", "ctx")),
        ),
        check_vma=False,
    )
```

```python
import functools

import jax
import jax.numpy as jnp
from jax import lax
from jax.experimental import pallas as pl
from jax.experimental.pallas import tpu as pltpu
from jax.sharding import PartitionSpec as P

HD = 80
epsilon = 1e-05
masked_score = -1e30
LOG2E = 1.4426950408889634
f32 = jnp.float32
bf16 = jnp.bfloat16
MESH = pl.DeviceIdType.MESH
VMEM = pl.BlockSpec(memory_space=pltpu.VMEM)
HBM = pl.BlockSpec(memory_space=pltpu.HBM)
VMEM_LIMIT = 62 * 1024 * 1024


def params(**kw):
    return pltpu.CompilerParams(vmem_limit_bytes=VMEM_LIMIT, **kw)


def dot(a, b, dims=((1,), (0,))):
    return lax.dot_general(a, b, (dims, ((), ())), preferred_element_type=f32)


NT = ((1,), (1,))
TN = ((0,), (0,))


def swap(value, axis):
    return lax.ppermute(value, axis, [(0, 1), (1, 0)])


def vector_kernel(v_ref, o_ref, got, lsem, ss, sr):
    f = lax.axis_index("fsdp")
    c = lax.axis_index("ctx")
    y = lax.axis_index("tp")
    me = (f * 2 + c) * 2 + y
    bar = pltpu.get_barrier_semaphore()

    def device(i):
        return (i // 4, (i // 2) % 2, i % 2)

    peers = [(me + d) % 32 for d in range(1, 32)]
    for p in peers:
        pl.semaphore_signal(bar, 1, device_id=device(p), device_id_type=MESH)
    pl.semaphore_wait(bar, 31)
    sent = []
    for d, p in enumerate(peers):
        copy = pltpu.make_async_remote_copy(
            src_ref=v_ref.at[p // 2],
            dst_ref=got.at[d + 1],
            send_sem=ss.at[d],
            recv_sem=sr.at[d],
            device_id=device(p),
            device_id_type=MESH,
        )
        copy.start()
        sent.append(copy)
    local = pltpu.make_async_copy(v_ref.at[me // 2], got.at[0], lsem)
    local.start()
    local.wait()
    total = got[0].astype(f32)
    for d in range(31):
        sent[d].wait_recv()
    for d in range(31):
        total = total + got[d + 1].astype(f32)
    o_ref[...] = total
    for copy in sent:
        copy.wait_send()


def sum_vectors(vectors, fsdp_count):
    if fsdp_count == 8:
        sem = pltpu.SemaphoreType.DMA
        return pl.pallas_call(
            vector_kernel,
            out_shape=jax.ShapeDtypeStruct(vectors.shape[1:], f32),
            in_specs=[VMEM],
            out_specs=VMEM,
            scratch_shapes=[
                pltpu.VMEM((32,) + vectors.shape[1:], bf16),
                sem,
                sem((31,)),
                sem((31,)),
            ],
            compiler_params=params(collective_id=2, has_side_effects=True),
        )(vectors.astype(bf16))
    partial = lax.psum(vectors, "tp")
    return lax.psum_scatter(partial, ("fsdp", "ctx"), scatter_dimension=0, tiled=False)


def scatter_kernel(spans, arrays, *refs):
    ins = refs[:arrays]
    outs = refs[arrays : 2 * arrays]
    own, near, mine, far, pair, last, lsem, cs, cr, xs, xr, zs, zr = refs[2 * arrays :]
    f = lax.axis_index("fsdp")
    c = lax.axis_index("ctx")
    y = lax.axis_index("tp")
    z, x = f // 2, f % 2
    bar = pltpu.get_barrier_semaphore()
    sibling = (f, 1 - c, y)
    across = (z * 2 + (1 - x), c, y)
    column = [None] + [(((z + d) % 4) * 2 + x, c, y) for d in (1, 2, 3)]
    for p in [sibling, across] + column[1:]:
        pl.semaphore_signal(bar, 1, device_id=p, device_id_type=MESH)
    pl.semaphore_wait(bar, 5)

    def remote(src, dst, s, r, dev):
        copy = pltpu.make_async_remote_copy(
            src_ref=src, dst_ref=dst, send_sem=s, recv_sem=r, device_id=dev, device_id_type=MESH
        )
        copy.start()
        return copy

    local, over_ctx, over_x, over_z = {}, {}, {}, {}
    for k, (a, start, width) in enumerate(spans):
        cols = pl.ds(start, width)
        fit = pl.ds(0, width)
        copy = pltpu.make_async_copy(ins[a].at[:, c, :, cols], own.at[k, :, :, fit], lsem.at[k])
        copy.start()
        local[k] = copy
        over_ctx[k] = remote(
            ins[a].at[:, 1 - c, :, cols], near.at[k, :, :, fit], cs.at[k], cr.at[k], sibling
        )

    def first(k):
        width = spans[k][2]
        local[k].wait()
        over_ctx[k].wait_recv()
        for i in range(8):
            total = own[k, i, :, :width].astype(f32) + near[k, i, :, :width].astype(f32)
            mine[k, i // 2, i % 2, :, :width] = total.astype(bf16)
        src = mine.at[k, :, 1 - x, :, pl.ds(0, width)]
        over_x[k] = remote(src, far.at[k, :, :, pl.ds(0, width)], xs.at[k], xr.at[k], across)

    def second(k):
        width = spans[k][2]
        over_x[k].wait_recv()
        for i in range(4):
            total = mine[k, i, x, :, :width].astype(f32) + far[k, i, :, :width].astype(f32)
            pair[k, i, :, :width] = total.astype(bf16)
        over_z[k] = [
            remote(
                pair.at[k, (z + d) % 4, :, pl.ds(0, width)],
                last.at[k, d - 1, :, pl.ds(0, width)],
                zs.at[k, d - 1],
                zr.at[k, d - 1],
                column[d],
            )
            for d in (1, 2, 3)
        ]

    def third(k):
        a, start, width = spans[k]
        total = pair[k, z, :, :width].astype(f32)
        for d in range(3):
            over_z[k][d].wait_recv()
            total = total + last[k, d, :, :width].astype(f32)
        outs[a][:, start : start + width] = total

    count = len(spans)
    for step in range(count + 2):
        if step < count:
            first(step)
        if 0 <= step - 1 < count:
            second(step - 1)
        if 0 <= step - 2 < count:
            third(step - 2)
    for k in range(count):
        over_ctx[k].wait_send()
        over_x[k].wait_send()
        for copy in over_z[k]:
            copy.wait_send()


def scatter_sums(grads, widest, fsdp_count):
    rows = grads[0].shape[0]
    owned = rows // (fsdp_count * 2)
    if fsdp_count == 8 and owned % 16 == 0:
        spans = []
        for a, grad in enumerate(grads):
            for start in range(0, grad.shape[1], widest):
                spans.append((a, start, min(widest, grad.shape[1] - start)))
        count = len(spans)
        sem = pltpu.SemaphoreType.DMA
        return pl.pallas_call(
            functools.partial(scatter_kernel, spans, len(grads)),
            in_specs=[HBM] * len(grads),
            out_specs=tuple([VMEM] * len(grads)),
            out_shape=tuple(jax.ShapeDtypeStruct((owned, g.shape[1]), f32) for g in grads),
            scratch_shapes=[
                pltpu.VMEM((count, 8, owned, widest), bf16),
                pltpu.VMEM((count, 8, owned, widest), bf16),
                pltpu.VMEM((count, 4, 2, owned, widest), bf16),
                pltpu.VMEM((count, 4, owned, widest), bf16),
                pltpu.VMEM((count, 4, owned, widest), bf16),
                pltpu.VMEM((count, 3, owned, widest), bf16),
            ]
            + [sem((count,))] * 5
            + [sem((count, 3))] * 2,
            compiler_params=params(collective_id=3, has_side_effects=True),
        )(*[g.reshape(8, 2, owned, g.shape[1]) for g in grads])
    whole = lax.psum_scatter(
        jnp.concatenate(grads, axis=1), ("fsdp", "ctx"), scatter_dimension=0, tiled=True
    ).astype(f32)
    edges = [sum(g.shape[1] for g in grads[:i]) for i in range(len(grads) + 1)]
    return [whole[:, a:b] for a, b in zip(edges, edges[1:])]


def normalize(values):
    centered = values - jnp.mean(values, axis=-1, keepdims=True)
    inverse = lax.rsqrt(jnp.mean(centered * centered, axis=-1, keepdims=True) + epsilon)
    return centered * inverse, inverse


def project_kernel(x_ref, gain_ref, shift_ref, w_ref, b_ref, n_ref, p_ref):
    values = x_ref[...].astype(f32)
    hat, _ = normalize(values)
    low = (hat * gain_ref[...] + shift_ref[...]).astype(bf16)
    n_ref[...] = low
    p_ref[...] = (dot(low, w_ref[...]) + b_ref[...]).astype(bf16)


def project(x_all, gain, shift, weight, bias):
    rows, model = x_all.shape
    width = weight.shape[1]
    block = 256
    fixed = lambda i: (0, 0)
    return pl.pallas_call(
        project_kernel,
        grid=(rows // block,),
        in_specs=[
            pl.BlockSpec((block, model), lambda i: (i, 0)),
            pl.BlockSpec((1, model), fixed),
            pl.BlockSpec((1, model), fixed),
            pl.BlockSpec((model, width), fixed),
            pl.BlockSpec((1, width), fixed),
        ],
        out_specs=(
            pl.BlockSpec((block, model), lambda i: (i, 0)),
            pl.BlockSpec((block, width), lambda i: (i, 0)),
        ),
        out_shape=(
            jax.ShapeDtypeStruct((rows, model), bf16),
            jax.ShapeDtypeStruct((rows, width), bf16),
        ),
        compiler_params=params(),
        cost_estimate=pl.CostEstimate(
            flops=2 * rows * model * width, bytes_accessed=12 << 20, transcendentals=0
        ),
    )(x_all, gain, shift, weight, bias)


def head_window(head):
    start = head * HD // 128 * 128
    stop = -(-(head * HD + HD) // 128) * 128
    lanes = lax.broadcasted_iota(jnp.int32, (1, stop - start), 1) + start
    return start, stop, (lanes >= head * HD) & (lanes < head * HD + HD)


def attend_kernel(heads, proj_ref, far_ref, bias_ref, att_ref, lse_ref, acc_ref, stat_ref):
    rows = proj_ref.shape[0]
    width = heads * HD
    block = 256
    acc_ref[...] = jnp.zeros_like(acc_ref)
    stat_ref[...] = jnp.zeros_like(stat_ref)
    score_factor = HD ** (-0.5) * LOG2E

    def step(i, carry):
        at = pl.ds(pl.multiple_of(i * block, block), block)
        for head in range(heads):
            start, stop, mask = head_window(head)
            query = jnp.where(mask, proj_ref[at, start:stop], jnp.zeros((), bf16))
            near = dot(query, proj_ref[:, width + start : width + stop], NT)
            far = dot(query, far_ref[:, start:stop], NT)
            near = near * score_factor + bias_ref[0:1, :rows]
            far = far * score_factor + bias_ref[0:1, rows:]
            top = jnp.maximum(
                jnp.max(near, axis=-1, keepdims=True), jnp.max(far, axis=-1, keepdims=True)
            )
            near = jnp.exp2(near - top)
            far = jnp.exp2(far - top)
            total = jnp.sum(near, axis=-1, keepdims=True) + jnp.sum(far, axis=-1, keepdims=True)
            mixed = dot(near.astype(bf16), proj_ref[:, 2 * width + start : 2 * width + stop])
            mixed = mixed + dot(far.astype(bf16), far_ref[:, width + start : width + stop])
            mixed = mixed * (1.0 / total)
            acc_ref[at, start:stop] += jnp.where(mask, mixed, 0.0)
            lane = lax.broadcasted_iota(jnp.int32, (1, 128), 1)
            stat_ref[at, :] += jnp.where(lane == head, top + jnp.log2(total), 0.0)
        return carry

    lax.fori_loop(0, rows // block, step, 0)
    att_ref[...] = acc_ref[...].astype(bf16)
    lse_ref[...] = stat_ref[...].T


def attend(proj, far, bias, heads):
    rows = proj.shape[0]
    return pl.pallas_call(
        functools.partial(attend_kernel, heads),
        in_specs=[VMEM] * 3,
        out_specs=(VMEM, VMEM),
        out_shape=(
            jax.ShapeDtypeStruct((rows, heads * HD), bf16),
            jax.ShapeDtypeStruct((128, rows), f32),
        ),
        scratch_shapes=[pltpu.VMEM((rows, heads * HD), f32), pltpu.VMEM((rows, 128), f32)],
        compiler_params=params(),
        cost_estimate=pl.CostEstimate(
            flops=4 * heads * rows * 2 * rows * 256, bytes_accessed=8 << 20, transcendentals=0
        ),
    )(proj, far, bias)


def attend_back_kernel(
    heads, proj_ref, far_ref, bias_ref, att_ref, grad_ref, lse_ref,
    dq_ref, dnear_ref, dfar_ref, key_ref, value_ref, keyt_ref, dqt_ref, dot_ref, dkv_ref,
):
    rows = proj_ref.shape[0]
    width = heads * HD
    block = 256
    score_factor = HD ** (-0.5) * LOG2E
    key_ref[:rows] = proj_ref[:, width : 2 * width]
    key_ref[rows:] = far_ref[:, :width]
    value_ref[:rows] = proj_ref[:, 2 * width :]
    value_ref[rows:] = far_ref[:, width:]
    keyt_ref[...] = key_ref[...].T
    dqt_ref[...] = jnp.zeros_like(dqt_ref)
    dkv_ref[...] = jnp.zeros_like(dkv_ref)
    product = grad_ref[...].astype(f32) * att_ref[...].astype(f32)
    high = product.astype(bf16)
    low = (product - high.astype(f32)).astype(bf16)
    lane = lax.broadcasted_iota(jnp.int32, (16, width), 1)
    row = lax.broadcasted_iota(jnp.int32, (16, width), 0)
    pick = jnp.where((lane >= row * HD) & (lane < row * HD + HD), 1.0, 0.0).astype(bf16)
    dot_ref[...] = dot(pick, high, NT) + dot(pick, low, NT)

    def step(i, carry):
        at = pl.ds(pl.multiple_of(i * block, block), block)
        bias = bias_ref[at, 0:1]
        for head in range(heads):
            start, stop, mask = head_window(head)
            zero = jnp.zeros((), bf16)
            query = jnp.where(mask, proj_ref[:, start:stop], zero)
            grad = jnp.where(mask, grad_ref[:, start:stop], zero)
            scores = dot(key_ref[at, start:stop], query, NT) * score_factor + bias
            probs = jnp.exp2(scores - lse_ref[head : head + 1, :])
            grad_probs = dot(value_ref[at, start:stop], grad, NT)
            grad_scores = (probs * (grad_probs - dot_ref[head : head + 1, :])).astype(bf16)
            dkv_ref[at, start:stop] += dot(grad_scores, query)
            dkv_ref[at, width + start : width + stop] += dot(probs.astype(bf16), grad)
            keyt = keyt_ref[head * HD : head * HD + HD, at]
            dqt_ref[head * HD : head * HD + HD, :] += dot(keyt, grad_scores)
        return carry

    lax.fori_loop(0, 2 * rows // block, step, 0)
    scale = HD ** (-0.5)
    dq_ref[...] = (dqt_ref[...].T * scale).astype(bf16)
    dnear_ref[:, :width] = dkv_ref[:rows, :width] * scale
    dnear_ref[:, width:] = dkv_ref[:rows, width:]
    dfar_ref[:, :width] = (dkv_ref[rows:, :width] * scale).astype(bf16)
    dfar_ref[:, width:] = dkv_ref[rows:, width:].astype(bf16)


def attend_back(proj, far, bias, attended, grad, lse, heads):
    rows = proj.shape[0]
    width = heads * HD
    return pl.pallas_call(
        functools.partial(attend_back_kernel, heads),
        in_specs=[VMEM] * 6,
        out_specs=(VMEM, VMEM, VMEM),
        out_shape=(
            jax.ShapeDtypeStruct((rows, width), bf16),
            jax.ShapeDtypeStruct((rows, 2 * width), f32),
            jax.ShapeDtypeStruct((rows, 2 * width), bf16),
        ),
        scratch_shapes=[
            pltpu.VMEM((2 * rows, width), bf16),
            pltpu.VMEM((2 * rows, width), bf16),
            pltpu.VMEM((width, 2 * rows), bf16),
            pltpu.VMEM((width, rows), f32),
            pltpu.VMEM((16, rows), f32),
            pltpu.VMEM((2 * rows, 2 * width), f32),
        ],
        compiler_params=params(),
        cost_estimate=pl.CostEstimate(
            flops=10 * heads * rows * 2 * rows * 256, bytes_accessed=16 << 20, transcendentals=0
        ),
    )(proj, far, bias, attended, grad, lse)


def residual_kernel(x_ref, own_ref, oth_ref, wa_ref, wb_ref, vec_ref, r_ref, n_ref):
    mixed = dot(own_ref[...], wa_ref[...], NT) + dot(oth_ref[...], wb_ref[...], NT)
    residual = x_ref[...].astype(f32) + (mixed + vec_ref[0:1, :])
    r_ref[...] = residual
    hat, _ = normalize(residual)
    n_ref[...] = (hat * vec_ref[1:2, :] + vec_ref[2:3, :]).astype(bf16)


def residual_step(x_all, own, oth, weights, width, vectors):
    rows, model = x_all.shape
    block = 128
    return pl.pallas_call(
        residual_kernel,
        grid=(rows // block,),
        in_specs=[
            pl.BlockSpec((block, model), lambda i: (i, 0)),
            pl.BlockSpec((block, width), lambda i: (i, 0)),
            pl.BlockSpec((block, width), lambda i: ((i + rows // block // 2) % (rows // block), 0)),
            pl.BlockSpec((model, width), lambda i: (0, 0)),
            pl.BlockSpec((model, width), lambda i: (0, 1)),
            pl.BlockSpec(vectors.shape, lambda i: (0, 0)),
        ],
        out_specs=(
            pl.BlockSpec((block, model), lambda i: (i, 0)),
            pl.BlockSpec((block, model), lambda i: (i, 0)),
        ),
        out_shape=(
            jax.ShapeDtypeStruct((rows, model), f32),
            jax.ShapeDtypeStruct((rows, model), bf16),
        ),
        compiler_params=params(),
        cost_estimate=pl.CostEstimate(
            flops=4 * rows * model * width, bytes_accessed=12 << 20, transcendentals=0
        ),
    )(x_all, own, oth, weights, weights, vectors)


def hidden_kernel(blocks, n_ref, g_ref, we_ref, wc_ref, b_ref, act_ref, pre_ref, sum_ref, own_ref, oth_ref, acc_ref):
    k = pl.program_id(0)
    rows = n_ref.shape[0]
    half = rows // 2
    piece = 256

    @pl.when(k == 0)
    def _():
        acc_ref[...] = jnp.zeros_like(acc_ref)

    total = jnp.zeros((1, b_ref.shape[1]), f32)
    for i in range(rows // piece):
        at = slice(i * piece, (i + 1) * piece)
        pre = dot(n_ref[at], we_ref[...]) + b_ref[...]
        back = dot(g_ref[at], wc_ref[...])
        cdf = 0.5 + 0.5 * lax.erf(pre * (0.5**0.5))
        density = jnp.exp(pre * pre * -0.5) * 0.3989422804014327
        act_ref[at] = (pre * cdf).astype(bf16)
        low = (back * (cdf + pre * density)).astype(bf16)
        pre_ref[at] = low
        total = total + jnp.sum(low.astype(f32), axis=0, keepdims=True)
        acc_ref[at] += dot(low, we_ref[...], NT)
    sum_ref[...] = total

    @pl.when(k == blocks - 1)
    def _():
        own_ref[...] = acc_ref[:half]
        oth_ref[...] = acc_ref[half:].astype(bf16)


def hidden_step(normed, grad, weights, expand_at, contract_at, width, bias):
    rows, model = normed.shape
    block = 256
    blocks = width // block
    half = rows // 2
    fixed = lambda k: (0, 0)
    return pl.pallas_call(
        functools.partial(hidden_kernel, blocks),
        grid=(blocks,),
        in_specs=[
            pl.BlockSpec((rows, model), fixed),
            pl.BlockSpec((rows, model), fixed),
            pl.BlockSpec((model, block), lambda k: (0, expand_at // block + k)),
            pl.BlockSpec((model, block), lambda k: (0, contract_at // block + k)),
            pl.BlockSpec((1, block), lambda k: (0, k)),
        ],
        out_specs=(
            pl.BlockSpec((rows, block), lambda k: (0, k)),
            pl.BlockSpec((rows, block), lambda k: (0, k)),
            pl.BlockSpec((1, block), lambda k: (0, k)),
            pl.BlockSpec((half, model), fixed),
            pl.BlockSpec((half, model), fixed),
        ),
        out_shape=(
            jax.ShapeDtypeStruct((rows, width), bf16),
            jax.ShapeDtypeStruct((rows, width), bf16),
            jax.ShapeDtypeStruct((1, width), f32),
            jax.ShapeDtypeStruct((half, model), f32),
            jax.ShapeDtypeStruct((half, model), bf16),
        ),
        scratch_shapes=[pltpu.VMEM((rows, model), f32)],
        compiler_params=params(),
        cost_estimate=pl.CostEstimate(
            flops=6 * rows * model * width, bytes_accessed=28 << 20, transcendentals=0
        ),
    )(normed, grad, weights, weights, bias)


def norm_back_kernel(round_low, own_ref, oth_ref, base_ref, add_ref, gain_ref, *outs):
    i = pl.program_id(0)
    grad = own_ref[...].astype(f32) + oth_ref[...].astype(f32)
    hat, inverse = normalize(base_ref[...].astype(f32))
    scaled = grad * gain_ref[...]
    first = jnp.mean(scaled, axis=-1, keepdims=True)
    second = jnp.mean(scaled * hat, axis=-1, keepdims=True)
    result = add_ref[...].astype(f32) + inverse * (scaled - first - hat * second)
    outs[0][...] = result
    sums = outs[-1]

    @pl.when(i == 0)
    def _():
        sums[...] = jnp.zeros_like(sums)

    sums[0:1] += jnp.sum(grad * hat, axis=0, keepdims=True)
    sums[1:2] += jnp.sum(grad, axis=0, keepdims=True)
    if round_low:
        low = result.astype(bf16)
        outs[1][...] = low
        sums[2:3] += jnp.sum(low.astype(f32), axis=0, keepdims=True)


def norm_back(own, oth, base, add, gain, round_low):
    rows, model = own.shape
    block = 128
    spec = pl.BlockSpec((block, model), lambda i: (i, 0))
    outs = [jax.ShapeDtypeStruct((rows, model), f32)]
    if round_low:
        outs.append(jax.ShapeDtypeStruct((rows, model), bf16))
    outs.append(jax.ShapeDtypeStruct((8, model), f32))
    return pl.pallas_call(
        functools.partial(norm_back_kernel, round_low),
        grid=(rows // block,),
        in_specs=[spec] * 4 + [pl.BlockSpec((1, model), lambda i: (0, 0))],
        out_specs=tuple([spec] * (len(outs) - 1) + [pl.BlockSpec((8, model), lambda i: (0, 0))]),
        out_shape=tuple(outs),
        compiler_params=params(),
    )(own, oth, base, add, gain)


def forward_kernel(
    x_in, g_in, s_in, wa, wo, we, wc, bias_ref,
    inner_out, outer_out, n1_out, proj_out, far_out, att_out, lse_ref, res_out, n2_out, g_out,
    act_out, pre_out, esum_ref, dn_own, dn_oth, ho_own, ho_oth, vec_ref,
    so, ina, oa, ob, la, xb, gb, n1, proj, far, tb, eb, acc, stat, att, atto, res, n2, stage, dn, ho,
    ld, ss, sr, zs, zr, xs, xr, cs, cr, ys, yr, fs, fr, outs,
):
    f = lax.axis_index("fsdp")
    c = lax.axis_index("ctx")
    y = lax.axis_index("tp")
    z, x = f // 2, f % 2
    rows, model = xb.shape
    slot = rows // 2
    width = wo.shape[2]
    hidden = we.shape[2]
    each = wa.shape[1] * 2
    blocks = la.shape[0] // 2
    block = la.shape[-1]
    a_count, a_width = ina.shape[0], ina.shape[-1]
    heads = width // HD
    sibling = (f, 1 - c, y)
    across = (z * 2 + (1 - x), c, y)
    partner = (f, c, 1 - y)
    column = [(((z + d) % 4) * 2 + x, c, y) for d in (1, 2, 3)]
    others = [((f + d) % 8, c, y) for d in range(1, 8)]

    def remote(src, dst, s, r, dev):
        copy = pltpu.make_async_remote_copy(
            src_ref=src, dst_ref=dst, send_sem=s, recv_sem=r, device_id=dev, device_id_type=MESH
        )
        copy.start()
        return copy

    def local(src, dst, s):
        copy = pltpu.make_async_copy(src, dst, s)
        copy.start()
        return copy

    def taken(ref, sem):
        pltpu.make_async_copy(ref, ref, sem).wait()

    order = list(range(1, a_count)) + [0]
    own_x = local(x_in, xb.at[pl.ds(0, slot)], ld.at[0])
    own_s = local(s_in, so.at[f], ld.at[1])
    own_g = local(g_in, gb.at[pl.ds(0, slot)], ld.at[2])
    own_o = local(wo.at[c], oa.at[z, x, c], ld.at[3])
    own_a = [
        local(wa.at[c, :, pl.ds(k * a_width, a_width)], ina.at[k, z, x, c], ld.at[4 + k])
        for k in order
    ]
    own_l = [
        local(
            (we if j % 2 == 0 else wc).at[c, :, pl.ds(j // 2 * block, block)],
            la.at[j, z, x, c],
            ld.at[4 + a_count + j],
        )
        for j in range(2 * blocks)
    ]
    bar = pltpu.get_barrier_semaphore()
    for p in others + [sibling, partner]:
        pl.semaphore_signal(bar, 1, device_id=p, device_id_type=MESH)
    pl.semaphore_wait(bar, 9)

    def over_z(q, buf):
        piece = buf.at[z, x, c]
        return [remote(piece, piece, zs.at[q, d], zr.at[q], column[d]) for d in range(3)]

    def over_x(q, buf):
        taken(buf.at[pl.ds(0, 3), 0, 0], zr.at[q])
        remote(buf.at[:, x, c], buf.at[:, x, c], xs.at[q], xr.at[q], across)

    def over_c(q, buf):
        taken(buf.at[:, 0, 0], xr.at[q])
        remote(buf.at[:, :, c], buf.at[:, :, c], cs.at[q], cr.at[q], sibling)

    def ready(q, buf):
        taken(buf.at[:, :, 0], cr.at[q])

    sent = []
    own_s.wait()
    sent += [remote(so.at[f], so.at[f], ss.at[d], sr.at[d], others[d]) for d in range(7)]
    own_x.wait()
    sent.append(
        remote(xb.at[pl.ds(0, slot)], xb.at[pl.ds(slot, slot)], ys.at[0], yr.at[0], partner)
    )
    a_at = {}
    for q, k in enumerate(order):
        own_a[q].wait()
        sent += over_z(q, ina.at[k])
        a_at[q] = ina.at[k]
    o_q = a_count
    l_q = a_count + 1
    own_o.wait()
    sent += over_z(o_q, oa)
    for j in range(2 * blocks):
        own_l[j].wait()
        sent += over_z(l_q + j, la.at[j])
    own_g.wait()
    sent.append(
        remote(gb.at[pl.ds(0, slot)], gb.at[pl.ds(slot, slot)], ys.at[1], yr.at[1], partner)
    )

    for d in range(7):
        taken(so.at[(f - d - 1 + 8) % 8], sr.at[d])
    lanes = so.shape[2]
    step_row = lax.broadcasted_iota(jnp.int32, (lanes, model), 0)
    step_col = lax.broadcasted_iota(jnp.int32, (lanes, model), 1)
    total = jnp.zeros((so.shape[1], model), f32)
    for i in range(8):
        pick = (step_col == step_row + i * each) & (step_row < each)
        total = total + dot(so[i], jnp.where(pick, 1.0, 0.0).astype(bf16))
    vec_ref[...] = total
    per = hidden // 4
    step_row = lax.broadcasted_iota(jnp.int32, (lanes, per), 0)
    step_col = lax.broadcasted_iota(jnp.int32, (lanes, per), 1)
    for i in range(4):
        total = jnp.zeros((so.shape[1], per), f32)
        which = lax.broadcasted_iota(jnp.int32, (so.shape[1], 1), 0)
        for r in range(per // each):
            pick = (step_col == step_row + r * each) & (step_row < each)
            row = jnp.where(which == 8 + r, so[4 * y + i], jnp.zeros((), bf16))
            total = total + dot(row, jnp.where(pick, 1.0, 0.0).astype(bf16))
        eb[:, i * per : (i + 1) * per] = jnp.sum(total, axis=0, keepdims=True)
    near = pl.ds(pl.multiple_of(y * width, 128), width)
    tb[:, :width] = vec_ref[2:3, near]
    tb[:, width : 2 * width] = jnp.zeros((1, width), f32)
    tb[:, 2 * width :] = vec_ref[3:4, near]

    def first_norm(start):
        def body(i, carry):
            at = pl.ds(pl.multiple_of(start + i * 128, 128), 128)
            hat, _ = normalize(xb[at].astype(f32))
            n1[at] = (hat * vec_ref[0:1] + vec_ref[1:2]).astype(bf16)
            return carry

        lax.fori_loop(0, slot // 128, body, 0)

    first_norm(0)
    over_x(0, a_at[0])
    over_x(1, a_at[1])
    over_c(0, a_at[0])
    over_x(2, a_at[2])
    over_c(1, a_at[1])
    over_x(3, a_at[3])
    over_c(2, a_at[2])
    taken(xb.at[pl.ds(slot, slot)], yr.at[0])
    first_norm(slot)

    def project_chunk(q):
        k = order[q]
        ready(q, a_at[q])
        cols = slice(k * a_width, (k + 1) * a_width)

        def body(i, carry):
            at = pl.ds(pl.multiple_of(i * 256, 256), 256)
            proj[at, cols] = (dot(n1[at], ina[k].reshape(model, a_width)) + tb[:, cols]).astype(bf16)
            return carry

        lax.fori_loop(0, rows // 256, body, 0)
        start, stop = max(k * a_width, width), (k + 1) * a_width
        if start < stop:
            sent.append(
                remote(
                    proj.at[:, pl.ds(start, stop - start)],
                    far.at[:, pl.ds(start - width, stop - start)],
                    fs.at[k],
                    fr.at[k],
                    sibling,
                )
            )

    project_chunk(0)
    project_chunk(1)
    over_x(4, a_at[4])
    over_c(3, a_at[3])
    project_chunk(2)
    project_chunk(3)
    over_c(4, a_at[4])
    over_x(o_q, oa)
    project_chunk(4)
    writes = [local(n1, n1_out, outs.at[0]), local(proj, proj_out, outs.at[1])]
    for k in range(1, a_count):
        start, stop = max(k * a_width, width), (k + 1) * a_width
        taken(far.at[:, pl.ds(start - width, stop - start)], fr.at[k])
    writes.append(local(far, far_out, outs.at[2]))

    stat[...] = jnp.zeros_like(stat)
    score_factor = HD ** (-0.5) * LOG2E
    tall = acc.shape[0]

    def attend_step(i, carry):
        at = pl.ds(pl.multiple_of(i * tall, tall), tall)
        acc[...] = jnp.zeros_like(acc)
        for head in range(heads):
            start, stop, mask = head_window(head)
            query = jnp.where(mask, proj[at, start:stop], jnp.zeros((), bf16))
            a = dot(query, proj[:, width + start : width + stop], NT)
            b = dot(query, far[:, start:stop], NT)
            a = a * score_factor + bias_ref[0:1, :rows]
            b = b * score_factor + bias_ref[0:1, rows:]
            top = jnp.maximum(
                jnp.max(a, axis=-1, keepdims=True), jnp.max(b, axis=-1, keepdims=True)
            )
            a = jnp.exp2(a - top)
            b = jnp.exp2(b - top)
            total = jnp.sum(a, axis=-1, keepdims=True) + jnp.sum(b, axis=-1, keepdims=True)
            mixed = dot(a.astype(bf16), proj[:, 2 * width + start : 2 * width + stop])
            mixed = mixed + dot(b.astype(bf16), far[:, width + start : width + stop])
            mixed = mixed * (1.0 / total)
            acc[:, start:stop] += jnp.where(mask, mixed, 0.0)
            lane = lax.broadcasted_iota(jnp.int32, (1, 128), 1)
            stat[at, :] += jnp.where(lane == head, top + jnp.log2(total), 0.0)
        att[at] = acc[...].astype(bf16)
        remote(att.at[at], atto.at[at], ys.at[3 + i], yr.at[3 + i], partner)
        over_x(l_q + i, la.at[i])

        @pl.when(i == 0)
        def _():
            over_c(o_q, oa)
            remote(oa.at[:, :, c], ob.at[:, :, c], ys.at[2], yr.at[2], partner)

        @pl.when(i > 0)
        def _():
            over_c(l_q + i - 1, la.at[i - 1])

        return carry

    steps = rows // tall
    lax.fori_loop(0, steps, attend_step, 0)
    lse_ref[...] = stat[...].T
    writes.append(local(att, att_out, outs.at[3]))
    over_x(l_q + 3, la.at[3])
    over_c(l_q + 2, la.at[2])
    taken(ob.at[:, :, c], yr.at[2])
    b_q = zs.shape[0] - 1
    remote(ob.at[:, :, c], ob.at[:, :, c], cs.at[b_q], cr.at[b_q], sibling)
    over_x(l_q + 4, la.at[4])
    over_c(l_q + 3, la.at[3])
    over_x(l_q + 5, la.at[5])
    over_c(l_q + 4, la.at[4])
    ready(o_q, oa)
    ready(b_q, ob)
    writes.append(local(oa, outer_out, outs.at[4]))
    for q, k in enumerate(order):
        writes.append(
            local(ina.at[k], inner_out.at[:, :, :, :, pl.ds(k * a_width, a_width)], outs.at[5 + k])
        )
    for i in range(steps):
        at = pl.ds(i * tall, tall)
        taken(atto.at[at], yr.at[3 + i])

    def residual_half(i):
        at = slice(i * slot, (i + 1) * slot)
        back = slice((1 - i) * slot, (2 - i) * slot)
        mixed = dot(att[at], oa[...].reshape(model, width), NT)
        res[at] = mixed + dot(atto[back], ob[...].reshape(model, width), NT)

        def body(j, carry):
            row = pl.ds(pl.multiple_of(i * slot + j * 128, 128), 128)
            value = xb[row].astype(f32) + (res[row] + vec_ref[4:5])
            res[row] = value
            hat, _ = normalize(value)
            n2[row] = (hat * vec_ref[5:6] + vec_ref[6:7]).astype(bf16)
            return carry

        lax.fori_loop(0, slot // 128, body, 0)

    residual_half(0)
    over_x(l_q + 6, la.at[6])
    over_c(l_q + 5, la.at[5])
    residual_half(1)
    late_writes = [
        local(res.at[pl.ds(0, slot)], res_out, outs.at[5 + a_count]),
        local(n2, n2_out, outs.at[6 + a_count]),
    ]
    taken(gb.at[pl.ds(slot, slot)], yr.at[1])
    late_writes.append(local(gb, g_out, outs.at[7 + a_count]))
    dn[...] = jnp.zeros_like(dn)
    ho[...] = jnp.zeros_like(ho)
    s_at = 8 + a_count

    def hidden_step_in(b, carry):
        ready(l_q + 2 * b, la.at[2 * b])
        ready(l_q + 2 * b + 1, la.at[2 * b + 1])
        turn = b % 2
        cols = pl.ds(pl.multiple_of(b * block, block), block)

        @pl.when(b > 1)
        def _():
            taken(stage.at[0, turn], outs.at[s_at + turn])
            taken(stage.at[1, turn], outs.at[s_at + 2 + turn])

        shift = eb[:, cols]
        total = jnp.zeros((1, block), f32)
        for i in range(rows // 256):
            at = slice(i * 256, (i + 1) * 256)
            pre = dot(n2[at], la[2 * b].reshape(model, block)) + shift
            back = dot(gb[at], la[2 * b + 1].reshape(model, block))
            cdf = 0.5 + 0.5 * lax.erf(pre * (0.5**0.5))
            density = jnp.exp(pre * pre * -0.5) * 0.3989422804014327
            low = (back * (cdf + pre * density)).astype(bf16)
            active = (pre * cdf).astype(bf16)
            stage[0, turn, at] = active
            stage[1, turn, at] = low
            total = total + jnp.sum(low.astype(f32), axis=0, keepdims=True)
            dn[at] += dot(low, la[2 * b].reshape(model, block), NT)
            ho[at] += dot(active, la[2 * b + 1].reshape(model, block), NT)
        esum_ref[:, cols] = total
        local(stage.at[0, turn], act_out.at[:, cols], outs.at[s_at + turn])
        local(stage.at[1, turn], pre_out.at[:, cols], outs.at[s_at + 2 + turn])

        @pl.when(b < 3)
        def _():
            over_x(l_q + 7 + b, la.at[7 + b])

        @pl.when(b < 4)
        def _():
            over_c(l_q + 6 + b, la.at[6 + b])

        return carry

    lax.fori_loop(0, blocks, hidden_step_in, 0)
    for copy in writes:
        copy.wait()
    n1[:slot] = dn[slot:].astype(bf16)
    n1[slot:] = ho[slot:].astype(bf16)
    last = [
        local(dn.at[pl.ds(0, slot)], dn_own, ld.at[0]),
        local(ho.at[pl.ds(0, slot)], ho_own, ld.at[1]),
        local(n1.at[pl.ds(0, slot)], dn_oth, ld.at[2]),
        local(n1.at[pl.ds(slot, slot)], ho_oth, ld.at[3]),
    ]
    for turn in range(2):
        taken(stage.at[0, turn], outs.at[s_at + turn])
        taken(stage.at[1, turn], outs.at[s_at + 2 + turn])
    for copy in late_writes + last:
        copy.wait()
    for copy in sent:
        copy.wait_send()
    for q in range(zs.shape[0]):
        if q < a_count:
            buf = a_at[q]
        elif q == o_q:
            buf = oa
        elif q == b_q:
            buf = ob
        else:
            buf = la.at[q - l_q]
        taken(buf.at[:, :, 0], cs.at[q])
        if q != b_q:
            taken(buf.at[:, 0, 0], xs.at[q])
    taken(oa.at[:, :, 0], ys.at[2])
    for i in range(steps):
        taken(att.at[pl.ds(i * tall, tall)], ys.at[3 + i])


def forward(x_own, g_own, smalls, wa, wo, we, wc, bias):
    slot, model = x_own.shape
    rows = 2 * slot
    each = wa.shape[0]
    width, hidden = wo.shape[1], we.shape[1]
    half = each // 2
    a_width, block = 384, 512
    a_count, blocks = 3 * width // a_width, hidden // block
    grid = (4, 2, 2, half)
    chunks = a_count + 2 + 2 * blocks
    sem = pltpu.SemaphoreType.DMA
    out = jax.ShapeDtypeStruct

    def halves(w):
        return w.reshape(2, half, w.shape[1])

    return pl.pallas_call(
        forward_kernel,
        in_specs=[HBM] * 7 + [VMEM],
        out_specs=(HBM,) * 6 + (VMEM,) + (HBM,) * 5 + (VMEM,) + (HBM,) * 4 + (VMEM,),
        out_shape=(
            out(grid + (3 * width,), bf16),
            out(grid + (width,), bf16),
            out((rows, model), bf16),
            out((rows, 3 * width), bf16),
            out((rows, 2 * width), bf16),
            out((rows, width), bf16),
            out((128, rows), f32),
            out((slot, model), f32),
            out((rows, model), bf16),
            out((rows, model), bf16),
            out((rows, hidden), bf16),
            out((rows, hidden), bf16),
            out((1, hidden), f32),
            out((slot, model), f32),
            out((slot, model), bf16),
            out((slot, model), f32),
            out((slot, model), bf16),
            out((16, model), f32),
        ),
        scratch_shapes=[
            pltpu.VMEM((8,) + smalls.shape, bf16),
            pltpu.VMEM((a_count,) + grid + (a_width,), bf16),
            pltpu.VMEM(grid + (width,), bf16),
            pltpu.VMEM(grid + (width,), bf16),
            pltpu.VMEM((2 * blocks,) + grid + (block,), bf16),
            pltpu.VMEM((rows, model), bf16),
            pltpu.VMEM((rows, model), bf16),
            pltpu.VMEM((rows, model), bf16),
            pltpu.VMEM((rows, 3 * width), bf16),
            pltpu.VMEM((rows, 2 * width), bf16),
            pltpu.VMEM((1, 3 * width), f32),
            pltpu.VMEM((1, hidden), f32),
            pltpu.VMEM((256, width), f32),
            pltpu.VMEM((rows, 128), f32),
            pltpu.VMEM((rows, width), bf16),
            pltpu.VMEM((rows, width), bf16),
            pltpu.VMEM((rows, model), f32),
            pltpu.VMEM((rows, model), bf16),
            pltpu.VMEM((2, 2, rows, block), bf16),
            pltpu.VMEM((rows, model), f32),
            pltpu.VMEM((rows, model), f32),
            sem((4 + a_count + 2 * blocks,)),
            sem((7,)),
            sem((7,)),
            sem((chunks, 3)),
            sem((chunks,)),
            sem((chunks,)),
            sem((chunks,)),
            sem((chunks,)),
            sem((chunks,)),
            sem((3 + rows // 256,)),
            sem((3 + rows // 256,)),
            sem((a_count,)),
            sem((a_count,)),
            sem((12 + a_count,)),
        ],
        compiler_params=params(collective_id=1, has_side_effects=True),
    )(x_own, g_own, smalls, halves(wa), halves(wo), halves(we), halves(wc), bias)


def backward_kernel(
    act_in, pre_in, n2_in, g_in, dn_in, dno_in, res_in, proj_in, far_in, att_in, n1_in, inner_in, outer_in, x_in,
    lse_ref, bias_ref, vec_ref, esum_ref,
    hg_out, ge_ref, gc_ref, go_ref, ga_ref, sum_ref, esum_out,
    u, att, dqt, keyt, dots, acc, drecv, oa, b1, b2, t1, t2, res, dn, dnr, stream, gproj, own, near, far, one, two, flat,
    part, got,
    ld, cs, cr, xs, xr, zs, zr, ws, wr, ys, yr, fs, fr, vs, vr, free,
):
    f = lax.axis_index("fsdp")
    c = lax.axis_index("ctx")
    y = lax.axis_index("tp")
    z, x = f // 2, f % 2
    hi, lo = z // 2, z % 2
    rows, model = b1.shape
    slot = rows // 2
    width = att.shape[1]
    heads = width // HD
    ring = own.shape[0]
    tile = 128
    per = pre_in.shape[1] // width
    pieces = slot // tile
    block = acc.shape[0]
    sibling = (f, 1 - c, y)
    across = (z * 2 + (1 - x), c, y)
    partner = (f, c, 1 - y)
    beside = ((hi * 2 + 1 - lo) * 2 + x, c, y)
    beyond = (((1 - hi) * 2 + lo) * 2 + x, c, y)
    opposite = (((1 - hi) * 2 + 1 - lo) * 2 + x, c, y)
    diagonal = (f, 1 - c, 1 - y)

    def remote(src, dst, s, r, dev):
        pltpu.make_async_remote_copy(
            src_ref=src, dst_ref=dst, send_sem=s, recv_sem=r, device_id=dev, device_id_type=MESH
        ).start()

    def local(src, dst, s):
        copy = pltpu.make_async_copy(src, dst, s)
        copy.start()
        return copy

    def taken(ref, sem):
        pltpu.make_async_copy(ref, ref, sem).wait()

    def columns(k):
        return pl.ds(pl.multiple_of(k * width, tile), width)

    own_n2 = local(n2_in, b1, ld.at[0])
    own_g = local(g_in, b2, ld.at[1])
    for k in range(2):
        local(pre_in.at[:, columns(k)], stream.at[k], ld.at[2 + k])
    own_res = local(res_in, res, ld.at[4])
    own_dn = local(dn_in, dn, ld.at[5])
    own_oa = local(outer_in, oa, ld.at[6])
    own_att = local(att_in, att, ld.at[7])
    own_proj = local(proj_in, u.at[pl.ds(0, rows)], ld.at[8])
    own_far = local(far_in, u.at[pl.ds(rows, rows), pl.ds(width, 2 * width)], ld.at[9])
    bar = pltpu.get_barrier_semaphore()
    for p in [sibling, across, partner, beside, beyond, opposite, diagonal]:
        pl.semaphore_signal(bar, 1, device_id=p, device_id_type=MESH)
    pl.semaphore_wait(bar, 7)
    remote(dno_in, dnr, ys.at[0], yr.at[0], partner)

    def turned(dst, src, start, count):
        def body(i, carry):
            at = pl.ds(pl.multiple_of(start + i * tile, tile), tile)
            dst[:, at] = src[at].T
            return carry

        lax.fori_loop(0, count // tile, body, 0)

    def produce(k, left, right):
        def body(i, carry):
            at = pl.ds(pl.multiple_of(i * (model // 2), tile), model // 2)
            piece = dot(left[at], right).astype(bf16)
            own[k % ring, i] = piece.reshape(own.shape[2:])
            return carry

        lax.fori_loop(0, 2, body, 0)
        remote(own.at[k % ring, :, :, :, 1 - c], near.at[k], cs.at[k], cr.at[k], sibling)

    def first(k):
        taken(near.at[k], cr.at[k])

        def body(i, carry):
            for j in range(4):
                at = (k, i, j // 2, j % 2)
                near[at] = near[at] + own[k % ring, i, j // 2, j % 2, c]
            return carry

        lax.fori_loop(0, 2, body, 0)
        remote(near.at[k, :, :, 1 - x], far.at[k], xs.at[k], xr.at[k], across)

    def second(k):
        taken(far.at[k], xr.at[k])

        def body(i, carry):
            for j in range(2):
                near[k, i, j, x] = near[k, i, j, x] + far[k, i, j]
            return carry

        lax.fori_loop(0, 2, body, 0)
        remote(near.at[k, :, 1 - lo, x], one.at[k], zs.at[k], zr.at[k], beside)

    def half(k):
        taken(one.at[k], zr.at[k])
        for i in range(2):
            near[k, i, lo, x] = near[k, i, lo, x] + one[k, i]
        remote(near.at[k, 1 - hi, lo, x], two.at[k], ws.at[k], wr.at[k], beyond)

    def third(k):
        taken(two.at[k], wr.at[k])
        total = near[k, hi, lo, x].astype(f32) + two[k].astype(f32)
        if k < per:
            ge_ref[:, k * width : (k + 1) * width] = total
        elif k < 2 * per:
            gc_ref[:, (k - per) * width : (k - per + 1) * width] = total
        elif k == 2 * per:
            go_ref[...] = total
        else:
            ga_ref[k - 2 * per - 1] = total

    own_n2.wait()
    turned(t1, b1, 0, rows)
    pl.semaphore_signal(free, 1, device_id=partner, device_id_type=MESH)

    def expand_chunk(k, carry):
        taken(stream.at[k % 2], ld.at[2 + k % 2])

        @pl.when(k >= ring)
        def _():
            taken(near.at[k - ring], cs.at[k - ring])

        produce(k, t1, stream[k % 2])

        @pl.when(k + 2 < per)
        def _():
            local(pre_in.at[:, columns(k + 2)], stream.at[k % 2], ld.at[2 + k % 2])

        @pl.when(k + 2 >= per)
        def _():
            local(act_in.at[:, columns(k + 2 - per)], stream.at[k % 2], ld.at[2 + k % 2])

        @pl.when(k > 0)
        def _():
            first(k - 1)

        return carry

    lax.fori_loop(0, per, expand_chunk, 0)
    own_g.wait()
    turned(t2, b2, 0, rows)

    def contract_chunk(k, carry):
        taken(stream.at[k % 2], ld.at[2 + k % 2])
        taken(near.at[k - ring], cs.at[k - ring])
        produce(k, t2, stream[k % 2])

        @pl.when(k + 2 < 2 * per)
        def _():
            local(act_in.at[:, columns(k + 2 - per)], stream.at[k % 2], ld.at[2 + k % 2])

        first(k - 1)
        return carry

    lax.fori_loop(per, 2 * per, contract_chunk, 0)
    o_at = 2 * per
    first(o_at - 1)
    second(0)

    own_res.wait()
    own_dn.wait()
    taken(dnr, yr.at[0])
    pl.semaphore_wait(free, 1)
    routes = [[sibling, partner, diagonal], [beside, beyond, opposite], [across]]

    def pass_on(n, i):
        if i > 0:
            total = part[n, i - 1]
            for r in range(len(routes[i - 1])):
                at = 3 * (i - 1) + r
                taken(got.at[n, at], vr.at[n, at])
                total = total + got[n, at]
            part[n, i] = total
        if i < len(routes):
            for r, there in enumerate(routes[i]):
                at = 3 * i + r
                remote(part.at[n, i], got.at[n, at], vs.at[n, at], vr.at[n, at], there)

    sums = part.at[0, 0]
    sums[...] = jnp.zeros(sums.shape, f32)
    part[1, 0] = jnp.zeros(sums.shape, f32)
    for i in range(esum_ref.shape[1] // model):
        part[1, 0, pl.ds(2 * y + i, 1), :] = esum_ref[:, i * model : (i + 1) * model]
    pass_on(1, 0)

    def second_norm(i, carry):
        at = pl.ds(pl.multiple_of(i * tile, tile), tile)
        grad = dn[at] + dnr[at].astype(f32)
        hat, inverse = normalize(res[at])
        scaled = grad * vec_ref[5:6]
        mean = jnp.mean(scaled, axis=-1, keepdims=True)
        slope = jnp.mean(scaled * hat, axis=-1, keepdims=True)
        out_grad = b2[at].astype(f32)
        result = out_grad + inverse * (scaled - mean - hat * slope)
        low = result.astype(bf16)
        dn[at] = result
        b1[at] = low
        sums[5:6] += jnp.sum(grad * hat, axis=0, keepdims=True)
        sums[6:7] += jnp.sum(grad, axis=0, keepdims=True)
        sums[4:5] += jnp.sum(low.astype(f32), axis=0, keepdims=True)
        sums[7:8] += jnp.sum(out_grad, axis=0, keepdims=True)
        there = pl.ds(pl.multiple_of(slot + i * tile, tile), tile)
        remote(b1.at[at], b1.at[there], ys.at[1 + i], yr.at[1 + i], partner)
        return carry

    lax.fori_loop(0, pieces, second_norm, 0)
    own_n1 = local(n1_in, b2, ld.at[1])
    second(1)
    own_oa.wait()
    own_proj.wait()
    own_far.wait()
    own_att.wait()

    def attended_grad(turn):
        at = slice(turn * slot, (turn + 1) * slot)
        turned(t2, b1, turn * slot, slot)
        low_grad = dot(b1[at], oa[...]).astype(bf16)
        u[rows + turn * slot : rows + (turn + 1) * slot, :width] = low_grad
        product = low_grad.astype(f32) * att[at].astype(f32)
        high = product.astype(bf16)
        low = (product - high.astype(f32)).astype(bf16)
        lane = lax.broadcasted_iota(jnp.int32, (16, width), 1)
        row = lax.broadcasted_iota(jnp.int32, (16, width), 0)
        pick = jnp.where((lane >= row * HD) & (lane < row * HD + HD), 1.0, 0.0).astype(bf16)
        dots[:, at] = dot(pick, high, NT) + dot(pick, low, NT)

    attended_grad(0)
    own_n1.wait()
    turned(t1, b2, 0, rows)
    pass_on(1, 1)

    dqt[...] = jnp.zeros_like(dqt)
    score_factor = HD ** (-0.5) * LOG2E
    scale = HD ** (-0.5)
    near_blocks = rows // block
    count = 2 * near_blocks

    def attend_step(i, carry):
        later = i // count
        j = i % count
        b = (j + near_blocks) % count

        @pl.when(i == count)
        def _():
            for n in range(pieces):
                taken(b1.at[pl.ds(slot + n * tile, tile)], yr.at[1 + n])
            attended_grad(1)
            taken(near.at[o_at - ring], cs.at[o_at - ring])
            produce(o_at, t2, att[...])

        at = pl.ds(pl.multiple_of(b * block, block), block)
        far_at = pl.ds(pl.multiple_of(j % near_blocks * block, block), block)
        asked = pl.ds(pl.multiple_of(later * slot, tile), slot)
        asked_grad = pl.ds(pl.multiple_of(rows + later * slot, tile), slot)

        @pl.when(later == 0)
        def _():
            acc[...] = jnp.zeros_like(acc)

        @pl.when((later == 1) & (j < near_blocks))
        def _():
            acc[:, :width] = stream[0, far_at].astype(f32)
            acc[:, width:] = stream[1, far_at].astype(f32)

        @pl.when((later == 1) & (j >= near_blocks))
        def _():
            acc[...] = gproj[far_at, width:].astype(f32)

        keyt[...] = u[at, width : 2 * width].T
        bias = jnp.broadcast_to(bias_ref[0:1, at], (tile, block)).T[:, 0:1]
        for head in range(heads):
            start, stop, mask = head_window(head)
            zero = jnp.zeros((), bf16)
            query = jnp.where(mask, u[asked, start:stop], zero)
            grad = jnp.where(mask, u[asked_grad, start:stop], zero)
            scores = dot(u[at, width + start : width + stop], query, NT) * score_factor + bias
            probs = jnp.exp2(scores - lse_ref[head : head + 1, asked])
            grad_probs = dot(u[at, 2 * width + start : 2 * width + stop], grad, NT)
            grad_scores = (probs * (grad_probs - dots[head : head + 1, asked])).astype(bf16)
            acc[:, start:stop] += dot(grad_scores, query)
            acc[:, width + start : width + stop] += dot(probs.astype(bf16), grad)
            lines = slice(head * HD, head * HD + HD)
            dqt[lines, asked] += dot(keyt[lines, :], grad_scores)

        @pl.when((later == 0) & (j < near_blocks))
        def _():
            stream[0, far_at] = acc[:, :width].astype(bf16)
            stream[1, far_at] = acc[:, width:].astype(bf16)

        @pl.when((later == 0) & (j >= near_blocks))
        def _():
            gproj[far_at, width:] = acc[...].astype(bf16)

        @pl.when((later == 1) & (j < near_blocks))
        def _():
            stream[0, far_at] = (acc[:, :width] * scale).astype(bf16)
            stream[1, far_at] = acc[:, width:].astype(bf16)
            remote(stream.at[:, far_at], drecv.at[:, far_at], fs.at[j % near_blocks], fr.at[j % near_blocks], sibling)

        @pl.when((later == 1) & (j >= near_blocks))
        def _():
            taken(drecv.at[:, far_at], fr.at[j % near_blocks])
            key = acc[:, :width] * scale + drecv[0, far_at].astype(f32)
            gproj[far_at, width : 2 * width] = key.astype(bf16)
            value = acc[:, width:] + drecv[1, far_at].astype(f32)
            gproj[far_at, 2 * width :] = value.astype(bf16)

        @pl.when(i == 2)
        def _():
            second(2)
            half(0)

        @pl.when(i == 4)
        def _():
            second(3)
            half(1)

        @pl.when(i == 6)
        def _():
            first(o_at)
            second(4)
            half(2)
            third(0)

        @pl.when(i == 8)
        def _():
            second(5)
            half(3)
            third(1)

        @pl.when(i == 10)
        def _():
            second(6)
            half(4)
            third(2)

        return carry

    lax.fori_loop(0, 2 * count, attend_step, 0)
    own_x = local(x_in, b1.at[pl.ds(slot, slot)], ld.at[10])
    own_inner = local(inner_in, u.at[pl.ds(0, model)], ld.at[8])
    gproj[:, :width] = (dqt[...].T * scale).astype(bf16)

    def project_chunk(j):
        k = o_at + 1 + j
        taken(near.at[k - ring], cs.at[k - ring])
        produce(k, t1, gproj[:, j * width : (j + 1) * width])

    for i in range(pieces):
        taken(b1.at[pl.ds(i * tile, tile)], ys.at[1 + i])
    own_inner.wait()
    split = model // 2
    for n in range(2):
        at = slice(n * split, (n + 1) * split)
        b1[:slot, at] = dot(gproj[slot:], u[at], NT).astype(bf16)
        at = pl.ds(n * split, split)
        remote(b1.at[pl.ds(0, slot), at], dnr.at[:, at], ys.at[1 + pieces + n], yr.at[1 + pieces + n], partner)
    project_chunk(0)
    project_chunk(1)
    first(o_at + 1)
    project_chunk(2)
    first(o_at + 2)
    second(7)
    half(5)
    third(3)
    first(o_at + 3)
    half(6)
    third(4)
    second(8)
    half(7)
    third(5)
    for n in range(2):
        at = slice(n * split, (n + 1) * split)
        res[:, at] = dot(gproj[:slot], u[at], NT)
    totals = dot(jnp.ones((8, rows), bf16), gproj[...])
    sums[2:3, columns(y)] = totals[0:1, :width]
    sums[3:4, columns(y)] = totals[0:1, 2 * width :]
    half(8)
    third(6)
    second(9)
    third(7)
    own_x.wait()
    for n in range(2):
        taken(dnr.at[:, pl.ds(n * split, split)], yr.at[1 + pieces + n])

    def first_norm(i, carry):
        at = pl.ds(pl.multiple_of(i * tile, tile), tile)
        grad = res[at] + dnr[at].astype(f32)
        there = pl.ds(pl.multiple_of(slot + i * tile, tile), tile)
        hat, inverse = normalize(b1[there].astype(f32))
        scaled = grad * vec_ref[0:1]
        mean = jnp.mean(scaled, axis=-1, keepdims=True)
        slope = jnp.mean(scaled * hat, axis=-1, keepdims=True)
        result = dn[at] + inverse * (scaled - mean - hat * slope)
        flat[at] = result.reshape(tile, 1, model)
        sums[0:1] += jnp.sum(grad * hat, axis=0, keepdims=True)
        sums[1:2] += jnp.sum(grad, axis=0, keepdims=True)
        return carry

    lax.fori_loop(0, pieces, first_norm, 0)
    write = local(flat.at[pl.ds(0, hg_out.shape[0])], hg_out, ld.at[5])

    pass_on(0, 0)
    half(9)
    third(8)
    second(10)
    third(9)
    pass_on(0, 1)
    pass_on(1, 2)
    half(10)
    pass_on(0, 2)
    third(10)
    owner = f * 2 + c

    def owned(total, span, lanes, start):
        high = total.astype(bf16)
        low = (total - high.astype(f32)).astype(bf16)
        row = lax.broadcasted_iota(jnp.int32, (model, lanes), 0)
        lane = lax.broadcasted_iota(jnp.int32, (model, lanes), 1)
        pick = jnp.where((row == lane + start) & (lane < span), 1.0, 0.0).astype(bf16)
        return dot(high, pick) + dot(low, pick)

    each = model // 16
    second(11)
    pass_on(1, 3)
    rows_of = owned(part[1, 3], 4 * each, esum_out.shape[1], owner % 4 * 4 * each)
    which = lax.broadcasted_iota(jnp.int32, rows_of.shape, 0)
    esum_out[...] = jnp.sum(jnp.where(which == owner // 4, rows_of, 0.0), axis=0, keepdims=True)
    half(11)
    pass_on(0, 3)
    sum_ref[...] = owned(part[0, 3], each, sum_ref.shape[1], owner * each)
    third(11)
    for n in range(2):
        for i in range(len(routes)):
            for r in range(len(routes[i])):
                taken(part.at[n, i], vs.at[n, 3 * i + r])
    write.wait()
    taken(dnr, ys.at[0])
    for n in range(2):
        taken(dnr.at[:, pl.ds(n * split, split)], ys.at[1 + pieces + n])
    for i in range(near_blocks):
        piece = pl.ds(i * block, block)
        taken(stream.at[:, piece], fs.at[i])
    for k in range(near.shape[0]):
        if k + ring >= near.shape[0]:
            taken(near.at[k], cs.at[k])
        taken(far.at[k], xs.at[k])
        taken(one.at[k], zs.at[k])
        taken(two.at[k], ws.at[k])


def backward(act, pre, n2, g, dn, dno, res, proj, far, att, n1, inner, outer, x_own, lse, bias, vectors, esum, share):
    rows, model = n2.shape
    slot = rows // 2
    width = att.shape[1]
    hidden = act.shape[1]
    owned = model // 16
    block = 256
    chunks = 2 * hidden // width + 4
    ring = 2
    sem = pltpu.SemaphoreType.DMA
    out = jax.ShapeDtypeStruct
    return pl.pallas_call(
        backward_kernel,
        in_specs=[HBM] * 14 + [VMEM] * 4,
        out_specs=(HBM,) + (VMEM,) * 6,
        out_shape=(
            out((share, 1, model), f32),
            out((owned, hidden), f32),
            out((owned, hidden), f32),
            out((owned, width), f32),
            out((3, owned, width), f32),
            out((8, 128), f32),
            out((1, 384), f32),
        ),
        scratch_shapes=[
            pltpu.VMEM((2 * rows, 3 * width), bf16),
            pltpu.VMEM((rows, width), bf16),
            pltpu.VMEM((width, rows), f32),
            pltpu.VMEM((width, block), bf16),
            pltpu.VMEM((16, rows), f32),
            pltpu.VMEM((block, 2 * width), f32),
            pltpu.VMEM((2, rows, width), bf16),
            pltpu.VMEM((model, width), bf16),
            pltpu.VMEM((rows, model), bf16),
            pltpu.VMEM((rows, model), bf16),
            pltpu.VMEM((model, rows), bf16),
            pltpu.VMEM((model, rows), bf16),
            pltpu.VMEM((slot, model), f32),
            pltpu.VMEM((slot, model), f32),
            pltpu.VMEM((slot, model), bf16),
            pltpu.VMEM((2, rows, width), bf16),
            pltpu.VMEM((rows, 3 * width), bf16),
            pltpu.VMEM((ring, 2, 2, 2, 2, owned, width), bf16),
            pltpu.VMEM((chunks, 2, 2, 2, owned, width), bf16),
            pltpu.VMEM((chunks, 2, 2, owned, width), bf16),
            pltpu.VMEM((chunks, 2, owned, width), bf16),
            pltpu.VMEM((chunks, owned, width), bf16),
            pltpu.VMEM((slot, 1, model), f32),
            pltpu.VMEM((2, 4, 8, model), f32),
            pltpu.VMEM((2, 7, 8, model), f32),
            sem((11,)),
            sem((chunks,)),
            sem((chunks,)),
            sem((chunks,)),
            sem((chunks,)),
            sem((chunks,)),
            sem((chunks,)),
            sem((chunks,)),
            sem((chunks,)),
            sem((3 + slot // 128,)),
            sem((3 + slot // 128,)),
            sem((rows // block,)),
            sem((rows // block,)),
            sem((2, 7)),
            sem((2, 7)),
            pltpu.SemaphoreType.REGULAR,
        ],
        compiler_params=params(collective_id=4, has_side_effects=True),
    )(act, pre, n2, g, dn, dno, res, proj, far, att, n1, inner, outer, x_own, lse, bias, vectors, esum)


def key_biases(share, slot, length, tp_rank, ctx_rank):
    places = lax.iota(jnp.int32, slot)
    pieces = []
    for ctx in (ctx_rank, 1 - ctx_rank):
        for tp in (tp_rank, 1 - tp_rank):
            start = (ctx * 2 + tp) * share
            valid = (places < share) & (start + places < length)
            pieces.append(jnp.where(valid, 0.0, masked_score).astype(f32))
    return jnp.concatenate(pieces)


def forward_parts(x_own, grad_own, smalls, inner, outer_t, expand_weight, contract_t, bias):
    slot, model = x_own.shape
    rows_each = inner.shape[0]
    half_each = rows_each // 2
    width, hidden = outer_t.shape[1], expand_weight.shape[1]
    heads = width // HD
    tp_rank = lax.axis_index("tp")
    ctx_rank = lax.axis_index("ctx")
    x_all = jnp.concatenate([x_own, swap(x_own, "tp")], axis=0)
    grad_all = jnp.concatenate([grad_own, swap(grad_own, "tp")], axis=0)
    inner = lax.all_gather(inner, "fsdp", axis=0, tiled=True)
    smalls_all = lax.all_gather(smalls, "fsdp", axis=0)
    late = jnp.concatenate([outer_t, swap(outer_t, "tp"), expand_weight, contract_t], axis=1)
    late = lax.dynamic_slice_in_dim(late, ctx_rank * half_each, half_each, 0)
    late = lax.all_gather(late, ("fsdp", "ctx"), axis=0, tiled=True)
    expand_at = 2 * width
    contract_at = 2 * width + hidden
    smalls_all = smalls_all[:, :, :rows_each].astype(f32)
    vectors = jnp.transpose(smalls_all[:, :8], (1, 0, 2)).reshape(8, model)
    expand_rows = smalls_all[:, 8 : 8 + hidden * 2 // model].reshape(1, 2 * hidden)
    expand_local = lax.dynamic_slice_in_dim(expand_rows, tp_rank * hidden, hidden, 1)
    pair = lax.dynamic_slice_in_dim(vectors[2:4], tp_rank * width, width, 1)
    triple = jnp.concatenate([pair[0:1], jnp.zeros((1, width), f32), pair[1:2]], axis=1)
    normed_one, proj = project(x_all, vectors[0:1], vectors[1:2], inner, triple)
    far = swap(proj[:, width:], "ctx")
    attended, lse = attend(proj, far, jnp.broadcast_to(bias[None], (8, bias.shape[0])), heads)
    attended_oth = swap(attended, "tp")
    residual, normed_two = residual_step(x_all, attended, attended_oth, late, width, vectors[4:7])
    activated, pre_grad, expand_sum, normed_own, normed_oth = hidden_step(
        normed_two, grad_all, late, expand_at, contract_at, hidden, expand_local
    )
    contracted = dot(activated, late[:, contract_at:], NT)
    return (
        inner, late[:, :width], normed_one, proj, far, attended, lse, residual[:slot], normed_two,
        grad_all, activated, pre_grad, expand_sum, normed_own, normed_oth, contracted[:slot],
        contracted[slot:].astype(bf16), vectors,
    )


def per_device(
    hidden_in,
    valid_lengths,
    output_grad,
    first_gain,
    first_shift,
    attention_in,
    query_value_bias,
    attention_out,
    attention_bias,
    second_gain,
    second_shift,
    expand_weight,
    expand_bias,
    contract_weight,
    contract_bias,
):
    _, share, model = hidden_in.shape
    tp_rank = lax.axis_index("tp")
    ctx_rank = lax.axis_index("ctx")
    fsdp_count = lax.axis_size("fsdp")
    rows_each = attention_in.shape[0]
    width = attention_in.shape[2]
    heads = width // HD
    hidden = expand_weight.shape[1]
    slot = -(-share // 128) * 128
    length = valid_lengths[0]

    def padded(value):
        return jnp.pad(value, ((0, slot - share), (0, 0)))

    own_start = (ctx_rank * 2 + tp_rank) * share
    token_valid = (own_start + lax.iota(jnp.int32, share)) < length
    grad_own = jnp.where(token_valid[:, None], output_grad[0], jnp.zeros((), bf16))
    grad_own = padded(grad_own)
    x_own = padded(hidden_in[0])

    small_list = [
        first_gain,
        first_shift,
        query_value_bias,
        attention_bias,
        second_gain,
        second_shift,
        contract_bias,
        expand_bias,
    ]
    smalls, row = None, 0
    for small in small_list:
        small = small.reshape(-1, rows_each)
        below = 16 - row - small.shape[0]
        small = jnp.pad(small, ((row, below), (0, -rows_each % 128)))
        smalls = small if smalls is None else smalls + small
        row = 16 - below
    bias = key_biases(share, slot, length, tp_rank, ctx_rank)
    inner = attention_in.reshape(rows_each, 3 * width)
    outer_t, contract_t = attention_out.T, contract_weight.T
    bias_rows = jnp.broadcast_to(bias[None], (8, bias.shape[0]))
    if fsdp_count == 8 and rows_each == 160 and 2 * hidden == 8 * width:
        (
            inner, outer_t, normed_one, proj, far, attended, lse, residual, normed_two, grad_all,
            activated, pre_grad, expand_sum, normed_own, normed_oth, out_own, out_oth, vectors,
        ) = forward(
            x_own, grad_own, smalls, inner, outer_t, expand_weight, contract_t, bias_rows,
        )
        hidden_grad, grad_expand, grad_contract, grad_outer, grad_inner, summed, expand_summed = backward(
            activated, pre_grad, normed_two, grad_all, normed_own, normed_oth, residual, proj, far,
            attended, normed_one, inner.reshape(model, 3 * width), outer_t.reshape(model, width), x_own, lse,
            bias_rows, vectors, expand_sum, share,
        )
        contracted = out_own + swap(out_oth, "tp").astype(f32)
        hidden_out = (residual + (contracted + vectors[7:8])).astype(bf16)
        summed = summed[:, : model // (2 * fsdp_count)]
        hidden_grad = hidden_grad.reshape(share, model)
        grad_contract, grad_outer = grad_contract.T, grad_outer.T
        grad_inner = jnp.transpose(grad_inner, (1, 0, 2))
        expand_summed = expand_summed[0, : 2 * hidden // (2 * fsdp_count)]
    else:
        (
            inner, outer_t, normed_one, proj, far, attended, lse, residual, normed_two, grad_all,
            activated, pre_grad, expand_sum, normed_own, normed_oth, out_own, out_oth, vectors,
        ) = forward_parts(
            x_own, grad_own, smalls, inner, outer_t, expand_weight, contract_t, bias
        )
        normed_oth = swap(normed_oth, "tp")
        grad_contract_t = dot(grad_all, activated, TN).astype(bf16)
        grad_expand = dot(normed_two, pre_grad, TN).astype(bf16)
        normed_own, normed_oth, grad_late = lax.optimization_barrier(
            (normed_own, normed_oth, jnp.concatenate([grad_expand, grad_contract_t], axis=1))
        )
        grad_late = lax.psum_scatter(
            grad_late, ("fsdp", "ctx"), scatter_dimension=0, tiled=True
        ).astype(f32)
        contracted = out_own + swap(out_oth, "tp").astype(f32)
        hidden_out = (residual + (contracted + vectors[7:8])).astype(bf16)

        residual_grad, residual_low, sums_two = norm_back(
            normed_own, normed_oth, residual, grad_own, vectors[5:6], True
        )
        residual_low_all = jnp.concatenate([residual_low, swap(residual_low, "tp")], axis=0)
        attended_grad = dot(residual_low_all, outer_t).astype(bf16)
        grad_outer_t = dot(residual_low_all, attended, TN).astype(bf16)

        grad_query, grad_near, grad_far = attend_back(
            proj, far, jnp.broadcast_to(bias[:, None], (bias.shape[0], 128)), attended, attended_grad, lse, heads
        )
        grad_near = (grad_near + swap(grad_far, "ctx").astype(f32)).astype(bf16)
        grad_proj = jnp.concatenate([grad_query, grad_near], axis=1)
        normed_grad = dot(grad_proj, inner, NT)
        normed_grad_oth = swap(normed_grad[slot:].astype(bf16), "tp")
        grad_inner = dot(normed_one, grad_proj, TN).astype(bf16)
        proj_sums = jnp.sum(grad_proj.astype(f32), axis=0)
        grad_inner, grad_outer_t = scatter_sums([grad_inner, grad_outer_t], 384, fsdp_count)
        hidden_grad, sums_one = norm_back(
            normed_grad[:slot], normed_grad_oth, x_own, residual_grad, vectors[0:1], False
        )
        grad_sum = jnp.sum(grad_own.astype(f32), axis=0)

        def placed(value, total):
            zero = jnp.zeros((total,), f32)
            return lax.dynamic_update_slice_in_dim(zero, value, tp_rank * value.shape[0], 0)

        owned = model // (fsdp_count * 2)
        stacked = jnp.stack(
            [
                sums_one[0],
                sums_one[1],
                placed(proj_sums[:width], model),
                placed(proj_sums[2 * width :], model),
                sums_two[2],
                sums_two[0],
                sums_two[1],
                grad_sum,
            ]
        )
        stacked = jnp.transpose(stacked.reshape(8, -1, owned), (1, 0, 2))
        expand_piece = placed(expand_sum[0], 2 * hidden).reshape(fsdp_count * 2, -1, owned)
        stacked = jnp.concatenate([stacked, expand_piece], axis=1)
        stacked = jnp.pad(stacked, ((0, 0), (0, 16 - stacked.shape[1]), (0, 128 - owned)))
        summed = sum_vectors(stacked, fsdp_count)[:, :owned]
        grad_outer = grad_outer_t.T
        grad_expand, grad_contract = grad_late[:, :hidden], grad_late[:, hidden:].T
        expand_summed = summed[8 : 8 + 2 * hidden // model].reshape(-1)

    return (
        hidden_out[None, :share],
        hidden_grad[None, :share],
        summed[0],
        summed[1],
        grad_inner.reshape(-1, 3, width),
        summed[2:4],
        grad_outer,
        summed[4],
        summed[5],
        summed[6],
        grad_expand,
        expand_summed,
        grad_contract,
        summed[7],
    )


def solution(mesh):
    return jax.shard_map(
        per_device,
        mesh=mesh,
        in_specs=(
            P("fsdp", ("ctx", "tp"), None),
            P("fsdp"),
            P("fsdp", ("ctx", "tp"), None),
            P("fsdp"),
            P("fsdp"),
            P("fsdp", None, "tp"),
            P(None, "fsdp"),
            P("tp", "fsdp"),
            P("fsdp"),
            P("fsdp"),
            P("fsdp"),
            P("fsdp", "tp"),
            P("fsdp"),
            P("tp", "fsdp"),
            P("fsdp"),
        ),
        out_specs=(
            P("fsdp", ("ctx", "tp"), None),
            P("fsdp", ("ctx", "tp"), None),
            P(("fsdp", "ctx")),
            P(("fsdp", "ctx")),
            P(("fsdp", "ctx"), None, "tp"),
            P(None, ("fsdp", "ctx")),
            P("tp", ("fsdp", "ctx")),
            P(("fsdp", "ctx")),
            P(("fsdp", "ctx")),
            P(("fsdp", "ctx")),
            P(("fsdp", "ctx"), "tp"),
            P(("fsdp", "ctx")),
            P("tp", ("fsdp", "ctx")),
            P(("fsdp", "ctx")),
        ),
        check_vma=False,
    )
```

```python
import functools

import jax
import jax.numpy as jnp
from jax import lax
from jax.experimental import pallas as pl
from jax.experimental.pallas import tpu as pltpu
from jax.sharding import PartitionSpec as P

HD = 80
epsilon = 1e-05
masked_score = -1e30
LOG2E = 1.4426950408889634
f32 = jnp.float32
bf16 = jnp.bfloat16
MESH = pl.DeviceIdType.MESH
VMEM = pl.BlockSpec(memory_space=pltpu.VMEM)
HBM = pl.BlockSpec(memory_space=pltpu.HBM)
VMEM_LIMIT = 62 * 1024 * 1024


def params(**kw):
    return pltpu.CompilerParams(vmem_limit_bytes=VMEM_LIMIT, **kw)


def dot(a, b, dims=((1,), (0,))):
    return lax.dot_general(a, b, (dims, ((), ())), preferred_element_type=f32)


NT = ((1,), (1,))
TN = ((0,), (0,))


def swap(value, axis):
    return lax.ppermute(value, axis, [(0, 1), (1, 0)])


def vector_kernel(v_ref, o_ref, got, lsem, ss, sr):
    f = lax.axis_index("fsdp")
    c = lax.axis_index("ctx")
    y = lax.axis_index("tp")
    me = (f * 2 + c) * 2 + y
    bar = pltpu.get_barrier_semaphore()

    def device(i):
        return (i // 4, (i // 2) % 2, i % 2)

    peers = [(me + d) % 32 for d in range(1, 32)]
    for p in peers:
        pl.semaphore_signal(bar, 1, device_id=device(p), device_id_type=MESH)
    pl.semaphore_wait(bar, 31)
    sent = []
    for d, p in enumerate(peers):
        copy = pltpu.make_async_remote_copy(
            src_ref=v_ref.at[p // 2],
            dst_ref=got.at[d + 1],
            send_sem=ss.at[d],
            recv_sem=sr.at[d],
            device_id=device(p),
            device_id_type=MESH,
        )
        copy.start()
        sent.append(copy)
    local = pltpu.make_async_copy(v_ref.at[me // 2], got.at[0], lsem)
    local.start()
    local.wait()
    total = got[0].astype(f32)
    for d in range(31):
        sent[d].wait_recv()
    for d in range(31):
        total = total + got[d + 1].astype(f32)
    o_ref[...] = total
    for copy in sent:
        copy.wait_send()


def sum_vectors(vectors, fsdp_count):
    if fsdp_count == 8:
        sem = pltpu.SemaphoreType.DMA
        return pl.pallas_call(
            vector_kernel,
            out_shape=jax.ShapeDtypeStruct(vectors.shape[1:], f32),
            in_specs=[VMEM],
            out_specs=VMEM,
            scratch_shapes=[
                pltpu.VMEM((32,) + vectors.shape[1:], bf16),
                sem,
                sem((31,)),
                sem((31,)),
            ],
            compiler_params=params(collective_id=2, has_side_effects=True),
        )(vectors.astype(bf16))
    partial = lax.psum(vectors, "tp")
    return lax.psum_scatter(partial, ("fsdp", "ctx"), scatter_dimension=0, tiled=False)


def scatter_kernel(spans, arrays, *refs):
    ins = refs[:arrays]
    outs = refs[arrays : 2 * arrays]
    own, near, mine, far, pair, last, lsem, cs, cr, xs, xr, zs, zr = refs[2 * arrays :]
    f = lax.axis_index("fsdp")
    c = lax.axis_index("ctx")
    y = lax.axis_index("tp")
    z, x = f // 2, f % 2
    bar = pltpu.get_barrier_semaphore()
    sibling = (f, 1 - c, y)
    across = (z * 2 + (1 - x), c, y)
    column = [None] + [(((z + d) % 4) * 2 + x, c, y) for d in (1, 2, 3)]
    for p in [sibling, across] + column[1:]:
        pl.semaphore_signal(bar, 1, device_id=p, device_id_type=MESH)
    pl.semaphore_wait(bar, 5)

    def remote(src, dst, s, r, dev):
        copy = pltpu.make_async_remote_copy(
            src_ref=src, dst_ref=dst, send_sem=s, recv_sem=r, device_id=dev, device_id_type=MESH
        )
        copy.start()
        return copy

    local, over_ctx, over_x, over_z = {}, {}, {}, {}
    for k, (a, start, width) in enumerate(spans):
        cols = pl.ds(start, width)
        fit = pl.ds(0, width)
        copy = pltpu.make_async_copy(ins[a].at[:, c, :, cols], own.at[k, :, :, fit], lsem.at[k])
        copy.start()
        local[k] = copy
        over_ctx[k] = remote(
            ins[a].at[:, 1 - c, :, cols], near.at[k, :, :, fit], cs.at[k], cr.at[k], sibling
        )

    def first(k):
        width = spans[k][2]
        local[k].wait()
        over_ctx[k].wait_recv()
        for i in range(8):
            total = own[k, i, :, :width].astype(f32) + near[k, i, :, :width].astype(f32)
            mine[k, i // 2, i % 2, :, :width] = total.astype(bf16)
        src = mine.at[k, :, 1 - x, :, pl.ds(0, width)]
        over_x[k] = remote(src, far.at[k, :, :, pl.ds(0, width)], xs.at[k], xr.at[k], across)

    def second(k):
        width = spans[k][2]
        over_x[k].wait_recv()
        for i in range(4):
            total = mine[k, i, x, :, :width].astype(f32) + far[k, i, :, :width].astype(f32)
            pair[k, i, :, :width] = total.astype(bf16)
        over_z[k] = [
            remote(
                pair.at[k, (z + d) % 4, :, pl.ds(0, width)],
                last.at[k, d - 1, :, pl.ds(0, width)],
                zs.at[k, d - 1],
                zr.at[k, d - 1],
                column[d],
            )
            for d in (1, 2, 3)
        ]

    def third(k):
        a, start, width = spans[k]
        total = pair[k, z, :, :width].astype(f32)
        for d in range(3):
            over_z[k][d].wait_recv()
            total = total + last[k, d, :, :width].astype(f32)
        outs[a][:, start : start + width] = total

    count = len(spans)
    for step in range(count + 2):
        if step < count:
            first(step)
        if 0 <= step - 1 < count:
            second(step - 1)
        if 0 <= step - 2 < count:
            third(step - 2)
    for k in range(count):
        over_ctx[k].wait_send()
        over_x[k].wait_send()
        for copy in over_z[k]:
            copy.wait_send()


def scatter_sums(grads, widest, fsdp_count):
    rows = grads[0].shape[0]
    owned = rows // (fsdp_count * 2)
    if fsdp_count == 8 and owned % 16 == 0:
        spans = []
        for a, grad in enumerate(grads):
            for start in range(0, grad.shape[1], widest):
                spans.append((a, start, min(widest, grad.shape[1] - start)))
        count = len(spans)
        sem = pltpu.SemaphoreType.DMA
        return pl.pallas_call(
            functools.partial(scatter_kernel, spans, len(grads)),
            in_specs=[HBM] * len(grads),
            out_specs=tuple([VMEM] * len(grads)),
            out_shape=tuple(jax.ShapeDtypeStruct((owned, g.shape[1]), f32) for g in grads),
            scratch_shapes=[
                pltpu.VMEM((count, 8, owned, widest), bf16),
                pltpu.VMEM((count, 8, owned, widest), bf16),
                pltpu.VMEM((count, 4, 2, owned, widest), bf16),
                pltpu.VMEM((count, 4, owned, widest), bf16),
                pltpu.VMEM((count, 4, owned, widest), bf16),
                pltpu.VMEM((count, 3, owned, widest), bf16),
            ]
            + [sem((count,))] * 5
            + [sem((count, 3))] * 2,
            compiler_params=params(collective_id=3, has_side_effects=True),
        )(*[g.reshape(8, 2, owned, g.shape[1]) for g in grads])
    whole = lax.psum_scatter(
        jnp.concatenate(grads, axis=1), ("fsdp", "ctx"), scatter_dimension=0, tiled=True
    ).astype(f32)
    edges = [sum(g.shape[1] for g in grads[:i]) for i in range(len(grads) + 1)]
    return [whole[:, a:b] for a, b in zip(edges, edges[1:])]


def normalize(values):
    centered = values - jnp.mean(values, axis=-1, keepdims=True)
    inverse = lax.rsqrt(jnp.mean(centered * centered, axis=-1, keepdims=True) + epsilon)
    return centered * inverse, inverse


def project_kernel(x_ref, gain_ref, shift_ref, w_ref, b_ref, n_ref, p_ref):
    values = x_ref[...].astype(f32)
    hat, _ = normalize(values)
    low = (hat * gain_ref[...] + shift_ref[...]).astype(bf16)
    n_ref[...] = low
    p_ref[...] = (dot(low, w_ref[...]) + b_ref[...]).astype(bf16)


def project(x_all, gain, shift, weight, bias):
    rows, model = x_all.shape
    width = weight.shape[1]
    block = 256
    fixed = lambda i: (0, 0)
    return pl.pallas_call(
        project_kernel,
        grid=(rows // block,),
        in_specs=[
            pl.BlockSpec((block, model), lambda i: (i, 0)),
            pl.BlockSpec((1, model), fixed),
            pl.BlockSpec((1, model), fixed),
            pl.BlockSpec((model, width), fixed),
            pl.BlockSpec((1, width), fixed),
        ],
        out_specs=(
            pl.BlockSpec((block, model), lambda i: (i, 0)),
            pl.BlockSpec((block, width), lambda i: (i, 0)),
        ),
        out_shape=(
            jax.ShapeDtypeStruct((rows, model), bf16),
            jax.ShapeDtypeStruct((rows, width), bf16),
        ),
        compiler_params=params(),
        cost_estimate=pl.CostEstimate(
            flops=2 * rows * model * width, bytes_accessed=12 << 20, transcendentals=0
        ),
    )(x_all, gain, shift, weight, bias)


def head_window(head):
    start = head * HD // 128 * 128
    stop = -(-(head * HD + HD) // 128) * 128
    lanes = lax.broadcasted_iota(jnp.int32, (1, stop - start), 1) + start
    return start, stop, (lanes >= head * HD) & (lanes < head * HD + HD)


def attend_kernel(heads, proj_ref, far_ref, bias_ref, att_ref, lse_ref, acc_ref, stat_ref):
    rows = proj_ref.shape[0]
    width = heads * HD
    block = 256
    acc_ref[...] = jnp.zeros_like(acc_ref)
    stat_ref[...] = jnp.zeros_like(stat_ref)
    score_factor = HD ** (-0.5) * LOG2E

    def step(i, carry):
        at = pl.ds(pl.multiple_of(i * block, block), block)
        for head in range(heads):
            start, stop, mask = head_window(head)
            query = jnp.where(mask, proj_ref[at, start:stop], jnp.zeros((), bf16))
            near = dot(query, proj_ref[:, width + start : width + stop], NT)
            far = dot(query, far_ref[:, start:stop], NT)
            near = near * score_factor + bias_ref[0:1, :rows]
            far = far * score_factor + bias_ref[0:1, rows:]
            top = jnp.maximum(
                jnp.max(near, axis=-1, keepdims=True), jnp.max(far, axis=-1, keepdims=True)
            )
            near = jnp.exp2(near - top)
            far = jnp.exp2(far - top)
            total = jnp.sum(near, axis=-1, keepdims=True) + jnp.sum(far, axis=-1, keepdims=True)
            mixed = dot(near.astype(bf16), proj_ref[:, 2 * width + start : 2 * width + stop])
            mixed = mixed + dot(far.astype(bf16), far_ref[:, width + start : width + stop])
            mixed = mixed * (1.0 / total)
            acc_ref[at, start:stop] += jnp.where(mask, mixed, 0.0)
            lane = lax.broadcasted_iota(jnp.int32, (1, 128), 1)
            stat_ref[at, :] += jnp.where(lane == head, top + jnp.log2(total), 0.0)
        return carry

    lax.fori_loop(0, rows // block, step, 0)
    att_ref[...] = acc_ref[...].astype(bf16)
    lse_ref[...] = stat_ref[...].T


def attend(proj, far, bias, heads):
    rows = proj.shape[0]
    return pl.pallas_call(
        functools.partial(attend_kernel, heads),
        in_specs=[VMEM] * 3,
        out_specs=(VMEM, VMEM),
        out_shape=(
            jax.ShapeDtypeStruct((rows, heads * HD), bf16),
            jax.ShapeDtypeStruct((128, rows), f32),
        ),
        scratch_shapes=[pltpu.VMEM((rows, heads * HD), f32), pltpu.VMEM((rows, 128), f32)],
        compiler_params=params(),
        cost_estimate=pl.CostEstimate(
            flops=4 * heads * rows * 2 * rows * 256, bytes_accessed=8 << 20, transcendentals=0
        ),
    )(proj, far, bias)


def attend_back_kernel(
    heads, proj_ref, far_ref, bias_ref, att_ref, grad_ref, lse_ref,
    dq_ref, dnear_ref, dfar_ref, key_ref, value_ref, keyt_ref, dqt_ref, dot_ref, dkv_ref,
):
    rows = proj_ref.shape[0]
    width = heads * HD
    block = 256
    score_factor = HD ** (-0.5) * LOG2E
    key_ref[:rows] = proj_ref[:, width : 2 * width]
    key_ref[rows:] = far_ref[:, :width]
    value_ref[:rows] = proj_ref[:, 2 * width :]
    value_ref[rows:] = far_ref[:, width:]
    keyt_ref[...] = key_ref[...].T
    dqt_ref[...] = jnp.zeros_like(dqt_ref)
    dkv_ref[...] = jnp.zeros_like(dkv_ref)
    product = grad_ref[...].astype(f32) * att_ref[...].astype(f32)
    high = product.astype(bf16)
    low = (product - high.astype(f32)).astype(bf16)
    lane = lax.broadcasted_iota(jnp.int32, (16, width), 1)
    row = lax.broadcasted_iota(jnp.int32, (16, width), 0)
    pick = jnp.where((lane >= row * HD) & (lane < row * HD + HD), 1.0, 0.0).astype(bf16)
    dot_ref[...] = dot(pick, high, NT) + dot(pick, low, NT)

    def step(i, carry):
        at = pl.ds(pl.multiple_of(i * block, block), block)
        bias = bias_ref[at, 0:1]
        for head in range(heads):
            start, stop, mask = head_window(head)
            zero = jnp.zeros((), bf16)
            query = jnp.where(mask, proj_ref[:, start:stop], zero)
            grad = jnp.where(mask, grad_ref[:, start:stop], zero)
            scores = dot(key_ref[at, start:stop], query, NT) * score_factor + bias
            probs = jnp.exp2(scores - lse_ref[head : head + 1, :])
            grad_probs = dot(value_ref[at, start:stop], grad, NT)
            grad_scores = (probs * (grad_probs - dot_ref[head : head + 1, :])).astype(bf16)
            dkv_ref[at, start:stop] += dot(grad_scores, query)
            dkv_ref[at, width + start : width + stop] += dot(probs.astype(bf16), grad)
            keyt = keyt_ref[head * HD : head * HD + HD, at]
            dqt_ref[head * HD : head * HD + HD, :] += dot(keyt, grad_scores)
        return carry

    lax.fori_loop(0, 2 * rows // block, step, 0)
    scale = HD ** (-0.5)
    dq_ref[...] = (dqt_ref[...].T * scale).astype(bf16)
    dnear_ref[:, :width] = dkv_ref[:rows, :width] * scale
    dnear_ref[:, width:] = dkv_ref[:rows, width:]
    dfar_ref[:, :width] = (dkv_ref[rows:, :width] * scale).astype(bf16)
    dfar_ref[:, width:] = dkv_ref[rows:, width:].astype(bf16)


def attend_back(proj, far, bias, attended, grad, lse, heads):
    rows = proj.shape[0]
    width = heads * HD
    return pl.pallas_call(
        functools.partial(attend_back_kernel, heads),
        in_specs=[VMEM] * 6,
        out_specs=(VMEM, VMEM, VMEM),
        out_shape=(
            jax.ShapeDtypeStruct((rows, width), bf16),
            jax.ShapeDtypeStruct((rows, 2 * width), f32),
            jax.ShapeDtypeStruct((rows, 2 * width), bf16),
        ),
        scratch_shapes=[
            pltpu.VMEM((2 * rows, width), bf16),
            pltpu.VMEM((2 * rows, width), bf16),
            pltpu.VMEM((width, 2 * rows), bf16),
            pltpu.VMEM((width, rows), f32),
            pltpu.VMEM((16, rows), f32),
            pltpu.VMEM((2 * rows, 2 * width), f32),
        ],
        compiler_params=params(),
        cost_estimate=pl.CostEstimate(
            flops=10 * heads * rows * 2 * rows * 256, bytes_accessed=16 << 20, transcendentals=0
        ),
    )(proj, far, bias, attended, grad, lse)


def residual_kernel(x_ref, own_ref, oth_ref, wa_ref, wb_ref, vec_ref, r_ref, n_ref):
    mixed = dot(own_ref[...], wa_ref[...], NT) + dot(oth_ref[...], wb_ref[...], NT)
    residual = x_ref[...].astype(f32) + (mixed + vec_ref[0:1, :])
    r_ref[...] = residual
    hat, _ = normalize(residual)
    n_ref[...] = (hat * vec_ref[1:2, :] + vec_ref[2:3, :]).astype(bf16)


def residual_step(x_all, own, oth, weights, width, vectors):
    rows, model = x_all.shape
    block = 128
    return pl.pallas_call(
        residual_kernel,
        grid=(rows // block,),
        in_specs=[
            pl.BlockSpec((block, model), lambda i: (i, 0)),
            pl.BlockSpec((block, width), lambda i: (i, 0)),
            pl.BlockSpec((block, width), lambda i: ((i + rows // block // 2) % (rows // block), 0)),
            pl.BlockSpec((model, width), lambda i: (0, 0)),
            pl.BlockSpec((model, width), lambda i: (0, 1)),
            pl.BlockSpec(vectors.shape, lambda i: (0, 0)),
        ],
        out_specs=(
            pl.BlockSpec((block, model), lambda i: (i, 0)),
            pl.BlockSpec((block, model), lambda i: (i, 0)),
        ),
        out_shape=(
            jax.ShapeDtypeStruct((rows, model), f32),
            jax.ShapeDtypeStruct((rows, model), bf16),
        ),
        compiler_params=params(),
        cost_estimate=pl.CostEstimate(
            flops=4 * rows * model * width, bytes_accessed=12 << 20, transcendentals=0
        ),
    )(x_all, own, oth, weights, weights, vectors)


def hidden_kernel(blocks, n_ref, g_ref, we_ref, wc_ref, b_ref, act_ref, pre_ref, sum_ref, own_ref, oth_ref, acc_ref):
    k = pl.program_id(0)
    rows = n_ref.shape[0]
    half = rows // 2
    piece = 256

    @pl.when(k == 0)
    def _():
        acc_ref[...] = jnp.zeros_like(acc_ref)

    total = jnp.zeros((1, b_ref.shape[1]), f32)
    for i in range(rows // piece):
        at = slice(i * piece, (i + 1) * piece)
        pre = dot(n_ref[at], we_ref[...]) + b_ref[...]
        back = dot(g_ref[at], wc_ref[...])
        cdf = 0.5 + 0.5 * lax.erf(pre * (0.5**0.5))
        density = jnp.exp(pre * pre * -0.5) * 0.3989422804014327
        act_ref[at] = (pre * cdf).astype(bf16)
        low = (back * (cdf + pre * density)).astype(bf16)
        pre_ref[at] = low
        total = total + jnp.sum(low.astype(f32), axis=0, keepdims=True)
        acc_ref[at] += dot(low, we_ref[...], NT)
    sum_ref[...] = total

    @pl.when(k == blocks - 1)
    def _():
        own_ref[...] = acc_ref[:half]
        oth_ref[...] = acc_ref[half:].astype(bf16)


def hidden_step(normed, grad, weights, expand_at, contract_at, width, bias):
    rows, model = normed.shape
    block = 256
    blocks = width // block
    half = rows // 2
    fixed = lambda k: (0, 0)
    return pl.pallas_call(
        functools.partial(hidden_kernel, blocks),
        grid=(blocks,),
        in_specs=[
            pl.BlockSpec((rows, model), fixed),
            pl.BlockSpec((rows, model), fixed),
            pl.BlockSpec((model, block), lambda k: (0, expand_at // block + k)),
            pl.BlockSpec((model, block), lambda k: (0, contract_at // block + k)),
            pl.BlockSpec((1, block), lambda k: (0, k)),
        ],
        out_specs=(
            pl.BlockSpec((rows, block), lambda k: (0, k)),
            pl.BlockSpec((rows, block), lambda k: (0, k)),
            pl.BlockSpec((1, block), lambda k: (0, k)),
            pl.BlockSpec((half, model), fixed),
            pl.BlockSpec((half, model), fixed),
        ),
        out_shape=(
            jax.ShapeDtypeStruct((rows, width), bf16),
            jax.ShapeDtypeStruct((rows, width), bf16),
            jax.ShapeDtypeStruct((1, width), f32),
            jax.ShapeDtypeStruct((half, model), f32),
            jax.ShapeDtypeStruct((half, model), bf16),
        ),
        scratch_shapes=[pltpu.VMEM((rows, model), f32)],
        compiler_params=params(),
        cost_estimate=pl.CostEstimate(
            flops=6 * rows * model * width, bytes_accessed=28 << 20, transcendentals=0
        ),
    )(normed, grad, weights, weights, bias)


def norm_back_kernel(round_low, own_ref, oth_ref, base_ref, add_ref, gain_ref, *outs):
    i = pl.program_id(0)
    grad = own_ref[...].astype(f32) + oth_ref[...].astype(f32)
    hat, inverse = normalize(base_ref[...].astype(f32))
    scaled = grad * gain_ref[...]
    first = jnp.mean(scaled, axis=-1, keepdims=True)
    second = jnp.mean(scaled * hat, axis=-1, keepdims=True)
    result = add_ref[...].astype(f32) + inverse * (scaled - first - hat * second)
    outs[0][...] = result
    sums = outs[-1]

    @pl.when(i == 0)
    def _():
        sums[...] = jnp.zeros_like(sums)

    sums[0:1] += jnp.sum(grad * hat, axis=0, keepdims=True)
    sums[1:2] += jnp.sum(grad, axis=0, keepdims=True)
    if round_low:
        low = result.astype(bf16)
        outs[1][...] = low
        sums[2:3] += jnp.sum(low.astype(f32), axis=0, keepdims=True)


def norm_back(own, oth, base, add, gain, round_low):
    rows, model = own.shape
    block = 128
    spec = pl.BlockSpec((block, model), lambda i: (i, 0))
    outs = [jax.ShapeDtypeStruct((rows, model), f32)]
    if round_low:
        outs.append(jax.ShapeDtypeStruct((rows, model), bf16))
    outs.append(jax.ShapeDtypeStruct((8, model), f32))
    return pl.pallas_call(
        functools.partial(norm_back_kernel, round_low),
        grid=(rows // block,),
        in_specs=[spec] * 4 + [pl.BlockSpec((1, model), lambda i: (0, 0))],
        out_specs=tuple([spec] * (len(outs) - 1) + [pl.BlockSpec((8, model), lambda i: (0, 0))]),
        out_shape=tuple(outs),
        compiler_params=params(),
    )(own, oth, base, add, gain)


def forward_kernel(
    x_in, g_in, s_in, wa, wo, we, wc, bias_ref,
    inner_out, outer_out, n1_out, proj_out, far_out, att_out, lse_ref, res_out, n2_out, g_out,
    act_out, pre_out, esum_ref, dn_own, dn_oth, ho_own, ho_oth, vec_ref,
    so, ina, oa, ob, la, xb, gb, n1, proj, far, tb, eb, acc, stat, att, atto, res, n2, stage, dn, ho,
    ld, ss, sr, zs, zr, bs, br, xs, xr, cs, cr, ys, yr, fs, fr, outs,
):
    f = lax.axis_index("fsdp")
    c = lax.axis_index("ctx")
    y = lax.axis_index("tp")
    z, x = f // 2, f % 2
    hi, lo = z // 2, z % 2
    rows, model = xb.shape
    slot = rows // 2
    width = wo.shape[2]
    hidden = we.shape[2]
    each = wo.shape[1] * 2
    blocks = la.shape[0] // 2
    block = la.shape[-1]
    a_count, a_width = ina.shape[0], ina.shape[-1]
    heads = width // HD
    sibling = (f, 1 - c, y)
    across = (z * 2 + (1 - x), c, y)
    partner = (f, c, 1 - y)
    beside = ((hi * 2 + 1 - lo) * 2 + x, c, y)
    beyond = (((1 - hi) * 2 + lo) * 2 + x, c, y)
    others = [((f + d) % 8, c, y) for d in range(1, 8)]

    def remote(src, dst, s, r, dev):
        copy = pltpu.make_async_remote_copy(
            src_ref=src, dst_ref=dst, send_sem=s, recv_sem=r, device_id=dev, device_id_type=MESH
        )
        copy.start()
        return copy

    def local(src, dst, s):
        copy = pltpu.make_async_copy(src, dst, s)
        copy.start()
        return copy

    def taken(ref, sem):
        pltpu.make_async_copy(ref, ref, sem).wait()

    order = list(range(1, a_count)) + [0]
    own_x = local(x_in, xb.at[pl.ds(0, slot)], ld.at[0])
    own_s = local(s_in, so.at[f], ld.at[1])
    own_g = local(g_in, gb.at[pl.ds(0, slot)], ld.at[2])
    own_o = local(wo.at[c], oa.at[hi, lo, x, c], ld.at[3])
    own_a = [local(wa.at[k, c], ina.at[k, hi, lo, x, c], ld.at[4 + k]) for k in order]
    for j in range(2 * blocks):
        local(
            (we if j % 2 == 0 else wc).at[c, :, pl.ds(j // 2 * block, block)],
            la.at[j, hi, lo, x, c],
            ld.at[4 + a_count + j],
        )
    bar = pltpu.get_barrier_semaphore()
    for p in others + [sibling, partner]:
        pl.semaphore_signal(bar, 1, device_id=p, device_id_type=MESH)
    pl.semaphore_wait(bar, 9)

    def start_z(q, buf):
        piece = buf.at[hi, lo, x, c]
        remote(piece, piece, zs.at[q], zr.at[q], beyond)

    def late_start(j):
        taken(la.at[j, 0, 0, 0, 0], ld.at[4 + a_count + j])
        start_z(l_q + j, la.at[j])

    def spread_z(q, buf):
        taken(buf.at[0, 0, 0, 0], zr.at[q])
        remote(buf.at[:, lo, x, c], buf.at[:, lo, x, c], bs.at[q], br.at[q], beside)

    def over_x(q, buf):
        taken(buf.at[:, 0, 0, 0], br.at[q])
        remote(buf.at[:, :, x, c], buf.at[:, :, x, c], xs.at[q], xr.at[q], across)

    def over_c(q, buf):
        taken(buf.at[:, :, 0, 0], xr.at[q])
        remote(buf.at[:, :, :, c], buf.at[:, :, :, c], cs.at[q], cr.at[q], sibling)

    def ready(q, buf):
        taken(buf.at[:, :, :, 0], cr.at[q])

    o_q = a_count
    l_q = a_count + 1

    def chunk(q):
        return ina.at[order[q]] if q < a_count else oa if q == o_q else la.at[q - l_q]

    def advance(q):
        over_x(q, chunk(q))
        spread_z(q + 1, chunk(q + 1))
        if q + 3 == o_q:
            own_o.wait()
            start_z(o_q, oa)
        else:
            late_start(q + 3 - l_q)
        if q > 1:
            over_c(q - 2, chunk(q - 2))

    sent = []
    own_s.wait()
    sent += [remote(so.at[f], so.at[f], ss.at[d], sr.at[d], others[d]) for d in range(7)]
    for q in range(a_count):
        own_a[q].wait()
        start_z(q, chunk(q))
    own_x.wait()
    sent.append(
        remote(xb.at[pl.ds(0, slot)], xb.at[pl.ds(slot, slot)], ys.at[0], yr.at[0], partner)
    )
    own_g.wait()
    sent.append(
        remote(gb.at[pl.ds(0, slot)], gb.at[pl.ds(slot, slot)], ys.at[1], yr.at[1], partner)
    )
    spread_z(0, chunk(0))

    for d in range(7):
        taken(so.at[(f - d - 1 + 8) % 8], sr.at[d])
    lanes = so.shape[2]
    step_row = lax.broadcasted_iota(jnp.int32, (lanes, model), 0)
    step_col = lax.broadcasted_iota(jnp.int32, (lanes, model), 1)
    total = jnp.zeros((so.shape[1], model), f32)
    for i in range(8):
        pick = (step_col == step_row + i * each) & (step_row < each)
        total = total + dot(so[i], jnp.where(pick, 1.0, 0.0).astype(bf16))
    vec_ref[...] = total
    per = hidden // 4
    step_row = lax.broadcasted_iota(jnp.int32, (lanes, per), 0)
    step_col = lax.broadcasted_iota(jnp.int32, (lanes, per), 1)
    for i in range(4):
        total = jnp.zeros((so.shape[1], per), f32)
        which = lax.broadcasted_iota(jnp.int32, (so.shape[1], 1), 0)
        for r in range(per // each):
            pick = (step_col == step_row + r * each) & (step_row < each)
            row = jnp.where(which == 8 + r, so[4 * y + i], jnp.zeros((), bf16))
            total = total + dot(row, jnp.where(pick, 1.0, 0.0).astype(bf16))
        eb[:, i * per : (i + 1) * per] = jnp.sum(total, axis=0, keepdims=True)
    near = pl.ds(pl.multiple_of(y * width, 128), width)
    tb[:, :width] = vec_ref[2:3, near]
    tb[:, width : 2 * width] = jnp.zeros((1, width), f32)
    tb[:, 2 * width :] = vec_ref[3:4, near]

    def first_norm(start):
        def body(i, carry):
            at = pl.ds(pl.multiple_of(start + i * 128, 128), 128)
            hat, _ = normalize(xb[at].astype(f32))
            n1[at] = (hat * vec_ref[0:1] + vec_ref[1:2]).astype(bf16)
            return carry

        lax.fori_loop(0, slot // 128, body, 0)

    advance(0)
    first_norm(0)
    advance(1)
    advance(2)
    taken(xb.at[pl.ds(slot, slot)], yr.at[0])
    first_norm(slot)
    advance(3)

    def project_chunk(q):
        k = order[q]
        ready(q, chunk(q))
        cols = slice(k * a_width, (k + 1) * a_width)

        def body(i, carry):
            at = pl.ds(pl.multiple_of(i * 256, 256), 256)
            proj[at, cols] = (dot(n1[at], ina[k].reshape(model, a_width)) + tb[:, cols]).astype(bf16)
            return carry

        lax.fori_loop(0, rows // 256, body, 0)
        start, stop = max(k * a_width, width), (k + 1) * a_width
        if start < stop:
            sent.append(
                remote(
                    proj.at[:, pl.ds(start, stop - start)],
                    far.at[:, pl.ds(start - width, stop - start)],
                    fs.at[k],
                    fr.at[k],
                    sibling,
                )
            )

    project_chunk(0)
    project_chunk(1)
    advance(4)
    project_chunk(2)
    writes = [local(n1, n1_out, outs.at[0]), local(proj, proj_out, outs.at[1])]
    for k in range(1, a_count):
        start, stop = max(k * a_width, width), (k + 1) * a_width
        taken(far.at[:, pl.ds(start - width, stop - start)], fr.at[k])
    writes.append(local(far, far_out, outs.at[2]))

    stat[...] = jnp.zeros_like(stat)
    score_factor = HD ** (-0.5) * LOG2E
    tall = acc.shape[0]

    def attend_step(i, carry):
        at = pl.ds(pl.multiple_of(i * tall, tall), tall)
        acc[...] = jnp.zeros_like(acc)
        for head in range(heads):
            start, stop, mask = head_window(head)
            query = jnp.where(mask, proj[at, start:stop], jnp.zeros((), bf16))
            a = dot(query, proj[:, width + start : width + stop], NT)
            b = dot(query, far[:, start:stop], NT)
            a = a * score_factor + bias_ref[0:1, :rows]
            b = b * score_factor + bias_ref[0:1, rows:]
            top = jnp.maximum(
                jnp.max(a, axis=-1, keepdims=True), jnp.max(b, axis=-1, keepdims=True)
            )
            a = jnp.exp2(a - top)
            b = jnp.exp2(b - top)
            total = jnp.sum(a, axis=-1, keepdims=True) + jnp.sum(b, axis=-1, keepdims=True)
            mixed = dot(a.astype(bf16), proj[:, 2 * width + start : 2 * width + stop])
            mixed = mixed + dot(b.astype(bf16), far[:, width + start : width + stop])
            mixed = mixed * (1.0 / total)
            acc[:, start:stop] += jnp.where(mask, mixed, 0.0)
            lane = lax.broadcasted_iota(jnp.int32, (1, 128), 1)
            stat[at, :] += jnp.where(lane == head, top + jnp.log2(total), 0.0)
        att[at] = acc[...].astype(bf16)
        remote(att.at[at], atto.at[at], ys.at[3 + i], yr.at[3 + i], partner)
        over_x(l_q + 1 + i, la.at[1 + i])
        spread_z(l_q + 2 + i, la.at[2 + i])
        late_start(4 + i)

        @pl.when(i == 0)
        def _():
            over_c(o_q, oa)
            remote(oa.at[:, :, :, c], ob.at[:, :, :, c], ys.at[2], yr.at[2], partner)

        @pl.when(i > 0)
        def _():
            over_c(l_q + i - 1, la.at[i - 1])

        return carry

    steps = rows // tall
    lax.fori_loop(0, steps, attend_step, 0)
    lse_ref[...] = stat[...].T
    writes.append(local(att, att_out, outs.at[3]))
    taken(ob.at[:, :, :, c], yr.at[2])
    b_q = zs.shape[0] - 1
    remote(ob.at[:, :, :, c], ob.at[:, :, :, c], cs.at[b_q], cr.at[b_q], sibling)
    advance(8)
    ready(o_q, oa)
    ready(b_q, ob)
    writes.append(local(oa, outer_out, outs.at[4]))
    for q, k in enumerate(order):
        writes.append(
            local(ina.at[k], inner_out.at[:, :, :, :, :, pl.ds(k * a_width, a_width)], outs.at[5 + k])
        )
    for i in range(steps):
        at = pl.ds(i * tall, tall)
        taken(atto.at[at], yr.at[3 + i])

    def residual_half(i):
        at = slice(i * slot, (i + 1) * slot)
        back = slice((1 - i) * slot, (2 - i) * slot)
        mixed = dot(att[at], oa[...].reshape(model, width), NT)
        res[at] = mixed + dot(atto[back], ob[...].reshape(model, width), NT)

        def body(j, carry):
            row = pl.ds(pl.multiple_of(i * slot + j * 128, 128), 128)
            value = xb[row].astype(f32) + (res[row] + vec_ref[4:5])
            res[row] = value
            hat, _ = normalize(value)
            n2[row] = (hat * vec_ref[5:6] + vec_ref[6:7]).astype(bf16)
            return carry

        lax.fori_loop(0, slot // 128, body, 0)

    residual_half(0)
    advance(9)
    residual_half(1)
    advance(10)
    late_writes = [
        local(res.at[pl.ds(0, slot)], res_out, outs.at[5 + a_count]),
        local(n2, n2_out, outs.at[6 + a_count]),
    ]
    taken(gb.at[pl.ds(slot, slot)], yr.at[1])
    late_writes.append(local(gb, g_out, outs.at[7 + a_count]))
    dn[...] = jnp.zeros_like(dn)
    ho[...] = jnp.zeros_like(ho)
    s_at = 8 + a_count

    def pass_chunks(b):
        @pl.when(b < 3)
        def _():
            over_x(l_q + 7 + b, la.at[7 + b])

        @pl.when(b < 2)
        def _():
            spread_z(l_q + 8 + b, la.at[8 + b])

        @pl.when(b < 3)
        def _():
            over_c(l_q + 5 + b, la.at[5 + b])

        @pl.when(b == 3)
        def _():
            over_c(l_q + 9, la.at[9])

    def hidden_step_in(b, carry):
        ready(l_q + 2 * b, la.at[2 * b])
        ready(l_q + 2 * b + 1, la.at[2 * b + 1])
        turn = b % 2
        cols = pl.ds(pl.multiple_of(b * block, block), block)

        @pl.when(b > 1)
        def _():
            taken(stage.at[0, turn], outs.at[s_at + turn])
            taken(stage.at[1, turn], outs.at[s_at + 2 + turn])

        shift = eb[:, cols]
        total = jnp.zeros((1, block), f32)
        for i in range(rows // 256):
            at = slice(i * 256, (i + 1) * 256)
            pre = dot(n2[at], la[2 * b].reshape(model, block)) + shift
            back = dot(gb[at], la[2 * b + 1].reshape(model, block))
            cdf = 0.5 + 0.5 * lax.erf(pre * (0.5**0.5))
            density = jnp.exp(pre * pre * -0.5) * 0.3989422804014327
            low = (back * (cdf + pre * density)).astype(bf16)
            active = (pre * cdf).astype(bf16)
            stage[0, turn, at] = active
            stage[1, turn, at] = low
            total = total + jnp.sum(low.astype(f32), axis=0, keepdims=True)
            dn[at] += dot(low, la[2 * b].reshape(model, block), NT)
            ho[at] += dot(active, la[2 * b + 1].reshape(model, block), NT)
            if i == 1:
                pass_chunks(b)
        esum_ref[:, cols] = total
        local(stage.at[0, turn], act_out.at[:, cols], outs.at[s_at + turn])
        local(stage.at[1, turn], pre_out.at[:, cols], outs.at[s_at + 2 + turn])

        @pl.when(b == 2)
        def _():
            over_c(l_q + 8, la.at[8])

        return carry

    lax.fori_loop(0, blocks, hidden_step_in, 0)
    for copy in writes:
        copy.wait()
    n1[:slot] = dn[slot:].astype(bf16)
    n1[slot:] = ho[slot:].astype(bf16)
    last = [
        local(dn.at[pl.ds(0, slot)], dn_own, ld.at[0]),
        local(ho.at[pl.ds(0, slot)], ho_own, ld.at[1]),
        local(n1.at[pl.ds(0, slot)], dn_oth, ld.at[2]),
        local(n1.at[pl.ds(slot, slot)], ho_oth, ld.at[3]),
    ]
    for turn in range(2):
        taken(stage.at[0, turn], outs.at[s_at + turn])
        taken(stage.at[1, turn], outs.at[s_at + 2 + turn])
    for copy in late_writes + last:
        copy.wait()
    for copy in sent:
        copy.wait_send()
    for q in range(b_q):
        taken(oa.at[:, :, :, 0] if q < l_q else la.at[0, :, :, :, 0], cs.at[q])
        taken(chunk(q).at[:, :, 0, 0], xs.at[q])
        taken(chunk(q).at[:, 0, 0, 0], bs.at[q])
        taken(chunk(q).at[0, 0, 0, 0], zs.at[q])
    taken(ob.at[:, :, :, 0], cs.at[b_q])
    taken(oa.at[:, :, :, 0], ys.at[2])
    for i in range(steps):
        taken(att.at[pl.ds(i * tall, tall)], ys.at[3 + i])


def forward(x_own, g_own, smalls, wa, wo, we, wc, bias):
    slot, model = x_own.shape
    rows = 2 * slot
    each = wo.shape[0]
    width, hidden = wo.shape[1], we.shape[1]
    half = each // 2
    a_width, block = width, 512
    a_count, blocks = 3 * width // a_width, hidden // block
    grid = (2, 2, 2, 2, half)
    chunks = a_count + 2 + 2 * blocks
    sem = pltpu.SemaphoreType.DMA
    out = jax.ShapeDtypeStruct

    def halves(w):
        return w.reshape(2, half, w.shape[1])

    return pl.pallas_call(
        forward_kernel,
        in_specs=[HBM] * 7 + [VMEM],
        out_specs=(HBM,) * 6 + (VMEM,) + (HBM,) * 5 + (VMEM,) + (HBM,) * 4 + (VMEM,),
        out_shape=(
            out(grid + (3 * width,), bf16),
            out(grid + (width,), bf16),
            out((rows, model), bf16),
            out((rows, 3 * width), bf16),
            out((rows, 2 * width), bf16),
            out((rows, width), bf16),
            out((128, rows), f32),
            out((slot, model), f32),
            out((rows, model), bf16),
            out((rows, model), bf16),
            out((rows, hidden), bf16),
            out((rows, hidden), bf16),
            out((1, hidden), f32),
            out((slot, model), f32),
            out((slot, model), bf16),
            out((slot, model), f32),
            out((slot, model), bf16),
            out((16, model), f32),
        ),
        scratch_shapes=[
            pltpu.VMEM((8,) + smalls.shape, bf16),
            pltpu.VMEM((a_count,) + grid + (a_width,), bf16),
            pltpu.VMEM(grid + (width,), bf16),
            pltpu.VMEM(grid + (width,), bf16),
            pltpu.VMEM((2 * blocks,) + grid + (block,), bf16),
            pltpu.VMEM((rows, model), bf16),
            pltpu.VMEM((rows, model), bf16),
            pltpu.VMEM((rows, model), bf16),
            pltpu.VMEM((rows, 3 * width), bf16),
            pltpu.VMEM((rows, 2 * width), bf16),
            pltpu.VMEM((1, 3 * width), f32),
            pltpu.VMEM((1, hidden), f32),
            pltpu.VMEM((256, width), f32),
            pltpu.VMEM((rows, 128), f32),
            pltpu.VMEM((rows, width), bf16),
            pltpu.VMEM((rows, width), bf16),
            pltpu.VMEM((rows, model), f32),
            pltpu.VMEM((rows, model), bf16),
            pltpu.VMEM((2, 2, rows, block), bf16),
            pltpu.VMEM((rows, model), f32),
            pltpu.VMEM((rows, model), f32),
            sem((4 + a_count + 2 * blocks,)),
            sem((7,)),
            sem((7,)),
            sem((chunks,)),
            sem((chunks,)),
            sem((chunks,)),
            sem((chunks,)),
            sem((chunks,)),
            sem((chunks,)),
            sem((chunks,)),
            sem((chunks,)),
            sem((3 + rows // 256,)),
            sem((3 + rows // 256,)),
            sem((a_count,)),
            sem((a_count,)),
            sem((12 + a_count,)),
        ],
        compiler_params=params(collective_id=1, has_side_effects=True),
    )(x_own, g_own, smalls, wa.reshape(3, 2, half, width), halves(wo), halves(we), halves(wc), bias)


def backward_kernel(
    act_in, pre_in, n2_in, g_in, dn_in, dno_in, res_in, proj_in, far_in, att_in, n1_in, inner_in, outer_in, x_in,
    lse_ref, bias_ref, vec_ref, esum_ref,
    hg_out, ge_ref, gc_ref, go_ref, ga_ref, sum_ref, esum_out,
    u, att, dqt, keyt, dots, acc, drecv, oa, b1, b2, t1, t2, res, dn, dnr, stream, gproj, own, near, far, one, two, flat,
    part, got,
    ld, cs, cr, xs, xr, zs, zr, ws, wr, ys, yr, fs, fr, vs, vr, free,
):
    f = lax.axis_index("fsdp")
    c = lax.axis_index("ctx")
    y = lax.axis_index("tp")
    z, x = f // 2, f % 2
    hi, lo = z // 2, z % 2
    rows, model = b1.shape
    slot = rows // 2
    width = att.shape[1]
    heads = width // HD
    ring = own.shape[0]
    tile = 128
    per = pre_in.shape[1] // width
    pieces = slot // tile
    block = acc.shape[0]
    sibling = (f, 1 - c, y)
    across = (z * 2 + (1 - x), c, y)
    partner = (f, c, 1 - y)
    beside = ((hi * 2 + 1 - lo) * 2 + x, c, y)
    beyond = (((1 - hi) * 2 + lo) * 2 + x, c, y)
    opposite = (((1 - hi) * 2 + 1 - lo) * 2 + x, c, y)
    diagonal = (f, 1 - c, 1 - y)

    def remote(src, dst, s, r, dev):
        pltpu.make_async_remote_copy(
            src_ref=src, dst_ref=dst, send_sem=s, recv_sem=r, device_id=dev, device_id_type=MESH
        ).start()

    def local(src, dst, s):
        copy = pltpu.make_async_copy(src, dst, s)
        copy.start()
        return copy

    def taken(ref, sem):
        pltpu.make_async_copy(ref, ref, sem).wait()

    def columns(k):
        return pl.ds(pl.multiple_of(k * width, tile), width)

    own_n2 = local(n2_in, b1, ld.at[0])
    own_g = local(g_in, b2, ld.at[1])
    for k in range(2):
        local(pre_in.at[:, columns(k)], stream.at[k], ld.at[2 + k])
    own_res = local(res_in, res, ld.at[4])
    own_dn = local(dn_in, dn, ld.at[5])
    own_oa = local(outer_in, oa, ld.at[6])
    own_att = local(att_in, att, ld.at[7])
    own_proj = local(proj_in, u.at[pl.ds(0, rows)], ld.at[8])
    own_far = local(far_in, u.at[pl.ds(rows, rows), pl.ds(width, 2 * width)], ld.at[9])
    bar = pltpu.get_barrier_semaphore()
    for p in [sibling, across, partner, beside, beyond, opposite, diagonal]:
        pl.semaphore_signal(bar, 1, device_id=p, device_id_type=MESH)
    pl.semaphore_wait(bar, 7)
    remote(dno_in, dnr, ys.at[0], yr.at[0], partner)

    def turned(dst, src, start, count):
        def body(i, carry):
            at = pl.ds(pl.multiple_of(start + i * tile, tile), tile)
            dst[:, at] = src[at].T
            return carry

        lax.fori_loop(0, count // tile, body, 0)

    def produce(k, left, right):
        def body(i, carry):
            at = pl.ds(pl.multiple_of(i * (model // 2), tile), model // 2)
            piece = dot(left[at], right).astype(bf16)
            own[k % ring, i] = piece.reshape(own.shape[2:])
            return carry

        lax.fori_loop(0, 2, body, 0)
        remote(own.at[k % ring, :, :, :, 1 - c], near.at[k], cs.at[k], cr.at[k], sibling)

    def first(k):
        taken(near.at[k], cr.at[k])

        def body(i, carry):
            for j in range(4):
                at = (k, i, j // 2, j % 2)
                near[at] = near[at] + own[k % ring, i, j // 2, j % 2, c]
            return carry

        lax.fori_loop(0, 2, body, 0)
        remote(near.at[k, :, :, 1 - x], far.at[k], xs.at[k], xr.at[k], across)

    def second(k):
        taken(far.at[k], xr.at[k])

        def body(i, carry):
            for j in range(2):
                near[k, i, j, x] = near[k, i, j, x] + far[k, i, j]
            return carry

        lax.fori_loop(0, 2, body, 0)
        remote(near.at[k, :, 1 - lo, x], one.at[k], zs.at[k], zr.at[k], beside)

    def half(k):
        taken(one.at[k], zr.at[k])
        for i in range(2):
            near[k, i, lo, x] = near[k, i, lo, x] + one[k, i]
        remote(near.at[k, 1 - hi, lo, x], two.at[k], ws.at[k], wr.at[k], beyond)

    def third(k):
        taken(two.at[k], wr.at[k])
        total = near[k, hi, lo, x].astype(f32) + two[k].astype(f32)
        if k < per:
            ge_ref[:, k * width : (k + 1) * width] = total
        elif k < 2 * per:
            gc_ref[:, (k - per) * width : (k - per + 1) * width] = total
        elif k == 2 * per:
            go_ref[...] = total
        else:
            ga_ref[k - 2 * per - 1] = total

    own_n2.wait()
    turned(t1, b1, 0, rows)
    pl.semaphore_signal(free, 1, device_id=partner, device_id_type=MESH)

    def expand_chunk(k, carry):
        taken(stream.at[k % 2], ld.at[2 + k % 2])

        @pl.when(k >= ring)
        def _():
            taken(near.at[k - ring], cs.at[k - ring])

        produce(k, t1, stream[k % 2])

        @pl.when(k + 2 < per)
        def _():
            local(pre_in.at[:, columns(k + 2)], stream.at[k % 2], ld.at[2 + k % 2])

        @pl.when(k + 2 >= per)
        def _():
            local(act_in.at[:, columns(k + 2 - per)], stream.at[k % 2], ld.at[2 + k % 2])

        @pl.when(k > 0)
        def _():
            first(k - 1)

        return carry

    lax.fori_loop(0, per, expand_chunk, 0)
    own_g.wait()
    turned(t2, b2, 0, rows)

    def contract_chunk(k, carry):
        taken(stream.at[k % 2], ld.at[2 + k % 2])
        taken(near.at[k - ring], cs.at[k - ring])
        produce(k, t2, stream[k % 2])

        @pl.when(k + 2 < 2 * per)
        def _():
            local(act_in.at[:, columns(k + 2 - per)], stream.at[k % 2], ld.at[2 + k % 2])

        first(k - 1)
        return carry

    lax.fori_loop(per, 2 * per, contract_chunk, 0)
    o_at = 2 * per
    first(o_at - 1)
    second(0)

    own_res.wait()
    own_dn.wait()
    taken(dnr, yr.at[0])
    pl.semaphore_wait(free, 1)
    routes = [[sibling, partner, diagonal], [beside, beyond, opposite], [across]]

    def pass_on(n, i):
        if i > 0:
            total = part[n, i - 1]
            for r in range(len(routes[i - 1])):
                at = 3 * (i - 1) + r
                taken(got.at[n, at], vr.at[n, at])
                total = total + got[n, at]
            part[n, i] = total
        if i < len(routes):
            for r, there in enumerate(routes[i]):
                at = 3 * i + r
                remote(part.at[n, i], got.at[n, at], vs.at[n, at], vr.at[n, at], there)

    sums = part.at[0, 0]
    sums[...] = jnp.zeros(sums.shape, f32)
    part[1, 0] = jnp.zeros(sums.shape, f32)
    for i in range(esum_ref.shape[1] // model):
        part[1, 0, pl.ds(2 * y + i, 1), :] = esum_ref[:, i * model : (i + 1) * model]
    pass_on(1, 0)

    def second_norm(i, carry):
        at = pl.ds(pl.multiple_of(i * tile, tile), tile)
        grad = dn[at] + dnr[at].astype(f32)
        hat, inverse = normalize(res[at])
        scaled = grad * vec_ref[5:6]
        mean = jnp.mean(scaled, axis=-1, keepdims=True)
        slope = jnp.mean(scaled * hat, axis=-1, keepdims=True)
        out_grad = b2[at].astype(f32)
        result = out_grad + inverse * (scaled - mean - hat * slope)
        low = result.astype(bf16)
        dn[at] = result
        b1[at] = low
        sums[5:6] += jnp.sum(grad * hat, axis=0, keepdims=True)
        sums[6:7] += jnp.sum(grad, axis=0, keepdims=True)
        sums[4:5] += jnp.sum(low.astype(f32), axis=0, keepdims=True)
        sums[7:8] += jnp.sum(out_grad, axis=0, keepdims=True)
        there = pl.ds(pl.multiple_of(slot + i * tile, tile), tile)
        remote(b1.at[at], b1.at[there], ys.at[1 + i], yr.at[1 + i], partner)
        return carry

    lax.fori_loop(0, pieces, second_norm, 0)
    own_n1 = local(n1_in, b2, ld.at[1])
    second(1)
    own_oa.wait()
    own_proj.wait()
    own_far.wait()
    own_att.wait()

    def attended_grad(turn):
        at = slice(turn * slot, (turn + 1) * slot)
        turned(t2, b1, turn * slot, slot)
        low_grad = dot(b1[at], oa[...]).astype(bf16)
        u[rows + turn * slot : rows + (turn + 1) * slot, :width] = low_grad
        product = low_grad.astype(f32) * att[at].astype(f32)
        high = product.astype(bf16)
        low = (product - high.astype(f32)).astype(bf16)
        lane = lax.broadcasted_iota(jnp.int32, (16, width), 1)
        row = lax.broadcasted_iota(jnp.int32, (16, width), 0)
        pick = jnp.where((lane >= row * HD) & (lane < row * HD + HD), 1.0, 0.0).astype(bf16)
        dots[:, at] = dot(pick, high, NT) + dot(pick, low, NT)

    attended_grad(0)
    own_n1.wait()
    turned(t1, b2, 0, rows)
    pass_on(1, 1)

    dqt[...] = jnp.zeros_like(dqt)
    score_factor = HD ** (-0.5) * LOG2E
    scale = HD ** (-0.5)
    near_blocks = rows // block
    count = 2 * near_blocks

    def attend_step(i, carry):
        later = i // count
        j = i % count
        b = (j + near_blocks) % count

        @pl.when(i == count)
        def _():
            for n in range(pieces):
                taken(b1.at[pl.ds(slot + n * tile, tile)], yr.at[1 + n])
            attended_grad(1)
            taken(near.at[o_at - ring], cs.at[o_at - ring])
            produce(o_at, t2, att[...])

        at = pl.ds(pl.multiple_of(b * block, block), block)
        far_at = pl.ds(pl.multiple_of(j % near_blocks * block, block), block)
        asked = pl.ds(pl.multiple_of(later * slot, tile), slot)
        asked_grad = pl.ds(pl.multiple_of(rows + later * slot, tile), slot)

        @pl.when(later == 0)
        def _():
            acc[...] = jnp.zeros_like(acc)

        @pl.when((later == 1) & (j < near_blocks))
        def _():
            acc[:, :width] = stream[0, far_at].astype(f32)
            acc[:, width:] = stream[1, far_at].astype(f32)

        @pl.when((later == 1) & (j >= near_blocks))
        def _():
            acc[...] = gproj[far_at, width:].astype(f32)

        keyt[...] = u[at, width : 2 * width].T
        bias = jnp.broadcast_to(bias_ref[0:1, at], (tile, block)).T[:, 0:1]
        for head in range(heads):
            start, stop, mask = head_window(head)
            zero = jnp.zeros((), bf16)
            query = jnp.where(mask, u[asked, start:stop], zero)
            grad = jnp.where(mask, u[asked_grad, start:stop], zero)
            scores = dot(u[at, width + start : width + stop], query, NT) * score_factor + bias
            probs = jnp.exp2(scores - lse_ref[head : head + 1, asked])
            grad_probs = dot(u[at, 2 * width + start : 2 * width + stop], grad, NT)
            grad_scores = (probs * (grad_probs - dots[head : head + 1, asked])).astype(bf16)
            acc[:, start:stop] += dot(grad_scores, query)
            acc[:, width + start : width + stop] += dot(probs.astype(bf16), grad)
            lines = slice(head * HD, head * HD + HD)
            dqt[lines, asked] += dot(keyt[lines, :], grad_scores)

        @pl.when((later == 0) & (j < near_blocks))
        def _():
            stream[0, far_at] = acc[:, :width].astype(bf16)
            stream[1, far_at] = acc[:, width:].astype(bf16)

        @pl.when((later == 0) & (j >= near_blocks))
        def _():
            gproj[far_at, width:] = acc[...].astype(bf16)

        @pl.when((later == 1) & (j < near_blocks))
        def _():
            stream[0, far_at] = (acc[:, :width] * scale).astype(bf16)
            stream[1, far_at] = acc[:, width:].astype(bf16)
            remote(stream.at[:, far_at], drecv.at[:, far_at], fs.at[j % near_blocks], fr.at[j % near_blocks], sibling)

        @pl.when((later == 1) & (j >= near_blocks))
        def _():
            taken(drecv.at[:, far_at], fr.at[j % near_blocks])
            key = acc[:, :width] * scale + drecv[0, far_at].astype(f32)
            gproj[far_at, width : 2 * width] = key.astype(bf16)
            value = acc[:, width:] + drecv[1, far_at].astype(f32)
            gproj[far_at, 2 * width :] = value.astype(bf16)

        @pl.when(i == 2)
        def _():
            second(2)
            half(0)

        @pl.when(i == 4)
        def _():
            second(3)
            half(1)

        @pl.when(i == 6)
        def _():
            first(o_at)
            second(4)
            half(2)
            third(0)

        @pl.when(i == 8)
        def _():
            second(5)
            half(3)
            third(1)

        @pl.when(i == 10)
        def _():
            second(6)
            half(4)
            third(2)

        return carry

    lax.fori_loop(0, 2 * count, attend_step, 0)
    own_x = local(x_in, b1.at[pl.ds(slot, slot)], ld.at[10])
    own_inner = local(inner_in, u.at[pl.ds(0, model)], ld.at[8])
    gproj[:, :width] = (dqt[...].T * scale).astype(bf16)

    def project_chunk(j):
        k = o_at + 1 + j
        taken(near.at[k - ring], cs.at[k - ring])
        produce(k, t1, gproj[:, j * width : (j + 1) * width])

    for i in range(pieces):
        taken(b1.at[pl.ds(i * tile, tile)], ys.at[1 + i])
    own_inner.wait()
    split = model // 2
    for n in range(2):
        at = slice(n * split, (n + 1) * split)
        b1[:slot, at] = dot(gproj[slot:], u[at], NT).astype(bf16)
        at = pl.ds(n * split, split)
        remote(b1.at[pl.ds(0, slot), at], dnr.at[:, at], ys.at[1 + pieces + n], yr.at[1 + pieces + n], partner)
    project_chunk(0)
    project_chunk(1)
    first(o_at + 1)
    project_chunk(2)
    first(o_at + 2)
    second(7)
    half(5)
    third(3)
    first(o_at + 3)
    half(6)
    third(4)
    second(8)
    half(7)
    third(5)
    for n in range(2):
        at = slice(n * split, (n + 1) * split)
        res[:, at] = dot(gproj[:slot], u[at], NT)
    totals = dot(jnp.ones((8, rows), bf16), gproj[...])
    sums[2:3, columns(y)] = totals[0:1, :width]
    sums[3:4, columns(y)] = totals[0:1, 2 * width :]
    half(8)
    third(6)
    second(9)
    third(7)
    own_x.wait()
    for n in range(2):
        taken(dnr.at[:, pl.ds(n * split, split)], yr.at[1 + pieces + n])

    def first_norm(i, carry):
        at = pl.ds(pl.multiple_of(i * tile, tile), tile)
        grad = res[at] + dnr[at].astype(f32)
        there = pl.ds(pl.multiple_of(slot + i * tile, tile), tile)
        hat, inverse = normalize(b1[there].astype(f32))
        scaled = grad * vec_ref[0:1]
        mean = jnp.mean(scaled, axis=-1, keepdims=True)
        slope = jnp.mean(scaled * hat, axis=-1, keepdims=True)
        result = dn[at] + inverse * (scaled - mean - hat * slope)
        flat[at] = result.reshape(tile, 1, model)
        sums[0:1] += jnp.sum(grad * hat, axis=0, keepdims=True)
        sums[1:2] += jnp.sum(grad, axis=0, keepdims=True)
        return carry

    lax.fori_loop(0, pieces, first_norm, 0)
    write = local(flat.at[pl.ds(0, hg_out.shape[0])], hg_out, ld.at[5])

    pass_on(0, 0)
    half(9)
    third(8)
    second(10)
    third(9)
    pass_on(0, 1)
    pass_on(1, 2)
    half(10)
    pass_on(0, 2)
    third(10)
    owner = f * 2 + c

    def owned(total, span, lanes, start):
        high = total.astype(bf16)
        low = (total - high.astype(f32)).astype(bf16)
        row = lax.broadcasted_iota(jnp.int32, (model, lanes), 0)
        lane = lax.broadcasted_iota(jnp.int32, (model, lanes), 1)
        pick = jnp.where((row == lane + start) & (lane < span), 1.0, 0.0).astype(bf16)
        return dot(high, pick) + dot(low, pick)

    each = model // 16
    second(11)
    pass_on(1, 3)
    rows_of = owned(part[1, 3], 4 * each, esum_out.shape[1], owner % 4 * 4 * each)
    which = lax.broadcasted_iota(jnp.int32, rows_of.shape, 0)
    esum_out[...] = jnp.sum(jnp.where(which == owner // 4, rows_of, 0.0), axis=0, keepdims=True)
    half(11)
    pass_on(0, 3)
    sum_ref[...] = owned(part[0, 3], each, sum_ref.shape[1], owner * each)
    third(11)
    for n in range(2):
        for i in range(len(routes)):
            for r in range(len(routes[i])):
                taken(part.at[n, i], vs.at[n, 3 * i + r])
    write.wait()
    taken(dnr, ys.at[0])
    for n in range(2):
        taken(dnr.at[:, pl.ds(n * split, split)], ys.at[1 + pieces + n])
    for i in range(near_blocks):
        piece = pl.ds(i * block, block)
        taken(stream.at[:, piece], fs.at[i])
    for k in range(near.shape[0]):
        if k + ring >= near.shape[0]:
            taken(near.at[k], cs.at[k])
        taken(far.at[k], xs.at[k])
        taken(one.at[k], zs.at[k])
        taken(two.at[k], ws.at[k])


def backward(act, pre, n2, g, dn, dno, res, proj, far, att, n1, inner, outer, x_own, lse, bias, vectors, esum, share):
    rows, model = n2.shape
    slot = rows // 2
    width = att.shape[1]
    hidden = act.shape[1]
    owned = model // 16
    block = 256
    chunks = 2 * hidden // width + 4
    ring = 2
    sem = pltpu.SemaphoreType.DMA
    out = jax.ShapeDtypeStruct
    return pl.pallas_call(
        backward_kernel,
        in_specs=[HBM] * 14 + [VMEM] * 4,
        out_specs=(HBM,) + (VMEM,) * 6,
        out_shape=(
            out((share, 1, model), f32),
            out((owned, hidden), f32),
            out((owned, hidden), f32),
            out((owned, width), f32),
            out((3, owned, width), f32),
            out((8, 128), f32),
            out((1, 384), f32),
        ),
        scratch_shapes=[
            pltpu.VMEM((2 * rows, 3 * width), bf16),
            pltpu.VMEM((rows, width), bf16),
            pltpu.VMEM((width, rows), f32),
            pltpu.VMEM((width, block), bf16),
            pltpu.VMEM((16, rows), f32),
            pltpu.VMEM((block, 2 * width), f32),
            pltpu.VMEM((2, rows, width), bf16),
            pltpu.VMEM((model, width), bf16),
            pltpu.VMEM((rows, model), bf16),
            pltpu.VMEM((rows, model), bf16),
            pltpu.VMEM((model, rows), bf16),
            pltpu.VMEM((model, rows), bf16),
            pltpu.VMEM((slot, model), f32),
            pltpu.VMEM((slot, model), f32),
            pltpu.VMEM((slot, model), bf16),
            pltpu.VMEM((2, rows, width), bf16),
            pltpu.VMEM((rows, 3 * width), bf16),
            pltpu.VMEM((ring, 2, 2, 2, 2, owned, width), bf16),
            pltpu.VMEM((chunks, 2, 2, 2, owned, width), bf16),
            pltpu.VMEM((chunks, 2, 2, owned, width), bf16),
            pltpu.VMEM((chunks, 2, owned, width), bf16),
            pltpu.VMEM((chunks, owned, width), bf16),
            pltpu.VMEM((slot, 1, model), f32),
            pltpu.VMEM((2, 4, 8, model), f32),
            pltpu.VMEM((2, 7, 8, model), f32),
            sem((11,)),
            sem((chunks,)),
            sem((chunks,)),
            sem((chunks,)),
            sem((chunks,)),
            sem((chunks,)),
            sem((chunks,)),
            sem((chunks,)),
            sem((chunks,)),
            sem((3 + slot // 128,)),
            sem((3 + slot // 128,)),
            sem((rows // block,)),
            sem((rows // block,)),
            sem((2, 7)),
            sem((2, 7)),
            pltpu.SemaphoreType.REGULAR,
        ],
        compiler_params=params(collective_id=4, has_side_effects=True),
    )(act, pre, n2, g, dn, dno, res, proj, far, att, n1, inner, outer, x_own, lse, bias, vectors, esum)


def key_biases(share, slot, length, tp_rank, ctx_rank):
    places = lax.iota(jnp.int32, slot)
    pieces = []
    for ctx in (ctx_rank, 1 - ctx_rank):
        for tp in (tp_rank, 1 - tp_rank):
            start = (ctx * 2 + tp) * share
            valid = (places < share) & (start + places < length)
            pieces.append(jnp.where(valid, 0.0, masked_score).astype(f32))
    return jnp.concatenate(pieces)


def forward_parts(x_own, grad_own, smalls, inner, outer_t, expand_weight, contract_t, bias):
    slot, model = x_own.shape
    rows_each = inner.shape[0]
    half_each = rows_each // 2
    width, hidden = outer_t.shape[1], expand_weight.shape[1]
    heads = width // HD
    tp_rank = lax.axis_index("tp")
    ctx_rank = lax.axis_index("ctx")
    x_all = jnp.concatenate([x_own, swap(x_own, "tp")], axis=0)
    grad_all = jnp.concatenate([grad_own, swap(grad_own, "tp")], axis=0)
    inner = lax.all_gather(inner, "fsdp", axis=0, tiled=True)
    smalls_all = lax.all_gather(smalls, "fsdp", axis=0)
    late = jnp.concatenate([outer_t, swap(outer_t, "tp"), expand_weight, contract_t], axis=1)
    late = lax.dynamic_slice_in_dim(late, ctx_rank * half_each, half_each, 0)
    late = lax.all_gather(late, ("fsdp", "ctx"), axis=0, tiled=True)
    expand_at = 2 * width
    contract_at = 2 * width + hidden
    smalls_all = smalls_all[:, :, :rows_each].astype(f32)
    vectors = jnp.transpose(smalls_all[:, :8], (1, 0, 2)).reshape(8, model)
    expand_rows = smalls_all[:, 8 : 8 + hidden * 2 // model].reshape(1, 2 * hidden)
    expand_local = lax.dynamic_slice_in_dim(expand_rows, tp_rank * hidden, hidden, 1)
    pair = lax.dynamic_slice_in_dim(vectors[2:4], tp_rank * width, width, 1)
    triple = jnp.concatenate([pair[0:1], jnp.zeros((1, width), f32), pair[1:2]], axis=1)
    normed_one, proj = project(x_all, vectors[0:1], vectors[1:2], inner, triple)
    far = swap(proj[:, width:], "ctx")
    attended, lse = attend(proj, far, jnp.broadcast_to(bias[None], (8, bias.shape[0])), heads)
    attended_oth = swap(attended, "tp")
    residual, normed_two = residual_step(x_all, attended, attended_oth, late, width, vectors[4:7])
    activated, pre_grad, expand_sum, normed_own, normed_oth = hidden_step(
        normed_two, grad_all, late, expand_at, contract_at, hidden, expand_local
    )
    contracted = dot(activated, late[:, contract_at:], NT)
    return (
        inner, late[:, :width], normed_one, proj, far, attended, lse, residual[:slot], normed_two,
        grad_all, activated, pre_grad, expand_sum, normed_own, normed_oth, contracted[:slot],
        contracted[slot:].astype(bf16), vectors,
    )


def per_device(
    hidden_in,
    valid_lengths,
    output_grad,
    first_gain,
    first_shift,
    attention_in,
    query_value_bias,
    attention_out,
    attention_bias,
    second_gain,
    second_shift,
    expand_weight,
    expand_bias,
    contract_weight,
    contract_bias,
):
    _, share, model = hidden_in.shape
    tp_rank = lax.axis_index("tp")
    ctx_rank = lax.axis_index("ctx")
    fsdp_count = lax.axis_size("fsdp")
    rows_each = attention_in.shape[0]
    width = attention_in.shape[2]
    heads = width // HD
    hidden = expand_weight.shape[1]
    slot = -(-share // 128) * 128
    length = valid_lengths[0]

    def padded(value):
        return jnp.pad(value, ((0, slot - share), (0, 0)))

    own_start = (ctx_rank * 2 + tp_rank) * share
    token_valid = (own_start + lax.iota(jnp.int32, share)) < length
    grad_own = jnp.where(token_valid[:, None], output_grad[0], jnp.zeros((), bf16))
    grad_own = padded(grad_own)
    x_own = padded(hidden_in[0])

    small_list = [
        first_gain,
        first_shift,
        query_value_bias,
        attention_bias,
        second_gain,
        second_shift,
        contract_bias,
        expand_bias,
    ]
    smalls, row = None, 0
    for small in small_list:
        small = small.reshape(-1, rows_each)
        below = 16 - row - small.shape[0]
        small = jnp.pad(small, ((row, below), (0, -rows_each % 128)))
        smalls = small if smalls is None else smalls + small
        row = 16 - below
    bias = key_biases(share, slot, length, tp_rank, ctx_rank)
    inner = attention_in.reshape(rows_each, 3 * width)
    outer_t, contract_t = attention_out.T, contract_weight.T
    bias_rows = jnp.broadcast_to(bias[None], (8, bias.shape[0]))
    if fsdp_count == 8 and rows_each == 160 and 2 * hidden == 8 * width:
        (
            inner, outer_t, normed_one, proj, far, attended, lse, residual, normed_two, grad_all,
            activated, pre_grad, expand_sum, normed_own, normed_oth, out_own, out_oth, vectors,
        ) = forward(
            x_own, grad_own, smalls, jnp.transpose(attention_in, (1, 0, 2)), outer_t, expand_weight, contract_t,
            bias_rows,
        )
        hidden_grad, grad_expand, grad_contract, grad_outer, grad_inner, summed, expand_summed = backward(
            activated, pre_grad, normed_two, grad_all, normed_own, normed_oth, residual, proj, far,
            attended, normed_one, inner.reshape(model, 3 * width), outer_t.reshape(model, width), x_own, lse,
            bias_rows, vectors, expand_sum, share,
        )
        contracted = out_own + swap(out_oth, "tp").astype(f32)
        hidden_out = (residual + (contracted + vectors[7:8])).astype(bf16)
        summed = summed[:, : model // (2 * fsdp_count)]
        hidden_grad = hidden_grad.reshape(share, model)
        grad_contract, grad_outer = grad_contract.T, grad_outer.T
        grad_inner = jnp.transpose(grad_inner, (1, 0, 2))
        expand_summed = expand_summed[0, : 2 * hidden // (2 * fsdp_count)]
    else:
        (
            inner, outer_t, normed_one, proj, far, attended, lse, residual, normed_two, grad_all,
            activated, pre_grad, expand_sum, normed_own, normed_oth, out_own, out_oth, vectors,
        ) = forward_parts(
            x_own, grad_own, smalls, inner, outer_t, expand_weight, contract_t, bias
        )
        normed_oth = swap(normed_oth, "tp")
        grad_contract_t = dot(grad_all, activated, TN).astype(bf16)
        grad_expand = dot(normed_two, pre_grad, TN).astype(bf16)
        normed_own, normed_oth, grad_late = lax.optimization_barrier(
            (normed_own, normed_oth, jnp.concatenate([grad_expand, grad_contract_t], axis=1))
        )
        grad_late = lax.psum_scatter(
            grad_late, ("fsdp", "ctx"), scatter_dimension=0, tiled=True
        ).astype(f32)
        contracted = out_own + swap(out_oth, "tp").astype(f32)
        hidden_out = (residual + (contracted + vectors[7:8])).astype(bf16)

        residual_grad, residual_low, sums_two = norm_back(
            normed_own, normed_oth, residual, grad_own, vectors[5:6], True
        )
        residual_low_all = jnp.concatenate([residual_low, swap(residual_low, "tp")], axis=0)
        attended_grad = dot(residual_low_all, outer_t).astype(bf16)
        grad_outer_t = dot(residual_low_all, attended, TN).astype(bf16)

        grad_query, grad_near, grad_far = attend_back(
            proj, far, jnp.broadcast_to(bias[:, None], (bias.shape[0], 128)), attended, attended_grad, lse, heads
        )
        grad_near = (grad_near + swap(grad_far, "ctx").astype(f32)).astype(bf16)
        grad_proj = jnp.concatenate([grad_query, grad_near], axis=1)
        normed_grad = dot(grad_proj, inner, NT)
        normed_grad_oth = swap(normed_grad[slot:].astype(bf16), "tp")
        grad_inner = dot(normed_one, grad_proj, TN).astype(bf16)
        proj_sums = jnp.sum(grad_proj.astype(f32), axis=0)
        grad_inner, grad_outer_t = scatter_sums([grad_inner, grad_outer_t], 384, fsdp_count)
        hidden_grad, sums_one = norm_back(
            normed_grad[:slot], normed_grad_oth, x_own, residual_grad, vectors[0:1], False
        )
        grad_sum = jnp.sum(grad_own.astype(f32), axis=0)

        def placed(value, total):
            zero = jnp.zeros((total,), f32)
            return lax.dynamic_update_slice_in_dim(zero, value, tp_rank * value.shape[0], 0)

        owned = model // (fsdp_count * 2)
        stacked = jnp.stack(
            [
                sums_one[0],
                sums_one[1],
                placed(proj_sums[:width], model),
                placed(proj_sums[2 * width :], model),
                sums_two[2],
                sums_two[0],
                sums_two[1],
                grad_sum,
            ]
        )
        stacked = jnp.transpose(stacked.reshape(8, -1, owned), (1, 0, 2))
        expand_piece = placed(expand_sum[0], 2 * hidden).reshape(fsdp_count * 2, -1, owned)
        stacked = jnp.concatenate([stacked, expand_piece], axis=1)
        stacked = jnp.pad(stacked, ((0, 0), (0, 16 - stacked.shape[1]), (0, 128 - owned)))
        summed = sum_vectors(stacked, fsdp_count)[:, :owned]
        grad_outer = grad_outer_t.T
        grad_expand, grad_contract = grad_late[:, :hidden], grad_late[:, hidden:].T
        expand_summed = summed[8 : 8 + 2 * hidden // model].reshape(-1)

    return (
        hidden_out[None, :share],
        hidden_grad[None, :share],
        summed[0],
        summed[1],
        grad_inner.reshape(-1, 3, width),
        summed[2:4],
        grad_outer,
        summed[4],
        summed[5],
        summed[6],
        grad_expand,
        expand_summed,
        grad_contract,
        summed[7],
    )


def solution(mesh):
    return jax.shard_map(
        per_device,
        mesh=mesh,
        in_specs=(
            P("fsdp", ("ctx", "tp"), None),
            P("fsdp"),
            P("fsdp", ("ctx", "tp"), None),
            P("fsdp"),
            P("fsdp"),
            P("fsdp", None, "tp"),
            P(None, "fsdp"),
            P("tp", "fsdp"),
            P("fsdp"),
            P("fsdp"),
            P("fsdp"),
            P("fsdp", "tp"),
            P("fsdp"),
            P("tp", "fsdp"),
            P("fsdp"),
        ),
        out_specs=(
            P("fsdp", ("ctx", "tp"), None),
            P("fsdp", ("ctx", "tp"), None),
            P(("fsdp", "ctx")),
            P(("fsdp", "ctx")),
            P(("fsdp", "ctx"), None, "tp"),
            P(None, ("fsdp", "ctx")),
            P("tp", ("fsdp", "ctx")),
            P(("fsdp", "ctx")),
            P(("fsdp", "ctx")),
            P(("fsdp", "ctx")),
            P(("fsdp", "ctx"), "tp"),
            P(("fsdp", "ctx")),
            P("tp", ("fsdp", "ctx")),
            P(("fsdp", "ctx")),
        ),
        check_vma=False,
    )
```
